32 devices in a mesh: tok: 8 (over z, core), rep: 4 (over y, x).
Axes of the slice: x: 2, y: 2, z: 4, core: 2. Of those that a mesh axis runs over, the one named last changes fastest.
Arguments:
- hidden_in: bfloat16 [4096, 4096], P('tok', 'rep'), may hold values from -9 to 9
- w_query: bfloat16 [4096, 4096], P(None, 'rep'), may hold values from -2 to 2
- w_key: bfloat16 [4096, 4096], P(None, 'rep'), may hold values from -2 to 2
- w_value: bfloat16 [4096, 4096], P(None, 'rep'), may hold values from -0.09375 to 0.09375
- w_out: bfloat16 [4096, 4096], P('rep'), may hold values from -3 to 3
- q_gain: float32 [4096], P('rep'), may hold values from 0.5 to 6
- k_gain: float32 [4096], P('rep'), may hold values from 0.5 to 6
- post_gain: float32 [4096], P('rep'), may hold values from 0.1 to 1.9
- prompt_lengths: int32 [8], replicated, may hold values from 1 to 2048, as said below
- segment_ids: int32 [4096], replicated, may hold values from 0 to 7, as said below
- deal: int32 [4096], replicated, may hold values from 0 to 4095, as said below
- inverse: int32 [4096], replicated, may hold values from 0 to 4095, as said below
- slots: int32 [4096], replicated, may hold values from 0 to 4095, as said below
Outputs:
- output: bfloat16 [4096, 4096], P('tok', 'rep')
- cache_keys: bfloat16 [4096, 4096], P('tok', 'rep')
- cache_values: bfloat16 [4096, 4096], P('tok', 'rep')
The draws below stay inside these ranges and needn't reach their ends.
Inputs may be any that keep to these rules, and one draw needn't show every extreme that they name: `prompt_lengths`: the lengths sum to 4096; the longest prompt has exactly 2048 tokens. `segment_ids`: prompts lie in order: prompt s holds the prompt_lengths[s] packed tokens after those of prompts 0 to s - 1. `deal`: A permutation. For any two indices a and b of tok, exactly 64 of the packed tokens a * 512 to (a + 1) * 512 - 1 sit in dealt rows b * 512 to (b + 1) * 512 - 1. inverse[deal[q]] = q for every dealt row q. `slots`: A permutation. For any two indices a and b of tok, exactly 64 of the dealt rows a * 512 to (a + 1) * 512 - 1 have cache rows b * 512 to (b + 1) * 512 - 1.
All inputs are finite; a program needn't handle non-finite values.
Results may differ from the reference program's by a relative error of at most 0.012.
Values may be sent and summed in bfloat16 or wider, within the bound.
A program may use at most 128 MiB of HBM per device.

```python
import math
import jax
import jax.numpy as jnp
from jax import lax

D = 4096
HEADS = 32
HEAD_DIM = 128
TOK_DEV = 512
NSEG = 8
TOKENS = 4096
MAXLEN = 2048


def bounded(key, shape):
    return jax.random.truncated_normal(key, -3.0, 3.0, shape, jnp.float32)


def projection_pair(key):
    lower_draw = bounded(jax.random.fold_in(key, 11), (D, D))
    upper_draw = bounded(jax.random.fold_in(key, 12), (D, D))
    wobble = jnp.exp(jax.random.uniform(jax.random.fold_in(key, 13), (1, D), jnp.float32, -0.7, 0.7))
    head_index = jnp.arange(HEADS, dtype=jnp.float32)
    head_scale = 0.6 * 3.0 ** (head_index / max(HEADS - 1, 1))
    scale = jnp.repeat(head_scale, HEAD_DIM)[None, :] * wobble / math.sqrt(D)
    key_part = upper_draw
    return (lower_draw * scale, key_part * scale)


def draw_w_query(key, part):
    return projection_pair(key)[0].astype(jnp.bfloat16)


def draw_w_key(key, part):
    return projection_pair(key)[1].astype(jnp.bfloat16)


def draw_w_out(key, part):
    base = bounded(jax.random.fold_in(key, 41), (D, D))
    columns = jnp.arange(D, dtype=jnp.float32)[None, :]
    scale = 0.6 * 3.0 ** (columns / max(D - 1, 1)) * jnp.exp(jax.random.uniform(jax.random.fold_in(key, 43), (1, D), jnp.float32, -0.7, 0.7))
    values = base * scale
    return (values / math.sqrt(D)).astype(jnp.bfloat16)


def draw_hidden_in(key, part):
    noise = bounded(jax.random.fold_in(key, 51), (TOKENS, D))
    row_scale = jnp.exp(jax.random.uniform(jax.random.fold_in(key, 53), (TOKENS, 1), jnp.float32, -0.7, 0.7))
    values = noise * row_scale
    return values.astype(jnp.bfloat16)


def gain_draw(key, salt):
    low_end, high_end = (0.5, 2.0)
    logs = jax.random.uniform(jax.random.fold_in(key, salt), (D,), jnp.float32, math.log(low_end), math.log(high_end))
    return jnp.exp(logs)


def draw_q_gain(key, part):
    return gain_draw(key, 61)


def draw_k_gain(key, part):
    return gain_draw(key, 62)


def pack_layout(key):
    remainder = TOKENS - MAXLEN
    picks = jax.random.permutation(jax.random.fold_in(key, 21), remainder - 1)[:NSEG - 2] + 1
    cuts = jnp.sort(picks.astype(jnp.int32))
    edges = jnp.concatenate([jnp.zeros((1,), jnp.int32), cuts, jnp.full((1,), remainder, jnp.int32)])
    pieces = edges[1:] - edges[:-1]
    lengths = jnp.concatenate([jnp.full((1,), MAXLEN, jnp.int32), pieces])
    offset = jax.random.randint(jax.random.fold_in(key, 22), (), 0, NSEG)
    lengths = jnp.roll(lengths, offset)
    prompt_ends = jnp.cumsum(lengths)
    token_ids = jnp.arange(TOKENS, dtype=jnp.int32)
    segments = jnp.sum((token_ids[:, None] >= prompt_ends[None, :]).astype(jnp.int32), axis=1)
    return (lengths, segments)


def draw_prompt_lengths(key, part):
    return pack_layout(key)[0]


def draw_segment_ids(key, part):
    return pack_layout(key)[1]


def deal_layout(key):
    shards = TOKENS // TOK_DEV
    group_size = TOK_DEV // shards

    def ranking(salt):
        split_keys = jax.random.split(jax.random.fold_in(key, salt), shards)
        return jax.vmap(lambda single: jax.random.permutation(single, TOK_DEV))(split_keys).astype(jnp.int32)

    def spread(ranks, within_order):
        target = ranks // group_size
        within = ranks % group_size
        source = jnp.arange(shards, dtype=jnp.int32)[:, None]
        placed = within_order[target, source * group_size + within]
        return (target * TOK_DEV + placed).reshape(-1).astype(jnp.int32)
    inverse_rows = spread(ranking(31), ranking(32))
    deal_rows = jnp.argsort(inverse_rows).astype(jnp.int32)
    slot_rows = spread(ranking(33), ranking(34))
    return (deal_rows, inverse_rows, slot_rows)


def draw_deal(key, part):
    return deal_layout(key)[0]


def draw_inverse(key, part):
    return deal_layout(key)[1]


def draw_slots(key, part):
    return deal_layout(key)[2]


def shard_levels(key, dims, cuts, low, largest):
    level, own = 1.0, jax.random.fold_in(key, 6)
    for axis_at, parts in cuts:
        draws = jnp.exp(jax.random.uniform(jax.random.fold_in(own, axis_at), (parts,), jnp.float32, low / len(cuts), largest / len(cuts)))
        level = level * jnp.repeat(draws, dims[axis_at] // parts).reshape([-1 if axis == axis_at else 1 for axis in range(len(dims))])
    return level


def gaussian(rng, extent, deviation, most, cuts=(), kind=jnp.bfloat16):
    values = jax.random.normal(rng, extent, jnp.float32) * deviation
    if len(cuts) > 0:
        values = shard_levels(rng, extent, cuts, -0.22, 0.18) * values
    return jnp.clip(values, min=-most, max=most).astype(kind)


def setup_inputs(seed: int = 0) -> dict:
    key_list = jax.random.split(jax.random.key(seed), 14)
    return {
        "hidden_in": draw_hidden_in(jax.random.fold_in(key_list[13], 71), 0),
        "w_query": draw_w_query(jax.random.fold_in(key_list[13], 71), 0),
        "w_key": draw_w_key(jax.random.fold_in(key_list[13], 71), 0),
        "w_value": gaussian(key_list[3], (D, D), D ** -0.5, 0.09375, ((1, 4),)),
        "w_out": draw_w_out(jax.random.fold_in(key_list[13], 71), 0),
        "q_gain": draw_q_gain(jax.random.fold_in(key_list[13], 71), 0),
        "k_gain": draw_k_gain(jax.random.fold_in(key_list[13], 71), 0),
        "post_gain": jnp.clip(1.0 + 0.18 * jax.random.normal(key_list[7], (D,), jnp.float32), 0.1, 1.9),
        "prompt_lengths": draw_prompt_lengths(jax.random.fold_in(key_list[13], 71), 0),
        "segment_ids": draw_segment_ids(jax.random.fold_in(key_list[13], 71), 0),
        "deal": draw_deal(jax.random.fold_in(key_list[13], 71), 0),
        "inverse": draw_inverse(jax.random.fold_in(key_list[13], 71), 0),
        "slots": draw_slots(jax.random.fold_in(key_list[13], 71), 0),
    }


EPSILON = 1e-06
ROPE_BASE = 500000.0

def rotate(values, positions):
    half_size = values.shape[-1] // 2
    frequency = ROPE_BASE ** (-jnp.arange(half_size, dtype=jnp.float32) * 2.0 / values.shape[-1])
    angles = positions.astype(jnp.float32)[:, None] * frequency[None, :]
    cosine = jnp.cos(angles)[:, None, :]
    sine_part = jnp.sin(angles)[:, None, :]
    lower_half = values[..., :half_size]
    upper_half = values[..., half_size:]
    return jnp.concatenate([lower_half * cosine - upper_half * sine_part, upper_half * cosine + lower_half * sine_part], axis=-1)

def reference(hidden_in, w_query, w_key, w_value, w_out, q_gain, k_gain, post_gain, prompt_lengths, segment_ids, deal, inverse, slots):
    packed = hidden_in[inverse]
    query_rows = jnp.dot(packed, w_query, preferred_element_type=jnp.float32)
    key_rows = jnp.dot(packed, w_key, preferred_element_type=jnp.float32)
    value_half = jnp.dot(packed, w_value, preferred_element_type=jnp.float32).astype(jnp.bfloat16)
    prompt_starts = jnp.cumsum(prompt_lengths) - prompt_lengths
    token_ids = jnp.arange(TOKENS, dtype=jnp.int32)
    positions = token_ids - prompt_starts[segment_ids]
    query_rows = query_rows * lax.rsqrt(lax.optimization_barrier(jnp.mean(query_rows * query_rows, axis=1, keepdims=True)) + EPSILON) * q_gain[None, :]
    key_rows = key_rows * lax.rsqrt(lax.optimization_barrier(jnp.mean(key_rows * key_rows, axis=1, keepdims=True)) + EPSILON) * k_gain[None, :]
    query_rot = rotate(query_rows.reshape(TOKENS, HEADS, HEAD_DIM), positions).astype(jnp.bfloat16)
    key_rot = rotate(key_rows.reshape(TOKENS, HEADS, HEAD_DIM), positions).astype(jnp.bfloat16)
    allowed = (segment_ids[:, None] == segment_ids[None, :]) & (token_ids[None, :] <= token_ids[:, None])
    scale = HEAD_DIM ** (-0.5)

    def one_head(operands):
        head_query, head_key, head_value = operands
        scores = jnp.dot(head_query.astype(jnp.float32), head_key.astype(jnp.float32).T) * scale
        masked = jnp.where(allowed, scores, -1e+30)
        row_top = lax.optimization_barrier(jnp.max(masked, axis=1, keepdims=True))
        weights = jnp.where(allowed, jnp.exp(masked - row_top), 0.0)
        totals = lax.optimization_barrier(jnp.sum(weights, axis=1, keepdims=True))
        rounded = lax.optimization_barrier(weights.astype(jnp.bfloat16))
        return jnp.dot(rounded.astype(jnp.float32), head_value.astype(jnp.float32)) / totals
    value_heads = value_half.reshape(TOKENS, HEADS, HEAD_DIM)
    per_head = lax.map(one_head, (query_rot.transpose(1, 0, 2), key_rot.transpose(1, 0, 2), value_heads.transpose(1, 0, 2)))
    attended = per_head.transpose(1, 0, 2).reshape(TOKENS, D).astype(jnp.bfloat16)
    mixed = jnp.dot(attended, w_out, preferred_element_type=jnp.float32)
    normed = mixed * lax.rsqrt(lax.optimization_barrier(jnp.mean(mixed * mixed, axis=1, keepdims=True)) + EPSILON) * post_gain[None, :]
    output = (packed.astype(jnp.float32) + normed).astype(jnp.bfloat16)
    key_flat = key_rot.reshape(TOKENS, D)
    cache_keys = jnp.zeros((TOKENS, D), jnp.bfloat16).at[slots].set(key_flat[deal])
    cache_values = jnp.zeros((TOKENS, D), jnp.bfloat16).at[slots].set(value_half[deal])
    return (output, cache_keys, cache_values)
```

```python
import functools
import math

import jax
import jax.numpy as jnp
from jax import lax
from jax.experimental import pallas as pl
from jax.experimental.pallas import tpu as pltpu
from jax.sharding import PartitionSpec as P

HEAD_DIM = 128


EPSILON = 1e-06
ROPE_BASE = 500000.0


def rotate(values, positions):
    half_size = values.shape[-1] // 2
    frequency = ROPE_BASE ** (-jnp.arange(half_size, dtype=jnp.float32) * 2.0 / values.shape[-1])
    angles = positions.astype(jnp.float32)[:, None] * frequency[None, :]
    cosine = jnp.cos(angles)[:, None, :]
    sine_part = jnp.sin(angles)[:, None, :]
    lower_half = values[..., :half_size]
    upper_half = values[..., half_size:]
    return jnp.concatenate(
        [
            lower_half * cosine - upper_half * sine_part,
            upper_half * cosine + lower_half * sine_part,
        ],
        axis=-1,
    )


def starts_of(lengths):
    index = jnp.arange(lengths.shape[0], dtype=jnp.int32)
    return jnp.sum(jnp.where(index[None, :] < index[:, None], lengths[None, :], 0), axis=1)


def bucketed(table_rows, row_order, shards):
    picked = table_rows[row_order]
    return picked.reshape(shards, picked.shape[0] // shards, picked.shape[1])


def placement_order(sources, shard_rows):
    local_ids = jnp.arange(sources.shape[0], dtype=jnp.int32)
    arrival = jnp.argsort(sources * shard_rows + local_ids)
    return jnp.argsort(arrival)


def body(
    hidden_in,
    w_query,
    w_key,
    w_value,
    w_out,
    q_gain,
    k_gain,
    post_gain,
    prompt_lengths,
    segment_ids,
    deal,
    inverse,
    slots,
):
    tok_rows, width_dev = hidden_in.shape
    full_width = w_query.shape[0]
    head_size = HEAD_DIM
    heads_dev = width_dev // head_size
    shards = lax.axis_size("tok")
    first_row = lax.axis_index("tok") * tok_rows
    my_packed = lax.dynamic_slice_in_dim(deal, first_row, tok_rows)
    my_segment = segment_ids[my_packed]
    prompt_ids = jnp.arange(prompt_lengths.shape[0], dtype=jnp.int32)
    prompt_starts = starts_of(prompt_lengths)
    my_start = jnp.sum(
        jnp.where(my_segment[:, None] == prompt_ids[None, :], prompt_starts[None, :], 0), axis=1
    )
    positions = my_packed - my_start
    pieces = lax.all_gather(hidden_in, "rep", axis=1, tiled=True)
    query_rows = jnp.dot(pieces, w_query, preferred_element_type=jnp.float32)
    key_rows = jnp.dot(pieces, w_key, preferred_element_type=jnp.float32)
    value_rows = jnp.dot(pieces, w_value, preferred_element_type=jnp.float32)
    query_sums, key_sums = lax.psum(
        (jnp.sum(query_rows * query_rows, axis=1), jnp.sum(key_rows * key_rows, axis=1)), "rep"
    )
    query_rows = (
        query_rows * lax.rsqrt(query_sums / full_width + EPSILON)[:, None] * q_gain[None, :]
    )
    key_rows = key_rows * lax.rsqrt(key_sums / full_width + EPSILON)[:, None] * k_gain[None, :]
    query_rot = rotate(query_rows.reshape(tok_rows, heads_dev, head_size), positions).astype(
        jnp.bfloat16
    )
    key_rot = (
        rotate(key_rows.reshape(tok_rows, heads_dev, head_size), positions)
        .astype(jnp.bfloat16)
        .reshape(tok_rows, width_dev)
    )
    value_half = value_rows.astype(jnp.bfloat16)
    scale = head_size ** (-0.5)

    def attend(state_now, key_block, value_block, key_packed):
        row_top, totals, weighted = state_now
        block_keys = key_block.reshape(key_block.shape[0], heads_dev, head_size)
        block_values = value_block.reshape(value_block.shape[0], heads_dev, head_size)
        key_segment = segment_ids[key_packed]
        allowed = (key_segment[None, :] == my_segment[:, None]) & (
            key_packed[None, :] <= my_packed[:, None]
        )
        scores = (
            jnp.einsum("qhd,khd->hqk", query_rot, block_keys, preferred_element_type=jnp.float32)
            * scale
        )
        masked = jnp.where(allowed[None], scores, -1e30)
        new_top = jnp.maximum(row_top, jnp.max(masked, axis=2))
        weights = jnp.where(allowed[None], jnp.exp(masked - new_top[:, :, None]), 0.0)
        factor = jnp.exp(row_top - new_top)
        totals = totals * factor + jnp.sum(weights, axis=2)
        weighted = weighted * factor[:, :, None] + jnp.einsum(
            "hqk,khd->hqd",
            weights.astype(jnp.bfloat16),
            block_values,
            preferred_element_type=jnp.float32,
        )
        return (new_top, totals, weighted)

    start_state = (
        jnp.full((heads_dev, tok_rows), -1e30, jnp.float32),
        jnp.zeros((heads_dev, tok_rows), jnp.float32),
        jnp.zeros((heads_dev, tok_rows, head_size), jnp.float32),
    )
    owned_rows = lax.dynamic_slice_in_dim(jnp.argsort(slots), first_row, tok_rows)
    my_slots = lax.dynamic_slice_in_dim(slots, first_row, tok_rows)
    slot_order = jnp.argsort(my_slots)
    sent_keys, sent_values = (
        lax.all_to_all(
            bucketed(key_rot, slot_order, shards), "tok", split_axis=0, concat_axis=0, tiled=True
        ),
        lax.all_to_all(
            bucketed(value_half, slot_order, shards), "tok", split_axis=0, concat_axis=0, tiled=True
        ),
    )
    arrival = placement_order(owned_rows // tok_rows, tok_rows)
    cache_keys = sent_keys.reshape(tok_rows, width_dev)[arrival]
    cache_values = sent_values.reshape(tok_rows, width_dev)[arrival]
    pieces = (
        lax.all_gather(key_rot, "tok", axis=0, tiled=True),
        lax.all_gather(value_half, "tok", axis=0, tiled=True),
    )
    key_all = pieces[0]
    block_size = math.gcd(key_all.shape[0], tok_rows)
    block_count = key_all.shape[0] // block_size

    def advance(state_in, block_set):
        return (attend(state_in, block_set[0], block_set[1], block_set[2]), None)

    state_out, _ = lax.scan(
        advance,
        start_state,
        (
            key_all.reshape(block_count, block_size, width_dev),
            pieces[1].reshape(block_count, block_size, width_dev),
            deal.reshape(block_count, block_size),
        ),
    )
    row_top, totals, weighted = state_out
    attended = (
        (weighted / totals[:, :, None])
        .transpose(1, 0, 2)
        .reshape(tok_rows, width_dev)
        .astype(jnp.bfloat16)
    )
    mixed_rows = (
        lax.psum_scatter(
            lax.dot_general(
                w_out, attended, (((0,), (1,)), ((), ())), preferred_element_type=jnp.float32
            ).astype(jnp.bfloat16),
            "rep",
            scatter_dimension=0,
            tiled=True,
        )
        .astype(jnp.float32)
        .T
    )
    mixed_sums = lax.psum(jnp.sum(mixed_rows * mixed_rows, axis=1), "rep")
    normed_rows = (
        mixed_rows * lax.rsqrt(mixed_sums / full_width + EPSILON)[:, None] * post_gain[None, :]
    )
    result_rows = (hidden_in.astype(jnp.float32) + normed_rows).astype(jnp.bfloat16)
    packed_order = jnp.argsort(my_packed)
    returned = lax.all_to_all(
        bucketed(result_rows, packed_order, shards), "tok", split_axis=0, concat_axis=0, tiled=True
    )
    my_dealt = lax.dynamic_slice_in_dim(inverse, first_row, tok_rows)
    output = returned.reshape(tok_rows, width_dev)[placement_order(my_dealt // tok_rows, tok_rows)]
    return (output, cache_keys, cache_values)


def select_rows(hits, rows):
    return jnp.dot(
        hits.astype(jnp.bfloat16), rows, preferred_element_type=jnp.float32
    ).astype(jnp.bfloat16)


def attend_kernel(
    starts_ref, target_ref, qk_ref, v_ref, out_ref, keys, values, *, size, head_size, part, parts
):
    share = size // parts
    skip = part * share
    block = pl.program_id(0)
    mine = pl.ds(pl.multiple_of(block * size, size), size)
    row_iota = lax.broadcasted_iota(jnp.int32, (size, size), 0)
    hits = jnp.where(row_iota == target_ref[0], 1.0, 0.0).astype(jnp.bfloat16)
    qk_rows = qk_ref[...].reshape(size, 2 * head_size)
    v_rows = v_ref[...].reshape(size, head_size)
    packed_qk = jnp.dot(hits, qk_rows, preferred_element_type=jnp.float32).astype(jnp.bfloat16)
    packed_v = jnp.dot(hits, v_rows, preferred_element_type=jnp.float32).astype(jnp.bfloat16)
    query = packed_qk[skip : skip + share, :head_size]
    keys[mine, :] = packed_qk[:, head_size:]
    values[mine, :] = packed_v
    base_row = block * size
    first = base_row + skip
    rows = first + lax.broadcasted_iota(jnp.int32, (share, 1), 0)
    row_start = jnp.zeros((share, 1), jnp.int32)
    low = jnp.int32(0)
    for prompt in range(starts_ref.shape[0]):
        start = starts_ref[prompt]
        row_start = jnp.where(rows >= start, jnp.maximum(row_start, start), row_start)
        low = jnp.where(first >= start, jnp.maximum(low, start), low)
    scale = head_size ** (-0.5) * math.log2(math.e)

    def scores_of(key_rows):
        return lax.dot_general(
            query, key_rows, (((1,), (1,)), ((), ())), preferred_element_type=jnp.float32
        ) * scale

    column_iota = lax.broadcasted_iota(jnp.int32, (share, size), 1)
    row_iota = lax.broadcasted_iota(jnp.int32, (share, size), 0)
    allowed = (column_iota >= row_start - base_row) & (column_iota <= row_iota + skip)
    scores = jnp.where(allowed, scores_of(packed_qk[:, head_size:]), -1e30)
    top = jnp.max(scores, axis=1, keepdims=True)
    weights = jnp.exp2(scores - top)
    totals = jnp.sum(weights, axis=1, keepdims=True)
    weighted = jnp.dot(
        weights.astype(jnp.bfloat16), packed_v, preferred_element_type=jnp.float32
    )

    def earlier(step, state):
        top, totals, weighted = state
        base = pl.multiple_of((block - 1 - step) * size, size)
        scores = scores_of(keys[pl.ds(base, size), :])
        scores = jnp.where(column_iota >= row_start - base, scores, -1e30)
        new_top = jnp.maximum(top, jnp.max(scores, axis=1, keepdims=True))
        factor = jnp.exp2(top - new_top)
        weights = jnp.exp2(scores - new_top)
        totals = totals * factor + jnp.sum(weights, axis=1, keepdims=True)
        weighted = weighted * factor + jnp.dot(
            weights.astype(jnp.bfloat16),
            values[pl.ds(base, size), :],
            preferred_element_type=jnp.float32,
        )
        return (new_top, totals, weighted)

    top, totals, weighted = lax.fori_loop(
        0, block - low // size, earlier, (top, totals, weighted)
    )
    out_ref[...] = (weighted / totals).astype(jnp.bfloat16)


def attend_head(starts, target, qk_rows, v_rows, part, parts):
    shards, tok_rows, head_size = v_rows.shape
    chunk = tok_rows // shards
    return pl.pallas_call(
        functools.partial(
            attend_kernel, size=tok_rows, head_size=head_size, part=part, parts=parts
        ),
        out_shape=jax.ShapeDtypeStruct((shards * tok_rows // parts, head_size), jnp.bfloat16),
        grid_spec=pltpu.PrefetchScalarGridSpec(
            num_scalar_prefetch=1,
            grid=(shards,),
            in_specs=[
                pl.BlockSpec((1, 1, tok_rows), lambda i, s: (i, 0, 0)),
                pl.BlockSpec((shards, chunk, 2 * head_size), lambda i, s: (0, i, 0)),
                pl.BlockSpec((shards, chunk, head_size), lambda i, s: (0, i, 0)),
            ],
            out_specs=pl.BlockSpec((tok_rows // parts, head_size), lambda i, s: (i, 0)),
            scratch_shapes=[
                pltpu.VMEM((shards * tok_rows, head_size), jnp.bfloat16),
                pltpu.VMEM((shards * tok_rows, head_size), jnp.bfloat16),
            ],
        ),
        compiler_params=pltpu.CompilerParams(
            dimension_semantics=("arbitrary",), vmem_limit_bytes=48 << 20
        ),
        cost_estimate=pl.CostEstimate(
            flops=8 * tok_rows * tok_rows * shards * head_size * 3 // parts,
            bytes_accessed=8 * shards * tok_rows * head_size,
            transcendentals=3 * shards * tok_rows * tok_rows,
        ),
    )(starts, target, qk_rows, v_rows)


def rope_kernel(q_ref, k_ref, q_scale, k_scale, q_gain, k_gain, cosine, sine, qk_ref, key_ref):
    head_size = q_ref.shape[1]

    def turned(rows, scale, gain):
        normed = rows[...] * scale[...] * gain[...]
        other = pltpu.roll(normed, head_size // 2, 1)
        return (normed * cosine[...] + other * sine[...]).astype(jnp.bfloat16)

    qk_ref[0, :, :head_size] = turned(q_ref, q_scale, q_gain)
    key_rows = turned(k_ref, k_scale, k_gain)
    qk_ref[0, :, head_size:] = key_rows
    key_ref[...] = key_rows


def rope_heads(query_rows, key_rows, q_scale, k_scale, q_gain, k_gain, cosine, sine):
    rows, width = query_rows.shape
    head_size = cosine.shape[1]
    heads = width // head_size
    wide = pl.BlockSpec((rows, head_size), lambda h: (0, h))
    thin = pl.BlockSpec((rows, 1), lambda h: (0, 0))
    gain = pl.BlockSpec((1, head_size), lambda h: (0, h))
    table = pl.BlockSpec((rows, head_size), lambda h: (0, 0))
    return pl.pallas_call(
        rope_kernel,
        out_shape=(
            jax.ShapeDtypeStruct((heads, rows, 2 * head_size), jnp.bfloat16),
            jax.ShapeDtypeStruct((rows, width), jnp.bfloat16),
        ),
        grid=(heads,),
        in_specs=[wide, wide, thin, thin, gain, gain, table, table],
        out_specs=(pl.BlockSpec((1, rows, 2 * head_size), lambda h: (h, 0, 0)), wide),
        compiler_params=pltpu.CompilerParams(vmem_limit_bytes=24 << 20),
        cost_estimate=pl.CostEstimate(
            flops=14 * rows * width, bytes_accessed=14 * rows * width, transcendentals=0
        ),
    )(query_rows, key_rows, q_scale, k_scale, q_gain, k_gain, cosine, sine)


def value_kernel(owner_ref, x_ref, w_ref, so_far_ref, flat_ref, heads_ref):
    rows = so_far_ref[...] + jnp.dot(x_ref[...], w_ref[...], preferred_element_type=jnp.float32)
    rows = rows.astype(jnp.bfloat16)
    flat_ref[...] = rows
    count, _, head_size = heads_ref.shape
    for head in range(count):
        heads_ref[head] = rows[:, head * head_size : (head + 1) * head_size]


def value_heads(owner, pieces, w_value, so_far, head_size):
    rows, depth = pieces.shape
    width = w_value.shape[1]
    count = 2
    return pl.pallas_call(
        value_kernel,
        out_shape=(
            jax.ShapeDtypeStruct((rows, width), jnp.bfloat16),
            jax.ShapeDtypeStruct((width // head_size, rows, head_size), jnp.bfloat16),
        ),
        grid_spec=pltpu.PrefetchScalarGridSpec(
            num_scalar_prefetch=1,
            grid=(width // (count * head_size),),
            in_specs=[
                pl.BlockSpec((rows, depth), lambda h, owner: (0, 0)),
                pl.BlockSpec((depth, count * head_size), lambda h, owner: (owner[0], h)),
                pl.BlockSpec((rows, count * head_size), lambda h, owner: (0, h)),
            ],
            out_specs=(
                pl.BlockSpec((rows, count * head_size), lambda h, owner: (0, h)),
                pl.BlockSpec((count, rows, head_size), lambda h, owner: (h, 0, 0)),
            ),
        ),
        compiler_params=pltpu.CompilerParams(vmem_limit_bytes=40 << 20),
        cost_estimate=pl.CostEstimate(
            flops=2 * rows * depth * width,
            bytes_accessed=2 * (rows * depth + depth * width + 2 * rows * width),
            transcendentals=0,
        ),
    )(owner, pieces, w_value, so_far)


def body_heads(
    hidden_in,
    w_query,
    w_key,
    w_value,
    w_out,
    q_gain,
    k_gain,
    post_gain,
    prompt_lengths,
    segment_ids,
    deal,
    inverse,
    slots,
):
    tok_rows, width_dev = hidden_in.shape
    full_width = w_query.shape[0]
    head_size = HEAD_DIM
    heads_dev = width_dev // head_size
    shards = lax.axis_size("tok")
    chunk = tok_rows // shards
    me = lax.axis_index("tok")
    first_row = me * tok_rows
    half_rows = tok_rows // 2
    corner = lax.axis_index("rep")
    across = [(i, i ^ 1) for i in range(4)]
    along = [(i, i ^ 2) for i in range(4)]

    local = jnp.arange(tok_rows, dtype=jnp.int32)
    starts = starts_of(prompt_lengths)
    my_packed = lax.dynamic_slice_in_dim(deal, first_row, tok_rows)
    my_slots = lax.dynamic_slice_in_dim(slots, first_row, tok_rows)
    rank = jnp.sum((my_packed[None, :] < my_packed[:, None]).astype(jnp.int32), axis=1)
    sort_hits = rank[None, :] == local[:, None]
    sorted_packed = jnp.sum(jnp.where(sort_hits, my_packed[None, :], 0), axis=1)
    sorted_slots = jnp.sum(jnp.where(sort_hits, my_slots[None, :], 0), axis=1)
    my_start = jnp.max(
        jnp.where(starts[None, :] <= sorted_packed[:, None], starts[None, :], 0), axis=1
    )
    positions = sorted_packed - my_start

    source = inverse.reshape(shards, tok_rows) // tok_rows
    before = (source[:, None, :] == source[:, :, None]) & (local[None, None, :] < local[None, :, None])
    arrived = source * chunk + jnp.sum(before.astype(jnp.int32), axis=2)
    target = jnp.sum(
        jnp.where(arrived[:, :, None] == local[None, None, :], local[None, :, None], 0), axis=1
    )

    slot_rank = jnp.sum((sorted_slots[None, :] < sorted_slots[:, None]).astype(jnp.int32), axis=1)
    slot_hits = slot_rank[None, :] == local[:, None]
    slot_rows = slots.reshape(shards, tok_rows) - first_row
    owned = (slot_rows >= 0) & (slot_rows < tok_rows)
    ahead = owned[:, None, :] & (slot_rows[:, None, :] < slot_rows[:, :, None])
    landed = jnp.arange(shards, dtype=jnp.int32)[:, None] * chunk + jnp.sum(
        ahead.astype(jnp.int32), axis=2
    )
    landed = jnp.where(owned, landed, -1).reshape(-1)
    slot_target = jnp.sum(
        jnp.where(landed[:, None] == local[None, :], slot_rows.reshape(-1)[:, None], 0), axis=0
    )

    piece = select_rows(sort_hits, hidden_in)
    piece_x = lax.ppermute(piece, "rep", across)
    piece_y = lax.ppermute(piece, "rep", along)
    piece_xy = jnp.concatenate(
        [
            lax.ppermute(piece_y[:half_rows], "rep", across),
            lax.ppermute(piece_x[half_rows:], "rep", along),
        ],
        axis=0,
    )

    def product(rows, weights, step):
        owned = lax.dynamic_slice_in_dim(weights, (corner ^ step) * width_dev, width_dev, axis=0)
        return jnp.dot(rows, owned, preferred_element_type=jnp.float32)

    sums_now = [product(piece, weights, 0) for weights in (w_value, w_query, w_key)]
    for step, rows in ((1, piece_x), (2, piece_y)):
        sums_now = [
            done + product(rows, weights, step)
            for done, weights in zip(sums_now, (w_value, w_query, w_key))
        ]

    sent_hidden = lax.all_to_all(
        piece.reshape(shards, chunk, width_dev),
        "tok",
        split_axis=0,
        concat_axis=0,
        tiled=True,
    )
    half_size = head_size // 2
    frequency = ROPE_BASE ** (-jnp.arange(half_size, dtype=jnp.float32) * 2.0 / head_size)
    angles = positions.astype(jnp.float32)[:, None] * frequency[None, :]
    cosine, sine = jnp.cos(angles), jnp.sin(angles)
    cosine = jnp.concatenate([cosine, cosine], axis=1)
    sine = jnp.concatenate([-sine, sine], axis=1)
    piece_xy, sent_hidden, cosine, sine, target, slot_target, sums_now = lax.optimization_barrier(
        (piece_xy, sent_hidden, cosine, sine, target, slot_target, sums_now)
    )
    my_target = lax.dynamic_index_in_dim(target, me, 0, keepdims=False)
    my_hits = my_target[None, :] == local[:, None]

    last = corner ^ 3
    value_half, value_sent = value_heads(last[None], piece_xy, w_value, sums_now[0], head_size)

    def exchange(rows):
        return lax.all_to_all(rows, "tok", split_axis=0, concat_axis=0, tiled=True)

    v_rows = exchange(value_sent)
    piece_xy, value_half = lax.optimization_barrier((piece_xy, value_half))
    query_rows = sums_now[1] + product(piece_xy, w_query, 3)
    key_rows = sums_now[2] + product(piece_xy, w_key, 3)
    sums = jnp.stack(
        [jnp.sum(query_rows * query_rows, axis=1), jnp.sum(key_rows * key_rows, axis=1)]
    )
    scales = lax.rsqrt(lax.psum(sums, "rep") / full_width + EPSILON)
    qk_sent, key_flat = rope_heads(
        query_rows,
        key_rows,
        scales[0][:, None],
        scales[1][:, None],
        q_gain[None, :],
        k_gain[None, :],
        cosine,
        sine,
    )
    qk_rows = exchange(qk_sent)
    qk_rows, v_rows, sent_hidden = lax.optimization_barrier((qk_rows, v_rows, sent_hidden))
    packed_hidden = select_rows(my_hits, sent_hidden.reshape(tok_rows, width_dev))

    parts = 2
    share = tok_rows // parts
    heads_out = [
        attend_head(starts, target[:, None, :], qk_rows, v_rows, part, parts).reshape(
            shards, share, head_size
        )
        for part in range(parts)
    ]
    first, last = lax.optimization_barrier((exchange(heads_out[0]), heads_out[1]))
    attended = [first, exchange(last)]
    attended[-1], key_flat, value_half = lax.optimization_barrier(
        (attended[-1], key_flat, value_half)
    )
    mixed = []
    for rows in attended:
        rows = rows.transpose(1, 0, 2).reshape(share, width_dev)
        mixed.append(
            lax.psum_scatter(
                lax.dot_general(
                    w_out, rows, (((0,), (1,)), ((), ())), preferred_element_type=jnp.float32
                ).astype(jnp.bfloat16),
                "rep",
                scatter_dimension=0,
                tiled=True,
            )
        )
    cache_hits = slot_target[None, :] == local[:, None]
    sent_keys, sent_values = [
        exchange(select_rows(slot_hits, rows).reshape(shards, chunk, width_dev)).reshape(
            tok_rows, width_dev
        )
        for rows in (key_flat, value_half)
    ]
    mixed_rows = jnp.concatenate([rows.astype(jnp.float32).T for rows in mixed], axis=0)
    mixed_sums = lax.psum(jnp.sum(mixed_rows * mixed_rows, axis=1), "rep")
    normed_rows = (
        mixed_rows * lax.rsqrt(mixed_sums / full_width + EPSILON)[:, None] * post_gain[None, :]
    )
    output = (packed_hidden.astype(jnp.float32) + normed_rows).astype(jnp.bfloat16)
    output, sent_keys = lax.optimization_barrier((output, sent_keys))
    cache_keys = select_rows(cache_hits, sent_keys)
    cache_values = select_rows(cache_hits, sent_values)
    return (output, cache_keys, cache_values)


def solution(mesh):
    def pick(*operands):
        heads_dev = operands[0].shape[1] // HEAD_DIM
        fits = heads_dev == mesh.shape["tok"] and mesh.shape["rep"] == 4
        chosen = body_heads if fits else body
        return chosen(*operands)

    return jax.shard_map(
        pick,
        mesh=mesh,
        in_specs=(
            P("tok", "rep"),
            P(None, "rep"),
            P(None, "rep"),
            P(None, "rep"),
            P("rep", None),
            P("rep"),
            P("rep"),
            P("rep"),
            P(),
            P(),
            P(),
            P(),
            P(),
        ),
        out_specs=(P("tok", "rep"), P("tok", "rep"), P("tok", "rep")),
        check_vma=False,
    )
```

```python
import functools
import math

import jax
import jax.numpy as jnp
from jax import lax
from jax.experimental import pallas as pl
from jax.experimental.pallas import tpu as pltpu
from jax.sharding import PartitionSpec as P

HEAD_DIM = 128


EPSILON = 1e-06
ROPE_BASE = 500000.0


def rotate(values, positions):
    half_size = values.shape[-1] // 2
    frequency = ROPE_BASE ** (-jnp.arange(half_size, dtype=jnp.float32) * 2.0 / values.shape[-1])
    angles = positions.astype(jnp.float32)[:, None] * frequency[None, :]
    cosine = jnp.cos(angles)[:, None, :]
    sine_part = jnp.sin(angles)[:, None, :]
    lower_half = values[..., :half_size]
    upper_half = values[..., half_size:]
    return jnp.concatenate(
        [
            lower_half * cosine - upper_half * sine_part,
            upper_half * cosine + lower_half * sine_part,
        ],
        axis=-1,
    )


def starts_of(lengths):
    index = jnp.arange(lengths.shape[0], dtype=jnp.int32)
    return jnp.sum(jnp.where(index[None, :] < index[:, None], lengths[None, :], 0), axis=1)


def bucketed(table_rows, row_order, shards):
    picked = table_rows[row_order]
    return picked.reshape(shards, picked.shape[0] // shards, picked.shape[1])


def placement_order(sources, shard_rows):
    local_ids = jnp.arange(sources.shape[0], dtype=jnp.int32)
    arrival = jnp.argsort(sources * shard_rows + local_ids)
    return jnp.argsort(arrival)


def body(
    hidden_in,
    w_query,
    w_key,
    w_value,
    w_out,
    q_gain,
    k_gain,
    post_gain,
    prompt_lengths,
    segment_ids,
    deal,
    inverse,
    slots,
):
    tok_rows, width_dev = hidden_in.shape
    full_width = w_query.shape[0]
    head_size = HEAD_DIM
    heads_dev = width_dev // head_size
    shards = lax.axis_size("tok")
    first_row = lax.axis_index("tok") * tok_rows
    my_packed = lax.dynamic_slice_in_dim(deal, first_row, tok_rows)
    my_segment = segment_ids[my_packed]
    prompt_ids = jnp.arange(prompt_lengths.shape[0], dtype=jnp.int32)
    prompt_starts = starts_of(prompt_lengths)
    my_start = jnp.sum(
        jnp.where(my_segment[:, None] == prompt_ids[None, :], prompt_starts[None, :], 0), axis=1
    )
    positions = my_packed - my_start
    pieces = lax.all_gather(hidden_in, "rep", axis=1, tiled=True)
    query_rows = jnp.dot(pieces, w_query, preferred_element_type=jnp.float32)
    key_rows = jnp.dot(pieces, w_key, preferred_element_type=jnp.float32)
    value_rows = jnp.dot(pieces, w_value, preferred_element_type=jnp.float32)
    query_sums, key_sums = lax.psum(
        (jnp.sum(query_rows * query_rows, axis=1), jnp.sum(key_rows * key_rows, axis=1)), "rep"
    )
    query_rows = (
        query_rows * lax.rsqrt(query_sums / full_width + EPSILON)[:, None] * q_gain[None, :]
    )
    key_rows = key_rows * lax.rsqrt(key_sums / full_width + EPSILON)[:, None] * k_gain[None, :]
    query_rot = rotate(query_rows.reshape(tok_rows, heads_dev, head_size), positions).astype(
        jnp.bfloat16
    )
    key_rot = (
        rotate(key_rows.reshape(tok_rows, heads_dev, head_size), positions)
        .astype(jnp.bfloat16)
        .reshape(tok_rows, width_dev)
    )
    value_half = value_rows.astype(jnp.bfloat16)
    scale = head_size ** (-0.5)

    def attend(state_now, key_block, value_block, key_packed):
        row_top, totals, weighted = state_now
        block_keys = key_block.reshape(key_block.shape[0], heads_dev, head_size)
        block_values = value_block.reshape(value_block.shape[0], heads_dev, head_size)
        key_segment = segment_ids[key_packed]
        allowed = (key_segment[None, :] == my_segment[:, None]) & (
            key_packed[None, :] <= my_packed[:, None]
        )
        scores = (
            jnp.einsum("qhd,khd->hqk", query_rot, block_keys, preferred_element_type=jnp.float32)
            * scale
        )
        masked = jnp.where(allowed[None], scores, -1e30)
        new_top = jnp.maximum(row_top, jnp.max(masked, axis=2))
        weights = jnp.where(allowed[None], jnp.exp(masked - new_top[:, :, None]), 0.0)
        factor = jnp.exp(row_top - new_top)
        totals = totals * factor + jnp.sum(weights, axis=2)
        weighted = weighted * factor[:, :, None] + jnp.einsum(
            "hqk,khd->hqd",
            weights.astype(jnp.bfloat16),
            block_values,
            preferred_element_type=jnp.float32,
        )
        return (new_top, totals, weighted)

    start_state = (
        jnp.full((heads_dev, tok_rows), -1e30, jnp.float32),
        jnp.zeros((heads_dev, tok_rows), jnp.float32),
        jnp.zeros((heads_dev, tok_rows, head_size), jnp.float32),
    )
    owned_rows = lax.dynamic_slice_in_dim(jnp.argsort(slots), first_row, tok_rows)
    my_slots = lax.dynamic_slice_in_dim(slots, first_row, tok_rows)
    slot_order = jnp.argsort(my_slots)
    sent_keys, sent_values = (
        lax.all_to_all(
            bucketed(key_rot, slot_order, shards), "tok", split_axis=0, concat_axis=0, tiled=True
        ),
        lax.all_to_all(
            bucketed(value_half, slot_order, shards), "tok", split_axis=0, concat_axis=0, tiled=True
        ),
    )
    arrival = placement_order(owned_rows // tok_rows, tok_rows)
    cache_keys = sent_keys.reshape(tok_rows, width_dev)[arrival]
    cache_values = sent_values.reshape(tok_rows, width_dev)[arrival]
    pieces = (
        lax.all_gather(key_rot, "tok", axis=0, tiled=True),
        lax.all_gather(value_half, "tok", axis=0, tiled=True),
    )
    key_all = pieces[0]
    block_size = math.gcd(key_all.shape[0], tok_rows)
    block_count = key_all.shape[0] // block_size

    def advance(state_in, block_set):
        return (attend(state_in, block_set[0], block_set[1], block_set[2]), None)

    state_out, _ = lax.scan(
        advance,
        start_state,
        (
            key_all.reshape(block_count, block_size, width_dev),
            pieces[1].reshape(block_count, block_size, width_dev),
            deal.reshape(block_count, block_size),
        ),
    )
    row_top, totals, weighted = state_out
    attended = (
        (weighted / totals[:, :, None])
        .transpose(1, 0, 2)
        .reshape(tok_rows, width_dev)
        .astype(jnp.bfloat16)
    )
    mixed_rows = (
        lax.psum_scatter(
            lax.dot_general(
                w_out, attended, (((0,), (1,)), ((), ())), preferred_element_type=jnp.float32
            ).astype(jnp.bfloat16),
            "rep",
            scatter_dimension=0,
            tiled=True,
        )
        .astype(jnp.float32)
        .T
    )
    mixed_sums = lax.psum(jnp.sum(mixed_rows * mixed_rows, axis=1), "rep")
    normed_rows = (
        mixed_rows * lax.rsqrt(mixed_sums / full_width + EPSILON)[:, None] * post_gain[None, :]
    )
    result_rows = (hidden_in.astype(jnp.float32) + normed_rows).astype(jnp.bfloat16)
    packed_order = jnp.argsort(my_packed)
    returned = lax.all_to_all(
        bucketed(result_rows, packed_order, shards), "tok", split_axis=0, concat_axis=0, tiled=True
    )
    my_dealt = lax.dynamic_slice_in_dim(inverse, first_row, tok_rows)
    output = returned.reshape(tok_rows, width_dev)[placement_order(my_dealt // tok_rows, tok_rows)]
    return (output, cache_keys, cache_values)


def select_rows(hits, rows):
    return jnp.dot(
        hits.astype(jnp.bfloat16), rows, preferred_element_type=jnp.float32
    ).astype(jnp.bfloat16)


def attend_kernel(
    starts_ref, target_ref, qk_ref, v_ref, out_ref, keys, values, *, size, head_size, part, parts
):
    share = size // parts
    skip = part * share
    block = pl.program_id(0)
    mine = pl.ds(pl.multiple_of(block * size, size), size)
    row_iota = lax.broadcasted_iota(jnp.int32, (size, size), 0)
    hits = jnp.where(row_iota == target_ref[0], 1.0, 0.0).astype(jnp.bfloat16)
    qk_rows = qk_ref[...].reshape(size, 2 * head_size)
    v_rows = v_ref[...].reshape(size, head_size)
    packed_qk = jnp.dot(hits, qk_rows, preferred_element_type=jnp.float32).astype(jnp.bfloat16)
    packed_v = jnp.dot(hits, v_rows, preferred_element_type=jnp.float32).astype(jnp.bfloat16)
    query = packed_qk[skip : skip + share, :head_size]
    keys[mine, :] = packed_qk[:, head_size:]
    values[mine, :] = packed_v
    base_row = block * size
    first = base_row + skip
    rows = first + lax.broadcasted_iota(jnp.int32, (share, 1), 0)
    row_start = jnp.zeros((share, 1), jnp.int32)
    low = jnp.int32(0)
    for prompt in range(starts_ref.shape[0]):
        start = starts_ref[prompt]
        row_start = jnp.where(rows >= start, jnp.maximum(row_start, start), row_start)
        low = jnp.where(first >= start, jnp.maximum(low, start), low)
    scale = head_size ** (-0.5) * math.log2(math.e)

    def scores_of(key_rows):
        return lax.dot_general(
            query, key_rows, (((1,), (1,)), ((), ())), preferred_element_type=jnp.float32
        ) * scale

    column_iota = lax.broadcasted_iota(jnp.int32, (share, size), 1)
    row_iota = lax.broadcasted_iota(jnp.int32, (share, size), 0)
    allowed = (column_iota >= row_start - base_row) & (column_iota <= row_iota + skip)
    scores = jnp.where(allowed, scores_of(packed_qk[:, head_size:]), -1e30)
    top = jnp.max(scores, axis=1, keepdims=True)
    weights = jnp.exp2(scores - top)
    totals = jnp.sum(weights, axis=1, keepdims=True)
    weighted = jnp.dot(
        weights.astype(jnp.bfloat16), packed_v, preferred_element_type=jnp.float32
    )

    def earlier(step, state):
        top, totals, weighted = state
        base = pl.multiple_of((block - 1 - step) * size, size)
        scores = scores_of(keys[pl.ds(base, size), :])
        scores = jnp.where(column_iota >= row_start - base, scores, -1e30)
        new_top = jnp.maximum(top, jnp.max(scores, axis=1, keepdims=True))
        factor = jnp.exp2(top - new_top)
        weights = jnp.exp2(scores - new_top)
        totals = totals * factor + jnp.sum(weights, axis=1, keepdims=True)
        weighted = weighted * factor + jnp.dot(
            weights.astype(jnp.bfloat16),
            values[pl.ds(base, size), :],
            preferred_element_type=jnp.float32,
        )
        return (new_top, totals, weighted)

    top, totals, weighted = lax.fori_loop(
        0, block - low // size, earlier, (top, totals, weighted)
    )
    out_ref[...] = (weighted / totals).astype(jnp.bfloat16)


def attend_head(starts, target, qk_rows, v_rows, part, parts):
    shards, tok_rows, head_size = v_rows.shape
    chunk = tok_rows // shards
    return pl.pallas_call(
        functools.partial(
            attend_kernel, size=tok_rows, head_size=head_size, part=part, parts=parts
        ),
        out_shape=jax.ShapeDtypeStruct((shards * tok_rows // parts, head_size), jnp.bfloat16),
        grid_spec=pltpu.PrefetchScalarGridSpec(
            num_scalar_prefetch=1,
            grid=(shards,),
            in_specs=[
                pl.BlockSpec((1, 1, tok_rows), lambda i, s: (i, 0, 0)),
                pl.BlockSpec((shards, chunk, 2 * head_size), lambda i, s: (0, i, 0)),
                pl.BlockSpec((shards, chunk, head_size), lambda i, s: (0, i, 0)),
            ],
            out_specs=pl.BlockSpec((tok_rows // parts, head_size), lambda i, s: (i, 0)),
            scratch_shapes=[
                pltpu.VMEM((shards * tok_rows, head_size), jnp.bfloat16),
                pltpu.VMEM((shards * tok_rows, head_size), jnp.bfloat16),
            ],
        ),
        compiler_params=pltpu.CompilerParams(
            dimension_semantics=("arbitrary",), vmem_limit_bytes=48 << 20
        ),
        cost_estimate=pl.CostEstimate(
            flops=8 * tok_rows * tok_rows * shards * head_size * 3 // parts,
            bytes_accessed=8 * shards * tok_rows * head_size,
            transcendentals=3 * shards * tok_rows * tok_rows,
        ),
    )(starts, target, qk_rows, v_rows)


MESH = pl.DeviceIdType.MESH


def greet(peers):
    barrier = pltpu.get_barrier_semaphore()
    for peer in peers:
        pl.semaphore_signal(barrier, inc=1, device_id=peer, device_id_type=MESH)
    pl.semaphore_wait(barrier, len(peers))


def places():
    corner = lax.axis_index("rep")
    right = corner + 1 - 2 * (corner % 2)
    over = corner + 2 - 4 * (corner // 2)
    return corner, right, over, 3 - corner


def turned_sums(columns):
    rows = columns[0].shape[0]
    lane = lax.broadcasted_iota(jnp.int32, (rows, 128), 1)
    wide = jnp.zeros((rows, 128), jnp.float32)
    for at, column in enumerate(columns):
        wide = jnp.where(lane == at, column, wide)
    return wide.T[0:8, :]


def project_kernel(
    piece, w_value, w_query, w_key, q_gain, k_gain, where, frequency, meta,
    qk_out, v_out, hid_out, meta_out, k_flat, v_flat,
    held, got, acc, turned, value, cosine, sine, sums,
    w_sem, near_send, near_recv, sum_send, sum_recv, far_send, far_recv, own_sem, flat_sem,
    *, shards, full_width,
):
    rows, width = piece.shape
    half = rows // 2
    quarter = half // 2
    chunk = rows // shards
    head = HEAD_DIM
    me = lax.axis_index("tok")
    corner, right, over, cross = places()
    weights = (w_value, w_query, w_key)
    owners = (corner, right, over, cross)

    def load(which, step):
        return pltpu.make_async_copy(
            weights[which].at[pl.ds(pl.multiple_of(owners[step] * width, width), width), :],
            held.at[which, step],
            w_sem.at[which, step],
        )

    for step in range(4):
        for which in range(3):
            load(which, step).start()

    others = [(me + 1 + d) % shards for d in range(shards - 1)]
    greet([{"rep": peer} for peer in (right, over, cross)] + [{"tok": peer} for peer in others])

    def near(src, slot, at, size, peer, sem):
        return pltpu.make_async_remote_copy(
            src_ref=src.at[pl.ds(at, size), :],
            dst_ref=got.at[slot, pl.ds(at, size), :],
            send_sem=near_send.at[sem],
            recv_sem=near_recv.at[sem],
            device_id={"rep": peer},
            device_id_type=MESH,
        )

    def own_copies(h):
        return (
            near(piece, 0, h * half, half, right, 4 * h),
            near(piece, 1, h * half, half, over, 4 * h + 1),
        )

    def forwards(h):
        return (
            near(got.at[1], 2, h * half, quarter, right, 4 * h + 2),
            near(got.at[0], 2, h * half + quarter, quarter, over, 4 * h + 3),
        )

    def to_far(kind, d, src, dst):
        return pltpu.make_async_remote_copy(
            src_ref=src,
            dst_ref=dst,
            send_sem=far_send.at[kind, d],
            recv_sem=far_recv.at[kind, d],
            device_id={"tok": (me + 1 + d) % shards},
            device_id_type=MESH,
        )

    def head_of(ref, h, owner):
        return ref.at[pl.ds(h * half, half), pl.ds(pl.multiple_of(owner * head, head), head)]

    def source_of(kind, peer):
        if kind < 2:
            return head_of(value, kind, peer)
        if kind < 6:
            return head_of(turned.at[(kind - 2) // 2], kind % 2, peer)
        if kind == 6:
            return piece.at[pl.ds(pl.multiple_of(peer * chunk, chunk), chunk), :]
        return meta

    def landing(kind):
        if kind < 2:
            return v_out.at[me, pl.ds(kind * half, half), :]
        if kind < 6:
            return qk_out.at[
                me, pl.ds((kind % 2) * half, half), pl.ds(((kind - 2) // 2) * head, head)
            ]
        return (hid_out if kind == 6 else meta_out).at[me]

    def own_copy(kind):
        return pltpu.make_async_copy(source_of(kind, me), landing(kind), own_sem.at[kind])

    def far_copy(kind, d):
        return to_far(kind, d, source_of(kind, (me + 1 + d) % shards), landing(kind))

    def send_far(kind):
        def one(d, _):
            far_copy(kind, d).start()
            return _

        lax.fori_loop(0, shards - 1, one, 0)
        own_copy(kind).start()

    def wait_far(kind):
        def one(d, _):
            far_copy(kind, d).wait()
            return _

        lax.fori_loop(0, shards - 1, one, 0)
        own_copy(kind).wait()

    def product(h, step, low, high):
        left = piece if step == 0 else got.at[step - 1]
        side = min(256, width)
        tiles = width // side

        def tile(n, _):
            which = low + n // tiles
            column = pl.ds(pl.multiple_of((n % tiles) * side, side), side)
            part = jnp.dot(
                left[pl.ds(h * half, half), :],
                held[which, step, :, column],
                preferred_element_type=jnp.float32,
            )
            if step > 0:
                part = part + acc[h, which, :, column]
            acc[h, which, :, column] = part
            return _

        lax.fori_loop(0, (high - low) * tiles, tile, 0)

    def squared(h, which):
        total = jnp.zeros((half, head), jnp.float32)
        for at in range(width // head):
            part = acc[h, which, :, at * head : (at + 1) * head]
            total = total + part * part
        return jnp.sum(total, axis=1, keepdims=True)

    def sum_copy(h, at, peer):
        return pltpu.make_async_remote_copy(
            src_ref=sums.at[h, 0],
            dst_ref=sums.at[h, at + 1],
            send_sem=sum_send.at[h, at],
            recv_sem=sum_recv.at[h, at],
            device_id={"rep": peer},
            device_id_type=MESH,
        )

    def sum_copies(h):
        return [sum_copy(h, at, peer) for at, peer in enumerate((right, over, cross))]

    def rotate_half(h):
        total = sums[h, 0] + sums[h, 1] + sums[h, 2] + sums[h, 3]
        scales = lax.rsqrt(total / full_width + EPSILON)
        scales = jnp.concatenate([scales] * (128 // 8), axis=0).T
        mine = pl.ds(h * half, half)
        for which, gain in ((0, q_gain), (1, k_gain)):
            scale = scales[:, which : which + 1]

            def one(at, _):
                column = pl.ds(pl.multiple_of(at * head, head), head)
                normed = acc[h, which + 1, :, column] * scale * gain[:, column]
                other = pltpu.roll(normed, head // 2, 1)
                turned[which, mine, column] = (
                    normed * cosine[mine, :] + other * sine[mine, :]
                ).astype(jnp.bfloat16)
                return _

            lax.fori_loop(0, width // head, one, 0)

    def finish_value(h):
        value[pl.ds(h * half, half), :] = acc[h, 0].astype(jnp.bfloat16)

    for copy in own_copies(0):
        copy.start()
    send_far(7)
    send_far(6)
    angles = where[...] * frequency[...]
    lane = lax.broadcasted_iota(jnp.int32, (rows, head), 1)
    cosine[...] = jnp.cos(angles)
    turn = jnp.sin(angles)
    sine[...] = jnp.where(lane < head // 2, -turn, turn)

    for which in range(3):
        load(which, 0).wait()
    product(0, 0, 0, 3)
    for h in range(2):
        if h == 1:
            product(1, 0, 0, 3)
            for copy in sum_copies(0):
                copy.wait()
            rotate_half(0)
            send_far(4)
            send_far(2)
        else:
            for copy in own_copies(0):
                copy.wait_recv()
            for copy in forwards(0):
                copy.start()
            for copy in own_copies(1):
                copy.start()
        for step in (1, 2):
            if h == 0:
                for which in range(3):
                    load(which, step).wait()
            product(h, step, 0, 3)
        for copy in forwards(h):
            copy.wait_recv()
        if h == 0:
            for which in range(3):
                load(which, 3).wait()
        product(h, 3, 0, 1)
        finish_value(h)
        send_far(h)
        product(h, 3, 1, 3)
        sums[h, 0] = turned_sums([squared(h, 1), squared(h, 2)])
        for copy in sum_copies(h):
            copy.start()
        if h == 0:
            for copy in own_copies(1):
                copy.wait_recv()
            for copy in forwards(1):
                copy.start()
    for copy in sum_copies(1):
        copy.wait()
    rotate_half(1)
    send_far(5)
    send_far(3)
    flat = (
        pltpu.make_async_copy(turned.at[1], k_flat, flat_sem.at[0]),
        pltpu.make_async_copy(value, v_flat, flat_sem.at[1]),
    )
    for copy in flat:
        copy.start()
    for h in range(2):
        for copy in own_copies(h) + forwards(h):
            copy.wait_send()
    for kind in range(8):
        wait_far(kind)
    for copy in flat:
        copy.wait()


def project_heads(piece, w_value, w_query, w_key, q_gain, k_gain, where, frequency, meta, shards):
    rows, width = piece.shape
    full_width = w_query.shape[0]
    half = rows // 2
    head = HEAD_DIM
    inside = pl.BlockSpec(memory_space=pltpu.VMEM)
    outside = pl.BlockSpec(memory_space=pl.ANY)
    dma = pltpu.SemaphoreType.DMA
    return pl.pallas_call(
        functools.partial(project_kernel, shards=shards, full_width=full_width),
        out_shape=(
            jax.ShapeDtypeStruct((shards, rows, 2 * head), jnp.bfloat16),
            jax.ShapeDtypeStruct((shards, rows, head), jnp.bfloat16),
            jax.ShapeDtypeStruct((shards, rows // shards, width), jnp.bfloat16),
            jax.ShapeDtypeStruct((shards,) + meta.shape, jnp.int32),
            jax.ShapeDtypeStruct((rows, width), jnp.bfloat16),
            jax.ShapeDtypeStruct((rows, width), jnp.bfloat16),
        ),
        in_specs=[inside, outside, outside, outside] + [inside] * 5,
        out_specs=(outside,) * 6,
        scratch_shapes=[
            pltpu.VMEM((3, 4, width, width), jnp.bfloat16),
            pltpu.VMEM((3, rows, width), jnp.bfloat16),
            pltpu.VMEM((2, 3, half, width), jnp.float32),
            pltpu.VMEM((2, rows, width), jnp.bfloat16),
            pltpu.VMEM((rows, width), jnp.bfloat16),
            pltpu.VMEM((rows, head), jnp.float32),
            pltpu.VMEM((rows, head), jnp.float32),
            pltpu.VMEM((2, 4, 8, half), jnp.float32),
            dma((3, 4)),
            dma((8,)),
            dma((8,)),
            dma((2, 3)),
            dma((2, 3)),
            dma((8, shards - 1)),
            dma((8, shards - 1)),
            dma((8,)),
            dma((2,)),
        ],
        compiler_params=pltpu.CompilerParams(
            collective_id=1, has_side_effects=True, vmem_limit_bytes=50 << 20
        ),
        cost_estimate=pl.CostEstimate(
            flops=6 * rows * full_width * width,
            bytes_accessed=6 * full_width * width + 16 * rows * width,
            transcendentals=0,
        ),
    )(piece, w_value, w_query, w_key, q_gain, k_gain, where, frequency, meta)


def body_heads(
    hidden_in,
    w_query,
    w_key,
    w_value,
    w_out,
    q_gain,
    k_gain,
    post_gain,
    prompt_lengths,
    segment_ids,
    deal,
    inverse,
    slots,
):
    tok_rows, width_dev = hidden_in.shape
    full_width = w_query.shape[0]
    head_size = HEAD_DIM
    shards = lax.axis_size("tok")
    chunk = tok_rows // shards
    me = lax.axis_index("tok")
    first_row = me * tok_rows

    local = jnp.arange(tok_rows, dtype=jnp.int32)
    starts = starts_of(prompt_lengths)
    my_packed = lax.dynamic_slice_in_dim(deal, first_row, tok_rows)
    my_slots = lax.dynamic_slice_in_dim(slots, first_row, tok_rows)

    def ranking(keys):
        return jnp.sum((keys[None, :] < keys[:, None]).astype(jnp.int32), axis=1)

    sort_hits = ranking(my_packed)[None, :] == local[:, None]
    sorted_packed = jnp.sum(jnp.where(sort_hits, my_packed[None, :], 0), axis=1)
    sorted_slots = jnp.sum(jnp.where(sort_hits, my_slots[None, :], 0), axis=1)
    slot_hits = ranking(sorted_slots)[None, :] == local[:, None]
    slots_rising = jnp.sum(jnp.where(slot_hits, sorted_slots[None, :], 0), axis=1)
    my_start = jnp.max(
        jnp.where(starts[None, :] <= sorted_packed[:, None], starts[None, :], 0), axis=1
    )
    positions = (sorted_packed - my_start).astype(jnp.float32)
    meta = jnp.concatenate(
        [sorted_packed[None], slots_rising[None], jnp.zeros((6, tok_rows), jnp.int32)], axis=0
    )
    half_size = head_size // 2
    frequency = ROPE_BASE ** (-jnp.arange(half_size, dtype=jnp.float32) * 2.0 / head_size)
    frequency = jnp.concatenate([frequency, frequency])[None, :]

    piece = select_rows(sort_hits, hidden_in)
    qk_rows, v_rows, sent_hidden, meta_all, key_flat, value_half = project_heads(
        piece,
        w_value,
        w_query,
        w_key,
        q_gain[None, :],
        k_gain[None, :],
        positions[:, None],
        frequency,
        meta,
        shards,
    )

    target = meta_all[:, 0, :].reshape(shards, shards, chunk).transpose(1, 0, 2)
    target = target.reshape(shards, tok_rows) - (
        jnp.arange(shards, dtype=jnp.int32)[:, None] * tok_rows
    )
    slot_target = lax.dynamic_slice_in_dim(meta_all[:, 1, :], me * chunk, chunk, axis=1)
    slot_target = slot_target.reshape(tok_rows) - first_row
    my_target = lax.dynamic_index_in_dim(target, me, 0, keepdims=False)
    my_hits = my_target[None, :] == local[:, None]

    def exchange(rows):
        return lax.all_to_all(rows, "tok", split_axis=0, concat_axis=0, tiled=True)

    packed_hidden = select_rows(my_hits, sent_hidden.reshape(tok_rows, width_dev))

    parts = 2
    share = tok_rows // parts
    heads_out = [
        attend_head(starts, target[:, None, :], qk_rows, v_rows, part, parts).reshape(
            shards, share, head_size
        )
        for part in range(parts)
    ]
    first, last = lax.optimization_barrier((exchange(heads_out[0]), heads_out[1]))
    attended = [first, exchange(last)]
    attended[-1], key_flat, value_half = lax.optimization_barrier(
        (attended[-1], key_flat, value_half)
    )
    mixed = []
    for rows in attended:
        rows = rows.transpose(1, 0, 2).reshape(share, width_dev)
        mixed.append(
            lax.psum_scatter(
                lax.dot_general(
                    w_out, rows, (((0,), (1,)), ((), ())), preferred_element_type=jnp.float32
                ).astype(jnp.bfloat16),
                "rep",
                scatter_dimension=0,
                tiled=True,
            )
        )
    cache_hits = slot_target[None, :] == local[:, None]
    sent_keys, sent_values = [
        exchange(select_rows(slot_hits, rows).reshape(shards, chunk, width_dev)).reshape(
            tok_rows, width_dev
        )
        for rows in (key_flat, value_half)
    ]
    mixed_rows = jnp.concatenate([rows.astype(jnp.float32).T for rows in mixed], axis=0)
    mixed_sums = lax.psum(jnp.sum(mixed_rows * mixed_rows, axis=1), "rep")
    normed_rows = (
        mixed_rows * lax.rsqrt(mixed_sums / full_width + EPSILON)[:, None] * post_gain[None, :]
    )
    output = (packed_hidden.astype(jnp.float32) + normed_rows).astype(jnp.bfloat16)
    output, sent_keys = lax.optimization_barrier((output, sent_keys))
    cache_keys = select_rows(cache_hits, sent_keys)
    cache_values = select_rows(cache_hits, sent_values)
    return (output, cache_keys, cache_values)


def solution(mesh):
    def pick(*operands):
        heads_dev = operands[0].shape[1] // HEAD_DIM
        fits = heads_dev == mesh.shape["tok"] and mesh.shape["rep"] == 4
        chosen = body_heads if fits else body
        return chosen(*operands)

    return jax.shard_map(
        pick,
        mesh=mesh,
        in_specs=(
            P("tok", "rep"),
            P(None, "rep"),
            P(None, "rep"),
            P(None, "rep"),
            P("rep", None),
            P("rep"),
            P("rep"),
            P("rep"),
            P(),
            P(),
            P(),
            P(),
            P(),
        ),
        out_specs=(P("tok", "rep"), P("tok", "rep"), P("tok", "rep")),
        check_vma=False,
    )
```

```python
import functools
import math

import jax
import jax.numpy as jnp
from jax import lax
from jax.experimental import pallas as pl
from jax.experimental.pallas import tpu as pltpu
from jax.sharding import PartitionSpec as P

HEAD_DIM = 128


EPSILON = 1e-06
ROPE_BASE = 500000.0


def rotate(values, positions):
    half_size = values.shape[-1] // 2
    frequency = ROPE_BASE ** (-jnp.arange(half_size, dtype=jnp.float32) * 2.0 / values.shape[-1])
    angles = positions.astype(jnp.float32)[:, None] * frequency[None, :]
    cosine = jnp.cos(angles)[:, None, :]
    sine_part = jnp.sin(angles)[:, None, :]
    lower_half = values[..., :half_size]
    upper_half = values[..., half_size:]
    return jnp.concatenate(
        [
            lower_half * cosine - upper_half * sine_part,
            upper_half * cosine + lower_half * sine_part,
        ],
        axis=-1,
    )


def starts_of(lengths):
    index = jnp.arange(lengths.shape[0], dtype=jnp.int32)
    return jnp.sum(jnp.where(index[None, :] < index[:, None], lengths[None, :], 0), axis=1)


def bucketed(table_rows, row_order, shards):
    picked = table_rows[row_order]
    return picked.reshape(shards, picked.shape[0] // shards, picked.shape[1])


def placement_order(sources, shard_rows):
    local_ids = jnp.arange(sources.shape[0], dtype=jnp.int32)
    arrival = jnp.argsort(sources * shard_rows + local_ids)
    return jnp.argsort(arrival)


def body(
    hidden_in,
    w_query,
    w_key,
    w_value,
    w_out,
    q_gain,
    k_gain,
    post_gain,
    prompt_lengths,
    segment_ids,
    deal,
    inverse,
    slots,
):
    tok_rows, width_dev = hidden_in.shape
    full_width = w_query.shape[0]
    head_size = HEAD_DIM
    heads_dev = width_dev // head_size
    shards = lax.axis_size("tok")
    first_row = lax.axis_index("tok") * tok_rows
    my_packed = lax.dynamic_slice_in_dim(deal, first_row, tok_rows)
    my_segment = segment_ids[my_packed]
    prompt_ids = jnp.arange(prompt_lengths.shape[0], dtype=jnp.int32)
    prompt_starts = starts_of(prompt_lengths)
    my_start = jnp.sum(
        jnp.where(my_segment[:, None] == prompt_ids[None, :], prompt_starts[None, :], 0), axis=1
    )
    positions = my_packed - my_start
    pieces = lax.all_gather(hidden_in, "rep", axis=1, tiled=True)
    query_rows = jnp.dot(pieces, w_query, preferred_element_type=jnp.float32)
    key_rows = jnp.dot(pieces, w_key, preferred_element_type=jnp.float32)
    value_rows = jnp.dot(pieces, w_value, preferred_element_type=jnp.float32)
    query_sums, key_sums = lax.psum(
        (jnp.sum(query_rows * query_rows, axis=1), jnp.sum(key_rows * key_rows, axis=1)), "rep"
    )
    query_rows = (
        query_rows * lax.rsqrt(query_sums / full_width + EPSILON)[:, None] * q_gain[None, :]
    )
    key_rows = key_rows * lax.rsqrt(key_sums / full_width + EPSILON)[:, None] * k_gain[None, :]
    query_rot = rotate(query_rows.reshape(tok_rows, heads_dev, head_size), positions).astype(
        jnp.bfloat16
    )
    key_rot = (
        rotate(key_rows.reshape(tok_rows, heads_dev, head_size), positions)
        .astype(jnp.bfloat16)
        .reshape(tok_rows, width_dev)
    )
    value_half = value_rows.astype(jnp.bfloat16)
    scale = head_size ** (-0.5)

    def attend(state_now, key_block, value_block, key_packed):
        row_top, totals, weighted = state_now
        block_keys = key_block.reshape(key_block.shape[0], heads_dev, head_size)
        block_values = value_block.reshape(value_block.shape[0], heads_dev, head_size)
        key_segment = segment_ids[key_packed]
        allowed = (key_segment[None, :] == my_segment[:, None]) & (
            key_packed[None, :] <= my_packed[:, None]
        )
        scores = (
            jnp.einsum("qhd,khd->hqk", query_rot, block_keys, preferred_element_type=jnp.float32)
            * scale
        )
        masked = jnp.where(allowed[None], scores, -1e30)
        new_top = jnp.maximum(row_top, jnp.max(masked, axis=2))
        weights = jnp.where(allowed[None], jnp.exp(masked - new_top[:, :, None]), 0.0)
        factor = jnp.exp(row_top - new_top)
        totals = totals * factor + jnp.sum(weights, axis=2)
        weighted = weighted * factor[:, :, None] + jnp.einsum(
            "hqk,khd->hqd",
            weights.astype(jnp.bfloat16),
            block_values,
            preferred_element_type=jnp.float32,
        )
        return (new_top, totals, weighted)

    start_state = (
        jnp.full((heads_dev, tok_rows), -1e30, jnp.float32),
        jnp.zeros((heads_dev, tok_rows), jnp.float32),
        jnp.zeros((heads_dev, tok_rows, head_size), jnp.float32),
    )
    owned_rows = lax.dynamic_slice_in_dim(jnp.argsort(slots), first_row, tok_rows)
    my_slots = lax.dynamic_slice_in_dim(slots, first_row, tok_rows)
    slot_order = jnp.argsort(my_slots)
    sent_keys, sent_values = (
        lax.all_to_all(
            bucketed(key_rot, slot_order, shards), "tok", split_axis=0, concat_axis=0, tiled=True
        ),
        lax.all_to_all(
            bucketed(value_half, slot_order, shards), "tok", split_axis=0, concat_axis=0, tiled=True
        ),
    )
    arrival = placement_order(owned_rows // tok_rows, tok_rows)
    cache_keys = sent_keys.reshape(tok_rows, width_dev)[arrival]
    cache_values = sent_values.reshape(tok_rows, width_dev)[arrival]
    pieces = (
        lax.all_gather(key_rot, "tok", axis=0, tiled=True),
        lax.all_gather(value_half, "tok", axis=0, tiled=True),
    )
    key_all = pieces[0]
    block_size = math.gcd(key_all.shape[0], tok_rows)
    block_count = key_all.shape[0] // block_size

    def advance(state_in, block_set):
        return (attend(state_in, block_set[0], block_set[1], block_set[2]), None)

    state_out, _ = lax.scan(
        advance,
        start_state,
        (
            key_all.reshape(block_count, block_size, width_dev),
            pieces[1].reshape(block_count, block_size, width_dev),
            deal.reshape(block_count, block_size),
        ),
    )
    row_top, totals, weighted = state_out
    attended = (
        (weighted / totals[:, :, None])
        .transpose(1, 0, 2)
        .reshape(tok_rows, width_dev)
        .astype(jnp.bfloat16)
    )
    mixed_rows = (
        lax.psum_scatter(
            lax.dot_general(
                w_out, attended, (((0,), (1,)), ((), ())), preferred_element_type=jnp.float32
            ).astype(jnp.bfloat16),
            "rep",
            scatter_dimension=0,
            tiled=True,
        )
        .astype(jnp.float32)
        .T
    )
    mixed_sums = lax.psum(jnp.sum(mixed_rows * mixed_rows, axis=1), "rep")
    normed_rows = (
        mixed_rows * lax.rsqrt(mixed_sums / full_width + EPSILON)[:, None] * post_gain[None, :]
    )
    result_rows = (hidden_in.astype(jnp.float32) + normed_rows).astype(jnp.bfloat16)
    packed_order = jnp.argsort(my_packed)
    returned = lax.all_to_all(
        bucketed(result_rows, packed_order, shards), "tok", split_axis=0, concat_axis=0, tiled=True
    )
    my_dealt = lax.dynamic_slice_in_dim(inverse, first_row, tok_rows)
    output = returned.reshape(tok_rows, width_dev)[placement_order(my_dealt // tok_rows, tok_rows)]
    return (output, cache_keys, cache_values)


def select_rows(hits, rows):
    return jnp.dot(
        hits.astype(jnp.bfloat16), rows, preferred_element_type=jnp.float32
    ).astype(jnp.bfloat16)


MESH = pl.DeviceIdType.MESH


def greet(peers):
    barrier = pltpu.get_barrier_semaphore()
    for peer in peers:
        pl.semaphore_signal(barrier, inc=1, device_id=peer, device_id_type=MESH)
    pl.semaphore_wait(barrier, len(peers))


def places():
    corner = lax.axis_index("rep")
    right = corner + 1 - 2 * (corner % 2)
    over = corner + 2 - 4 * (corner // 2)
    return corner, right, over, 3 - corner


def turned_sums(columns):
    rows = columns[0].shape[0]
    lane = lax.broadcasted_iota(jnp.int32, (rows, 128), 1)
    wide = jnp.zeros((rows, 128), jnp.float32)
    for at, column in enumerate(columns):
        wide = jnp.where(lane == at, column, wide)
    return wide.T[0:8, :]


def project_kernel(
    piece, w_value, w_query, w_key, q_gain, k_gain, where, frequency, meta,
    qk_out, v_out, hid_out, meta_out, k_flat, v_flat,
    held, got, acc, turned, value, cosine, sine, sums,
    w_sem, near_send, near_recv, sum_send, sum_recv, far_send, far_recv, own_sem, flat_sem,
    *, shards, full_width,
):
    rows, width = piece.shape
    half = rows // 2
    quarter = half // 2
    chunk = rows // shards
    head = HEAD_DIM
    me = lax.axis_index("tok")
    corner, right, over, cross = places()
    weights = (w_value, w_query, w_key)
    owners = (corner, right, over, cross)

    def load(which, step):
        return pltpu.make_async_copy(
            weights[which].at[pl.ds(pl.multiple_of(owners[step] * width, width), width), :],
            held.at[which, step],
            w_sem.at[which, step],
        )

    for step in range(4):
        for which in range(3):
            load(which, step).start()

    others = [(me + 1 + d) % shards for d in range(shards - 1)]
    greet([{"rep": peer} for peer in (right, over, cross)] + [{"tok": peer} for peer in others])

    def near(src, slot, at, size, peer, sem):
        return pltpu.make_async_remote_copy(
            src_ref=src.at[pl.ds(at, size), :],
            dst_ref=got.at[slot, pl.ds(at, size), :],
            send_sem=near_send.at[sem],
            recv_sem=near_recv.at[sem],
            device_id={"rep": peer},
            device_id_type=MESH,
        )

    def own_copies(h):
        return (
            near(piece, 0, h * half, half, right, 4 * h),
            near(piece, 1, h * half, half, over, 4 * h + 1),
        )

    def forwards(h):
        return (
            near(got.at[1], 2, h * half, quarter, right, 4 * h + 2),
            near(got.at[0], 2, h * half + quarter, quarter, over, 4 * h + 3),
        )

    def to_far(kind, d, src, dst):
        return pltpu.make_async_remote_copy(
            src_ref=src,
            dst_ref=dst,
            send_sem=far_send.at[kind, d],
            recv_sem=far_recv.at[kind, d],
            device_id={"tok": (me + 1 + d) % shards},
            device_id_type=MESH,
        )

    def head_of(ref, h, owner):
        return ref.at[pl.ds(h * half, half), pl.ds(pl.multiple_of(owner * head, head), head)]

    def source_of(kind, peer):
        if kind < 2:
            return head_of(value, kind, peer)
        if kind < 6:
            return head_of(turned.at[(kind - 2) // 2], kind % 2, peer)
        if kind == 6:
            return piece.at[pl.ds(pl.multiple_of(peer * chunk, chunk), chunk), :]
        return meta

    def landing(kind):
        if kind < 2:
            return v_out.at[me, pl.ds(kind * half, half), :]
        if kind < 6:
            return qk_out.at[
                me, pl.ds((kind % 2) * half, half), pl.ds(((kind - 2) // 2) * head, head)
            ]
        return (hid_out if kind == 6 else meta_out).at[me]

    def own_copy(kind):
        return pltpu.make_async_copy(source_of(kind, me), landing(kind), own_sem.at[kind])

    def far_copy(kind, d):
        return to_far(kind, d, source_of(kind, (me + 1 + d) % shards), landing(kind))

    def send_far(kind):
        def one(d, _):
            far_copy(kind, d).start()
            return _

        lax.fori_loop(0, shards - 1, one, 0)
        own_copy(kind).start()

    def wait_far(kind):
        def one(d, _):
            far_copy(kind, d).wait()
            return _

        lax.fori_loop(0, shards - 1, one, 0)
        own_copy(kind).wait()

    def product(h, step, low, high):
        left = piece if step == 0 else got.at[step - 1]
        side = min(256, width)
        tiles = width // side

        def tile(n, _):
            which = low + n // tiles
            column = pl.ds(pl.multiple_of((n % tiles) * side, side), side)
            part = jnp.dot(
                left[pl.ds(h * half, half), :],
                held[which, step, :, column],
                preferred_element_type=jnp.float32,
            )
            if step > 0:
                part = part + acc[h, which, :, column]
            acc[h, which, :, column] = part
            return _

        lax.fori_loop(0, (high - low) * tiles, tile, 0)

    def squared(h, which):
        total = jnp.zeros((half, head), jnp.float32)
        for at in range(width // head):
            part = acc[h, which, :, at * head : (at + 1) * head]
            total = total + part * part
        return jnp.sum(total, axis=1, keepdims=True)

    def sum_copy(h, at, peer):
        return pltpu.make_async_remote_copy(
            src_ref=sums.at[h, 0],
            dst_ref=sums.at[h, at + 1],
            send_sem=sum_send.at[h, at],
            recv_sem=sum_recv.at[h, at],
            device_id={"rep": peer},
            device_id_type=MESH,
        )

    def sum_copies(h):
        return [sum_copy(h, at, peer) for at, peer in enumerate((right, over, cross))]

    def rotate_half(h):
        total = sums[h, 0] + sums[h, 1] + sums[h, 2] + sums[h, 3]
        scales = lax.rsqrt(total / full_width + EPSILON)
        scales = jnp.concatenate([scales] * (128 // 8), axis=0).T
        mine = pl.ds(h * half, half)
        for which, gain in ((0, q_gain), (1, k_gain)):
            scale = scales[:, which : which + 1]

            def one(at, _):
                column = pl.ds(pl.multiple_of(at * head, head), head)
                normed = acc[h, which + 1, :, column] * scale * gain[:, column]
                other = pltpu.roll(normed, head // 2, 1)
                turned[which, mine, column] = (
                    normed * cosine[mine, :] + other * sine[mine, :]
                ).astype(jnp.bfloat16)
                return _

            lax.fori_loop(0, width // head, one, 0)

    def finish_value(h):
        value[pl.ds(h * half, half), :] = acc[h, 0].astype(jnp.bfloat16)

    for copy in own_copies(0):
        copy.start()
    send_far(7)
    send_far(6)
    angles = where[...] * frequency[...]
    lane = lax.broadcasted_iota(jnp.int32, (rows, head), 1)
    cosine[...] = jnp.cos(angles)
    turn = jnp.sin(angles)
    sine[...] = jnp.where(lane < head // 2, -turn, turn)

    for which in range(3):
        load(which, 0).wait()
    product(0, 0, 0, 3)
    for h in range(2):
        if h == 1:
            product(1, 0, 0, 3)
            for copy in sum_copies(0):
                copy.wait()
            rotate_half(0)
            send_far(4)
            send_far(2)
        else:
            for copy in own_copies(0):
                copy.wait_recv()
            for copy in forwards(0):
                copy.start()
            for copy in own_copies(1):
                copy.start()
        for step in (1, 2):
            if h == 0:
                for which in range(3):
                    load(which, step).wait()
            product(h, step, 0, 3)
        for copy in forwards(h):
            copy.wait_recv()
        if h == 0:
            for which in range(3):
                load(which, 3).wait()
        product(h, 3, 0, 1)
        finish_value(h)
        send_far(h)
        product(h, 3, 1, 3)
        sums[h, 0] = turned_sums([squared(h, 1), squared(h, 2)])
        for copy in sum_copies(h):
            copy.start()
        if h == 0:
            for copy in own_copies(1):
                copy.wait_recv()
            for copy in forwards(1):
                copy.start()
    for copy in sum_copies(1):
        copy.wait()
    rotate_half(1)
    send_far(5)
    send_far(3)
    flat = (
        pltpu.make_async_copy(turned.at[1], k_flat, flat_sem.at[0]),
        pltpu.make_async_copy(value, v_flat, flat_sem.at[1]),
    )
    for copy in flat:
        copy.start()
    for h in range(2):
        for copy in own_copies(h) + forwards(h):
            copy.wait_send()
    for kind in range(8):
        wait_far(kind)
    for copy in flat:
        copy.wait()


def project_heads(piece, w_value, w_query, w_key, q_gain, k_gain, where, frequency, meta, shards):
    rows, width = piece.shape
    full_width = w_query.shape[0]
    half = rows // 2
    head = HEAD_DIM
    inside = pl.BlockSpec(memory_space=pltpu.VMEM)
    outside = pl.BlockSpec(memory_space=pl.ANY)
    dma = pltpu.SemaphoreType.DMA
    return pl.pallas_call(
        functools.partial(project_kernel, shards=shards, full_width=full_width),
        out_shape=(
            jax.ShapeDtypeStruct((shards, rows, 2 * head), jnp.bfloat16),
            jax.ShapeDtypeStruct((shards, rows, head), jnp.bfloat16),
            jax.ShapeDtypeStruct((shards, rows // shards, width), jnp.bfloat16),
            jax.ShapeDtypeStruct((shards,) + meta.shape, jnp.int32),
            jax.ShapeDtypeStruct((rows, width), jnp.bfloat16),
            jax.ShapeDtypeStruct((rows, width), jnp.bfloat16),
        ),
        in_specs=[inside, outside, outside, outside] + [inside] * 5,
        out_specs=(outside,) * 6,
        scratch_shapes=[
            pltpu.VMEM((3, 4, width, width), jnp.bfloat16),
            pltpu.VMEM((3, rows, width), jnp.bfloat16),
            pltpu.VMEM((2, 3, half, width), jnp.float32),
            pltpu.VMEM((2, rows, width), jnp.bfloat16),
            pltpu.VMEM((rows, width), jnp.bfloat16),
            pltpu.VMEM((rows, head), jnp.float32),
            pltpu.VMEM((rows, head), jnp.float32),
            pltpu.VMEM((2, 4, 8, half), jnp.float32),
            dma((3, 4)),
            dma((8,)),
            dma((8,)),
            dma((2, 3)),
            dma((2, 3)),
            dma((8, shards - 1)),
            dma((8, shards - 1)),
            dma((8,)),
            dma((2,)),
        ],
        compiler_params=pltpu.CompilerParams(
            collective_id=1, has_side_effects=True, vmem_limit_bytes=50 << 20
        ),
        cost_estimate=pl.CostEstimate(
            flops=6 * rows * full_width * width,
            bytes_accessed=6 * full_width * width + 16 * rows * width,
            transcendentals=0,
        ),
    )(piece, w_value, w_query, w_key, q_gain, k_gain, where, frequency, meta)


def finish_kernel(
    qk_in, v_in, hid_in, keys_in, values_in, w_out, post_gain, orders, begins,
    out, cache_keys, cache_values,
    qk_rows, v_rows, hidden, flat, picked, landed, hits,
    queries, keys, values, scores, heads, attended, held,
    mine, sent, first_got, second_got, sums, placed,
    in_sem, w_sem, far_send, far_recv, own_sem, near_send, near_recv, sum_send, sum_recv, out_sem,
    *, shards, full_width,
):
    rows, width = attended.shape
    half = rows // 2
    side = width // 2
    chunk = rows // shards
    head = HEAD_DIM
    reach = shards // 2
    me = lax.axis_index("tok")
    corner, right, over, cross = places()
    owners = (cross, right, over, corner)

    loads = [
        pltpu.make_async_copy(src, dst, in_sem.at[at])
        for at, (src, dst) in enumerate(
            (
                (values_in, flat.at[1]),
                (qk_in, qk_rows),
                (v_in, v_rows),
                (keys_in, flat.at[0]),
                (hid_in, hidden),
            )
        )
    ]
    for copy in loads:
        copy.start()

    def load(step):
        return pltpu.make_async_copy(
            w_out.at[:, pl.ds(pl.multiple_of(owners[step] * width, width), width)],
            held.at[step],
            w_sem.at[step],
        )

    for step in range(4):
        load(step).start()
    others = [(me + 1 + d) % shards for d in range(shards - 1)]
    greet([{"rep": peer} for peer in (right, over, cross)] + [{"tok": peer} for peer in others])

    def source_of(kind, peer):
        if kind < 2:
            return picked.at[kind, pl.ds(pl.multiple_of(peer * chunk, chunk), chunk), :]
        return heads.at[kind - 2, peer]

    def landing(kind):
        if kind < 2:
            return landed.at[kind, pl.ds(pl.multiple_of(me * chunk, chunk), chunk), :]
        return attended.at[
            pl.ds((kind - 2) * half, half), pl.ds(pl.multiple_of(me * head, head), head)
        ]

    def own_copy(kind):
        return pltpu.make_async_copy(source_of(kind, me), landing(kind), own_sem.at[kind])

    def far_copy(kind, d):
        peer = (me + 1 + d) % shards
        return pltpu.make_async_remote_copy(
            src_ref=source_of(kind, peer),
            dst_ref=landing(kind),
            send_sem=far_send.at[kind, d],
            recv_sem=far_recv.at[kind, d],
            device_id={"tok": peer},
            device_id_type=MESH,
        )

    def send_far(kind):
        def one(d, _):
            far_copy(kind, d).start()
            return _

        lax.fori_loop(0, shards - 1, one, 0)
        own_copy(kind).start()

    def wait_far(kind):
        def one(d, _):
            far_copy(kind, d).wait()
            return _

        lax.fori_loop(0, shards - 1, one, 0)
        own_copy(kind).wait()

    def aim(order):
        row = lax.broadcasted_iota(jnp.int32, (rows, rows), 0)
        hits[...] = jnp.where(row == order, 1.0, 0.0).astype(jnp.bfloat16)

    def select(src, dst):
        tile = min(256, width)

        def one(n, _):
            column = pl.ds(pl.multiple_of(n * tile, tile), tile)
            dst[:, column] = jnp.dot(
                hits[...], src[:, column], preferred_element_type=jnp.float32
            ).astype(jnp.bfloat16)
            return _

        lax.fori_loop(0, width // tile, one, 0)

    loads[0].wait()
    aim(orders[shards : shards + 1, :])
    select(flat.at[1], picked.at[1])
    send_far(1)

    loads[1].wait()
    loads[2].wait()

    def pack(block, _):
        aim(orders[pl.ds(block, 1), :])
        at = pl.ds(pl.multiple_of(block * chunk, chunk), chunk)
        into = pl.ds(pl.multiple_of(block * rows, rows), rows)
        both = jnp.dot(
            hits[...],
            qk_rows[:, at, :].reshape(rows, 2 * head),
            preferred_element_type=jnp.float32,
        ).astype(jnp.bfloat16)
        queries[into, :] = both[:, :head]
        keys[into, :] = both[:, head:]
        values[:, into] = (
            jnp.dot(
                hits[...],
                v_rows[:, at, :].reshape(rows, head),
                preferred_element_type=jnp.float32,
            )
            .T.astype(jnp.bfloat16)
        )
        return _

    lax.fori_loop(0, shards, pack, 0)
    scale = head ** (-0.5) * math.log2(math.e)

    def attend(part):
        depth = half * (part + 1)

        def folded(tile, fold):
            return fold(tile.reshape(tile.shape[0] // 8, 8, half), axis=0)

        def block(b, _):
            query = queries[pl.ds(pl.multiple_of(b * rows + part * half, half), half), :]
            begin = begins[pl.ds(2 * b + part, 1), :]
            steps = b - (b // reach) * (b - reach)

            def score(base, count):
                return lax.dot_general(
                    keys[pl.ds(base, count), :],
                    query,
                    (((1,), (1,)), ((), ())),
                    preferred_element_type=jnp.float32,
                )

            base = pl.multiple_of(b * rows, rows)
            key_row = lax.broadcasted_iota(jnp.int32, (depth, half), 0)
            query_row = lax.broadcasted_iota(jnp.int32, (depth, half), 1) + part * half
            seen = (key_row >= begin - base) & (key_row <= query_row)
            last = jnp.where(seen, score(base, depth), -1e30)
            scores[reach * rows : reach * rows + depth, :] = last

            def first_pass(step, top):
                base = pl.multiple_of((b - 1 - step) * rows, rows)
                key_row = lax.broadcasted_iota(jnp.int32, (rows, half), 0)
                tile = jnp.where(key_row >= begin - base, score(base, rows), -1e30)
                scores[pl.ds(pl.multiple_of(step * rows, rows), rows), :] = tile
                return jnp.maximum(top, folded(tile, jnp.max))

            top = lax.fori_loop(0, steps, first_pass, folded(last, jnp.max))
            top = jnp.max(top, axis=0, keepdims=True)

            def weigh(tile, base, count):
                weights = jnp.exp2((tile - top) * scale)
                return folded(weights, jnp.sum), jnp.dot(
                    values[:, pl.ds(base, count)],
                    weights.astype(jnp.bfloat16),
                    preferred_element_type=jnp.float32,
                )

            def second_pass(step, state):
                base = pl.multiple_of((b - 1 - step) * rows, rows)
                tile = scores[pl.ds(pl.multiple_of(step * rows, rows), rows), :]
                total, weighted = weigh(tile, base, rows)
                return state[0] + total, state[1] + weighted

            state = weigh(scores[reach * rows : reach * rows + depth, :], base, depth)
            total, weighted = lax.fori_loop(0, steps, second_pass, state)
            total = jnp.sum(total, axis=0, keepdims=True)
            heads[part, b] = (weighted / total).T.astype(jnp.bfloat16)
            return _

        lax.fori_loop(0, shards, block, 0)

    def project(part):
        tile = min(256, width)

        def one(n, _):
            step = n // (width // tile)
            column = pl.ds(pl.multiple_of((n % (width // tile)) * tile, tile), tile)
            done = jnp.dot(
                attended[pl.ds(part * half, half), :],
                held[step, :, column],
                preferred_element_type=jnp.float32,
            )
            mine[part, :, column] = done
            sent[part, step, :, column] = done.astype(jnp.bfloat16)
            return _

        lax.fori_loop(0, 4 * (width // tile), one, 0)

    def near(src, dst, peer, sem):
        return pltpu.make_async_remote_copy(
            src_ref=src,
            dst_ref=dst,
            send_sem=near_send.at[sem],
            recv_sem=near_recv.at[sem],
            device_id={"rep": peer},
            device_id_type=MESH,
        )

    left, rest = pl.ds(0, side), pl.ds(side, side)

    def first_copies(part):
        return (
            near(sent.at[part, 0, :, left], first_got.at[part, 0], right, 6 * part),
            near(sent.at[part, 1, :, left], first_got.at[part, 1], right, 6 * part + 1),
            near(sent.at[part, 0, :, rest], first_got.at[part, 2], over, 6 * part + 2),
            near(sent.at[part, 2, :, rest], first_got.at[part, 3], over, 6 * part + 3),
        )

    def second_copies(part):
        return (
            near(sent.at[part, 2, :, left], second_got.at[part, 0], over, 6 * part + 4),
            near(sent.at[part, 1, :, rest], second_got.at[part, 1], right, 6 * part + 5),
        )

    def start(copies):
        for copy in copies:
            copy.start()

    def middle(part):
        for copy in first_copies(part):
            copy.wait_recv()
        for step, column, at in ((2, left, 0), (1, rest, 2)):
            sent[part, step, :, column] = (
                sent[part, step, :, column].astype(jnp.float32)
                + first_got[part, at].astype(jnp.float32)
            ).astype(jnp.bfloat16)
        start(second_copies(part))
        for column, at in ((left, 1), (rest, 3)):
            mine[part, :, column] = mine[part, :, column] + first_got[part, at].astype(jnp.float32)

    def sum_copies(part):
        return [
            pltpu.make_async_remote_copy(
                src_ref=sums.at[part, 0],
                dst_ref=sums.at[part, at + 1],
                send_sem=sum_send.at[part, at],
                recv_sem=sum_recv.at[part, at],
                device_id={"rep": peer},
                device_id_type=MESH,
            )
            for at, peer in enumerate((right, over, cross))
        ]

    def total(part):
        for copy in second_copies(part):
            copy.wait_recv()
        squares = jnp.zeros((half, head), jnp.float32)
        for at in range(width // head):
            column = pl.ds(at * head, head)
            got = second_got[part, at * head // side, :, pl.ds(at * head % side, head)]
            rows_now = mine[part, :, column] + got.astype(jnp.float32)
            mine[part, :, column] = rows_now
            squares = squares + rows_now * rows_now
        sums[part, 0] = turned_sums([jnp.sum(squares, axis=1, keepdims=True)])
        start(sum_copies(part))

    def settle(part):
        for copy in sum_copies(part):
            copy.wait()
        whole = sums[part, 0] + sums[part, 1] + sums[part, 2] + sums[part, 3]
        scales = lax.rsqrt(whole / full_width + EPSILON)
        scales = jnp.concatenate([scales] * (128 // 8), axis=0).T[:, 0:1]
        at = pl.ds(part * half, half)
        placed[0, at, :] = (
            hidden[at, :].astype(jnp.float32) + mine[part] * scales * post_gain[...]
        ).astype(jnp.bfloat16)

    def results(which):
        return pltpu.make_async_copy(
            placed.at[which], (out, cache_keys, cache_values)[which], out_sem.at[which]
        )

    attend(0)
    send_far(2)
    attend(1)
    send_far(3)
    loads[3].wait()
    aim(orders[shards : shards + 1, :])
    select(flat.at[0], picked.at[0])
    loads[4].wait()
    aim(orders[pl.ds(me, 1), :])
    select(hidden, flat.at[1])
    hidden[...] = flat[1]
    for step in range(4):
        load(step).wait()
    wait_far(2)
    project(0)
    start(first_copies(0))
    wait_far(3)
    send_far(0)
    project(1)
    start(first_copies(1))
    middle(0)
    total(0)
    middle(1)
    settle(0)
    aim(orders[shards + 1 : shards + 2, :])
    wait_far(1)
    select(landed.at[1], placed.at[2])
    results(2).start()
    total(1)
    settle(1)
    results(0).start()
    wait_far(0)
    select(landed.at[0], placed.at[1])
    results(1).start()
    for part in range(2):
        for copy in first_copies(part) + second_copies(part):
            copy.wait_send()
    for which in range(3):
        results(which).wait()


def finish_heads(
    qk_rows, v_rows, hid_rows, key_flat, value_flat, w_out, post_gain, orders, begins
):
    shards, rows, head = v_rows.shape
    width, full_width = w_out.shape
    half = rows // 2
    reach = shards // 2
    inside = pl.BlockSpec(memory_space=pltpu.VMEM)
    outside = pl.BlockSpec(memory_space=pl.ANY)
    dma = pltpu.SemaphoreType.DMA
    return pl.pallas_call(
        functools.partial(finish_kernel, shards=shards, full_width=full_width),
        out_shape=(jax.ShapeDtypeStruct((rows, width), jnp.bfloat16),) * 3,
        in_specs=[outside] * 6 + [inside] * 3,
        out_specs=(outside,) * 3,
        scratch_shapes=[
            pltpu.VMEM((shards, rows, 2 * head), jnp.bfloat16),
            pltpu.VMEM((shards, rows, head), jnp.bfloat16),
            pltpu.VMEM((rows, width), jnp.bfloat16),
            pltpu.VMEM((2, rows, width), jnp.bfloat16),
            pltpu.VMEM((2, rows, width), jnp.bfloat16),
            pltpu.VMEM((2, rows, width), jnp.bfloat16),
            pltpu.VMEM((rows, rows), jnp.bfloat16),
            pltpu.VMEM((shards * rows, head), jnp.bfloat16),
            pltpu.VMEM((shards * rows, head), jnp.bfloat16),
            pltpu.VMEM((head, shards * rows), jnp.bfloat16),
            pltpu.VMEM(((reach + 1) * rows, half), jnp.float32),
            pltpu.VMEM((2, shards, half, head), jnp.bfloat16),
            pltpu.VMEM((rows, width), jnp.bfloat16),
            pltpu.VMEM((4, width, width), jnp.bfloat16),
            pltpu.VMEM((2, half, width), jnp.float32),
            pltpu.VMEM((2, 4, half, width), jnp.bfloat16),
            pltpu.VMEM((2, 4, half, width // 2), jnp.bfloat16),
            pltpu.VMEM((2, 2, half, width // 2), jnp.bfloat16),
            pltpu.VMEM((2, 4, 8, half), jnp.float32),
            pltpu.VMEM((3, rows, width), jnp.bfloat16),
            dma((5,)),
            dma((4,)),
            dma((4, shards - 1)),
            dma((4, shards - 1)),
            dma((4,)),
            dma((12,)),
            dma((12,)),
            dma((2, 3)),
            dma((2, 3)),
            dma((3,)),
        ],
        compiler_params=pltpu.CompilerParams(
            collective_id=2, has_side_effects=True, vmem_limit_bytes=52 << 20
        ),
        cost_estimate=pl.CostEstimate(
            flops=2 * rows * full_width * width + 20 * rows * rows * shards * head,
            bytes_accessed=2 * full_width * width + 20 * rows * width,
            transcendentals=5 * rows * rows * shards,
        ),
    )(qk_rows, v_rows, hid_rows, key_flat, value_flat, w_out, post_gain, orders, begins)


def body_heads(
    hidden_in,
    w_query,
    w_key,
    w_value,
    w_out,
    q_gain,
    k_gain,
    post_gain,
    prompt_lengths,
    segment_ids,
    deal,
    inverse,
    slots,
):
    tok_rows, width_dev = hidden_in.shape
    full_width = w_query.shape[0]
    head_size = HEAD_DIM
    shards = lax.axis_size("tok")
    chunk = tok_rows // shards
    me = lax.axis_index("tok")
    first_row = me * tok_rows

    local = jnp.arange(tok_rows, dtype=jnp.int32)
    starts = starts_of(prompt_lengths)
    my_packed = lax.dynamic_slice_in_dim(deal, first_row, tok_rows)
    my_slots = lax.dynamic_slice_in_dim(slots, first_row, tok_rows)

    def ranking(keys):
        return jnp.sum((keys[None, :] < keys[:, None]).astype(jnp.int32), axis=1)

    sort_hits = ranking(my_packed)[None, :] == local[:, None]
    sorted_packed = jnp.sum(jnp.where(sort_hits, my_packed[None, :], 0), axis=1)
    sorted_slots = jnp.sum(jnp.where(sort_hits, my_slots[None, :], 0), axis=1)
    slot_rank = ranking(sorted_slots)
    slot_hits = slot_rank[None, :] == local[:, None]
    slots_rising = jnp.sum(jnp.where(slot_hits, sorted_slots[None, :], 0), axis=1)
    my_start = jnp.max(
        jnp.where(starts[None, :] <= sorted_packed[:, None], starts[None, :], 0), axis=1
    )
    positions = (sorted_packed - my_start).astype(jnp.float32)
    meta = jnp.concatenate(
        [sorted_packed[None], slots_rising[None], jnp.zeros((6, tok_rows), jnp.int32)], axis=0
    )
    half_size = head_size // 2
    frequency = ROPE_BASE ** (-jnp.arange(half_size, dtype=jnp.float32) * 2.0 / head_size)
    frequency = jnp.concatenate([frequency, frequency])[None, :]

    piece = select_rows(sort_hits, hidden_in)
    qk_rows, v_rows, sent_hidden, meta_all, key_flat, value_half = project_heads(
        piece,
        w_value,
        w_query,
        w_key,
        q_gain[None, :],
        k_gain[None, :],
        positions[:, None],
        frequency,
        meta,
        shards,
    )

    target = meta_all[:, 0, :].reshape(shards, shards, chunk).transpose(1, 0, 2)
    target = target.reshape(shards, tok_rows) - (
        jnp.arange(shards, dtype=jnp.int32)[:, None] * tok_rows
    )
    slot_target = lax.dynamic_slice_in_dim(meta_all[:, 1, :], me * chunk, chunk, axis=1)
    slot_target = slot_target.reshape(1, tok_rows) - first_row
    orders = jnp.concatenate(
        [
            target,
            slot_rank[None],
            slot_target,
            jnp.zeros((-(shards + 2) % 8, tok_rows), jnp.int32),
        ],
        axis=0,
    )
    every = jnp.arange(shards * tok_rows, dtype=jnp.int32)
    begins = jnp.max(jnp.where(starts[:, None] <= every[None, :], starts[:, None], 0), axis=0)
    return finish_heads(
        qk_rows,
        v_rows,
        sent_hidden.reshape(tok_rows, width_dev),
        key_flat,
        value_half,
        w_out,
        post_gain[None, :],
        orders,
        begins.reshape(2 * shards, tok_rows // 2),
    )


def solution(mesh):
    def pick(*operands):
        heads_dev = operands[0].shape[1] // HEAD_DIM
        fits = heads_dev == mesh.shape["tok"] and mesh.shape["rep"] == 4
        chosen = body_heads if fits else body
        return chosen(*operands)

    return jax.shard_map(
        pick,
        mesh=mesh,
        in_specs=(
            P("tok", "rep"),
            P(None, "rep"),
            P(None, "rep"),
            P(None, "rep"),
            P("rep", None),
            P("rep"),
            P("rep"),
            P("rep"),
            P(),
            P(),
            P(),
            P(),
            P(),
        ),
        out_specs=(P("tok", "rep"), P("tok", "rep"), P("tok", "rep")),
        check_vma=False,
    )
```

```python
import functools
import math

import jax
import jax.numpy as jnp
from jax import lax
from jax.experimental import pallas as pl
from jax.experimental.pallas import tpu as pltpu
from jax.sharding import PartitionSpec as P

HEAD_DIM = 128


EPSILON = 1e-06
ROPE_BASE = 500000.0


def rotate(values, positions):
    half_size = values.shape[-1] // 2
    frequency = ROPE_BASE ** (-jnp.arange(half_size, dtype=jnp.float32) * 2.0 / values.shape[-1])
    angles = positions.astype(jnp.float32)[:, None] * frequency[None, :]
    cosine = jnp.cos(angles)[:, None, :]
    sine_part = jnp.sin(angles)[:, None, :]
    lower_half = values[..., :half_size]
    upper_half = values[..., half_size:]
    return jnp.concatenate(
        [
            lower_half * cosine - upper_half * sine_part,
            upper_half * cosine + lower_half * sine_part,
        ],
        axis=-1,
    )


def starts_of(lengths):
    index = jnp.arange(lengths.shape[0], dtype=jnp.int32)
    return jnp.sum(jnp.where(index[None, :] < index[:, None], lengths[None, :], 0), axis=1)


def bucketed(table_rows, row_order, shards):
    picked = table_rows[row_order]
    return picked.reshape(shards, picked.shape[0] // shards, picked.shape[1])


def placement_order(sources, shard_rows):
    local_ids = jnp.arange(sources.shape[0], dtype=jnp.int32)
    arrival = jnp.argsort(sources * shard_rows + local_ids)
    return jnp.argsort(arrival)


def body(
    hidden_in,
    w_query,
    w_key,
    w_value,
    w_out,
    q_gain,
    k_gain,
    post_gain,
    prompt_lengths,
    segment_ids,
    deal,
    inverse,
    slots,
):
    tok_rows, width_dev = hidden_in.shape
    full_width = w_query.shape[0]
    head_size = HEAD_DIM
    heads_dev = width_dev // head_size
    shards = lax.axis_size("tok")
    first_row = lax.axis_index("tok") * tok_rows
    my_packed = lax.dynamic_slice_in_dim(deal, first_row, tok_rows)
    my_segment = segment_ids[my_packed]
    prompt_ids = jnp.arange(prompt_lengths.shape[0], dtype=jnp.int32)
    prompt_starts = starts_of(prompt_lengths)
    my_start = jnp.sum(
        jnp.where(my_segment[:, None] == prompt_ids[None, :], prompt_starts[None, :], 0), axis=1
    )
    positions = my_packed - my_start
    pieces = lax.all_gather(hidden_in, "rep", axis=1, tiled=True)
    query_rows = jnp.dot(pieces, w_query, preferred_element_type=jnp.float32)
    key_rows = jnp.dot(pieces, w_key, preferred_element_type=jnp.float32)
    value_rows = jnp.dot(pieces, w_value, preferred_element_type=jnp.float32)
    query_sums, key_sums = lax.psum(
        (jnp.sum(query_rows * query_rows, axis=1), jnp.sum(key_rows * key_rows, axis=1)), "rep"
    )
    query_rows = (
        query_rows * lax.rsqrt(query_sums / full_width + EPSILON)[:, None] * q_gain[None, :]
    )
    key_rows = key_rows * lax.rsqrt(key_sums / full_width + EPSILON)[:, None] * k_gain[None, :]
    query_rot = rotate(query_rows.reshape(tok_rows, heads_dev, head_size), positions).astype(
        jnp.bfloat16
    )
    key_rot = (
        rotate(key_rows.reshape(tok_rows, heads_dev, head_size), positions)
        .astype(jnp.bfloat16)
        .reshape(tok_rows, width_dev)
    )
    value_half = value_rows.astype(jnp.bfloat16)
    scale = head_size ** (-0.5)

    def attend(state_now, key_block, value_block, key_packed):
        row_top, totals, weighted = state_now
        block_keys = key_block.reshape(key_block.shape[0], heads_dev, head_size)
        block_values = value_block.reshape(value_block.shape[0], heads_dev, head_size)
        key_segment = segment_ids[key_packed]
        allowed = (key_segment[None, :] == my_segment[:, None]) & (
            key_packed[None, :] <= my_packed[:, None]
        )
        scores = (
            jnp.einsum("qhd,khd->hqk", query_rot, block_keys, preferred_element_type=jnp.float32)
            * scale
        )
        masked = jnp.where(allowed[None], scores, -1e30)
        new_top = jnp.maximum(row_top, jnp.max(masked, axis=2))
        weights = jnp.where(allowed[None], jnp.exp(masked - new_top[:, :, None]), 0.0)
        factor = jnp.exp(row_top - new_top)
        totals = totals * factor + jnp.sum(weights, axis=2)
        weighted = weighted * factor[:, :, None] + jnp.einsum(
            "hqk,khd->hqd",
            weights.astype(jnp.bfloat16),
            block_values,
            preferred_element_type=jnp.float32,
        )
        return (new_top, totals, weighted)

    start_state = (
        jnp.full((heads_dev, tok_rows), -1e30, jnp.float32),
        jnp.zeros((heads_dev, tok_rows), jnp.float32),
        jnp.zeros((heads_dev, tok_rows, head_size), jnp.float32),
    )
    owned_rows = lax.dynamic_slice_in_dim(jnp.argsort(slots), first_row, tok_rows)
    my_slots = lax.dynamic_slice_in_dim(slots, first_row, tok_rows)
    slot_order = jnp.argsort(my_slots)
    sent_keys, sent_values = (
        lax.all_to_all(
            bucketed(key_rot, slot_order, shards), "tok", split_axis=0, concat_axis=0, tiled=True
        ),
        lax.all_to_all(
            bucketed(value_half, slot_order, shards), "tok", split_axis=0, concat_axis=0, tiled=True
        ),
    )
    arrival = placement_order(owned_rows // tok_rows, tok_rows)
    cache_keys = sent_keys.reshape(tok_rows, width_dev)[arrival]
    cache_values = sent_values.reshape(tok_rows, width_dev)[arrival]
    pieces = (
        lax.all_gather(key_rot, "tok", axis=0, tiled=True),
        lax.all_gather(value_half, "tok", axis=0, tiled=True),
    )
    key_all = pieces[0]
    block_size = math.gcd(key_all.shape[0], tok_rows)
    block_count = key_all.shape[0] // block_size

    def advance(state_in, block_set):
        return (attend(state_in, block_set[0], block_set[1], block_set[2]), None)

    state_out, _ = lax.scan(
        advance,
        start_state,
        (
            key_all.reshape(block_count, block_size, width_dev),
            pieces[1].reshape(block_count, block_size, width_dev),
            deal.reshape(block_count, block_size),
        ),
    )
    row_top, totals, weighted = state_out
    attended = (
        (weighted / totals[:, :, None])
        .transpose(1, 0, 2)
        .reshape(tok_rows, width_dev)
        .astype(jnp.bfloat16)
    )
    mixed_rows = (
        lax.psum_scatter(
            lax.dot_general(
                w_out, attended, (((0,), (1,)), ((), ())), preferred_element_type=jnp.float32
            ).astype(jnp.bfloat16),
            "rep",
            scatter_dimension=0,
            tiled=True,
        )
        .astype(jnp.float32)
        .T
    )
    mixed_sums = lax.psum(jnp.sum(mixed_rows * mixed_rows, axis=1), "rep")
    normed_rows = (
        mixed_rows * lax.rsqrt(mixed_sums / full_width + EPSILON)[:, None] * post_gain[None, :]
    )
    result_rows = (hidden_in.astype(jnp.float32) + normed_rows).astype(jnp.bfloat16)
    packed_order = jnp.argsort(my_packed)
    returned = lax.all_to_all(
        bucketed(result_rows, packed_order, shards), "tok", split_axis=0, concat_axis=0, tiled=True
    )
    my_dealt = lax.dynamic_slice_in_dim(inverse, first_row, tok_rows)
    output = returned.reshape(tok_rows, width_dev)[placement_order(my_dealt // tok_rows, tok_rows)]
    return (output, cache_keys, cache_values)


def select_rows(hits, rows):
    return jnp.dot(
        hits.astype(jnp.bfloat16), rows, preferred_element_type=jnp.float32
    ).astype(jnp.bfloat16)


MESH = pl.DeviceIdType.MESH


def greet(peers):
    barrier = pltpu.get_barrier_semaphore()
    for peer in peers:
        pl.semaphore_signal(barrier, inc=1, device_id=peer, device_id_type=MESH)
    pl.semaphore_wait(barrier, len(peers))


def places():
    corner = lax.axis_index("rep")
    right = corner + 1 - 2 * (corner % 2)
    over = corner + 2 - 4 * (corner // 2)
    return corner, right, over, 3 - corner


def turned_sums(columns):
    rows = columns[0].shape[0]
    lane = lax.broadcasted_iota(jnp.int32, (rows, 128), 1)
    wide = jnp.zeros((rows, 128), jnp.float32)
    for at, column in enumerate(columns):
        wide = jnp.where(lane == at, column, wide)
    return wide.T[0:8, :]


def aim(hits, order):
    row = lax.broadcasted_iota(jnp.int32, hits.shape, 0)
    hits[...] = jnp.where(row == order, 1.0, 0.0).astype(jnp.bfloat16)


def select(hits, src, dst):
    dst[...] = jnp.dot(hits[...], src[...], preferred_element_type=jnp.float32).astype(
        jnp.bfloat16
    )


def project_kernel(
    piece, w_value, w_query, w_key, q_gain, k_gain, where, frequency, meta,
    qk_out, v_out, hid_out, meta_out, k_flat, v_flat,
    held, got, acc, turned, value, cosine, sine, sums, picked, hits,
    w_sem, near_send, near_recv, sum_send, sum_recv, far_send, far_recv, own_sem, flat_sem,
    *, shards, full_width,
):
    rows, width = piece.shape
    half = rows // 2
    quarter = half // 2
    chunk = rows // shards
    head = HEAD_DIM
    me = lax.axis_index("tok")
    corner, right, over, cross = places()
    weights = (w_value, w_query, w_key)
    owners = (corner, right, over, cross)

    def load(which, step):
        return pltpu.make_async_copy(
            weights[which].at[pl.ds(pl.multiple_of(owners[step] * width, width), width), :],
            held.at[which, step],
            w_sem.at[which, step],
        )

    for step in range(4):
        for which in range(3):
            load(which, step).start()

    others = [(me + 1 + d) % shards for d in range(shards - 1)]
    greet([{"rep": peer} for peer in (right, over, cross)] + [{"tok": peer} for peer in others])

    def near(src, slot, at, size, peer, sem):
        return pltpu.make_async_remote_copy(
            src_ref=src.at[pl.ds(at, size), :],
            dst_ref=got.at[slot, pl.ds(at, size), :],
            send_sem=near_send.at[sem],
            recv_sem=near_recv.at[sem],
            device_id={"rep": peer},
            device_id_type=MESH,
        )

    def own_copies(h):
        return (
            near(piece, 0, h * half, half, right, 4 * h),
            near(piece, 1, h * half, half, over, 4 * h + 1),
        )

    def forwards(h):
        return (
            near(got.at[1], 2, h * half, quarter, right, 4 * h + 2),
            near(got.at[0], 2, h * half + quarter, quarter, over, 4 * h + 3),
        )

    def to_far(kind, d, src, dst):
        return pltpu.make_async_remote_copy(
            src_ref=src,
            dst_ref=dst,
            send_sem=far_send.at[kind, d],
            recv_sem=far_recv.at[kind, d],
            device_id={"tok": (me + 1 + d) % shards},
            device_id_type=MESH,
        )

    def head_of(ref, h, owner):
        return ref.at[pl.ds(h * half, half), pl.ds(pl.multiple_of(owner * head, head), head)]

    def source_of(kind, peer):
        if kind < 2:
            return head_of(value, kind, peer)
        if kind < 6:
            return head_of(turned.at[(kind - 2) // 2], kind % 2, peer)
        if kind == 6:
            return piece.at[pl.ds(pl.multiple_of(peer * chunk, chunk), chunk), :]
        return meta

    def landing(kind):
        if kind < 2:
            return v_out.at[me, pl.ds(kind * half, half), :]
        if kind < 6:
            return qk_out.at[
                me, pl.ds((kind % 2) * half, half), pl.ds(((kind - 2) // 2) * head, head)
            ]
        return (hid_out if kind == 6 else meta_out).at[me]

    def own_copy(kind):
        return pltpu.make_async_copy(source_of(kind, me), landing(kind), own_sem.at[kind])

    def far_copy(kind, d):
        return to_far(kind, d, source_of(kind, (me + 1 + d) % shards), landing(kind))

    def send_far(kind):
        def one(d, _):
            far_copy(kind, d).start()
            return _

        lax.fori_loop(0, shards - 1, one, 0)
        own_copy(kind).start()

    def wait_far(kind):
        def one(d, _):
            far_copy(kind, d).wait()
            return _

        lax.fori_loop(0, shards - 1, one, 0)
        own_copy(kind).wait()

    def product(h, step, low, high):
        left = piece if step == 0 else got.at[step - 1]

        def one(which, _):
            part = jnp.dot(
                left[pl.ds(h * half, half), :],
                held[which, step],
                preferred_element_type=jnp.float32,
            )
            if step > 0:
                part = part + acc[h, which]
            acc[h, which] = part
            return _

        lax.fori_loop(low, high, one, 0)

    def squared(h, which):
        total = jnp.zeros((half, head), jnp.float32)
        for at in range(width // head):
            part = acc[h, which, :, at * head : (at + 1) * head]
            total = total + part * part
        return jnp.sum(total, axis=1, keepdims=True)

    def sum_copy(h, at, peer):
        return pltpu.make_async_remote_copy(
            src_ref=sums.at[h, 0],
            dst_ref=sums.at[h, at + 1],
            send_sem=sum_send.at[h, at],
            recv_sem=sum_recv.at[h, at],
            device_id={"rep": peer},
            device_id_type=MESH,
        )

    def sum_copies(h):
        return [sum_copy(h, at, peer) for at, peer in enumerate((right, over, cross))]

    def rotate_half(h):
        total = sums[h, 0] + sums[h, 1] + sums[h, 2] + sums[h, 3]
        scales = lax.rsqrt(total / full_width + EPSILON)
        scales = jnp.concatenate([scales] * (128 // 8), axis=0).T
        mine = pl.ds(h * half, half)
        for which, gain in ((0, q_gain), (1, k_gain)):
            scale = scales[:, which : which + 1]

            def one(at, _):
                column = pl.ds(pl.multiple_of(at * head, head), head)
                normed = acc[h, which + 1, :, column] * scale * gain[:, column]
                other = pltpu.roll(normed, head // 2, 1)
                turned[which, mine, column] = (
                    normed * cosine[mine, :] + other * sine[mine, :]
                ).astype(jnp.bfloat16)
                return _

            lax.fori_loop(0, width // head, one, 0)

    def finish_value(h):
        value[pl.ds(h * half, half), :] = acc[h, 0].astype(jnp.bfloat16)

    for copy in own_copies(0):
        copy.start()
    send_far(7)
    send_far(6)
    angles = where[...] * frequency[...]
    lane = lax.broadcasted_iota(jnp.int32, (rows, head), 1)
    cosine[...] = jnp.cos(angles)
    turn = jnp.sin(angles)
    sine[...] = jnp.where(lane < head // 2, -turn, turn)

    for which in range(3):
        load(which, 0).wait()
    product(0, 0, 0, 3)
    for h in range(2):
        if h == 1:
            product(1, 0, 0, 3)
            for copy in sum_copies(0):
                copy.wait()
            rotate_half(0)
            send_far(4)
            send_far(2)
        else:
            for copy in own_copies(0):
                copy.wait_recv()
            for copy in forwards(0):
                copy.start()
            for copy in own_copies(1):
                copy.start()
        for step in (1, 2):
            if h == 0:
                for which in range(3):
                    load(which, step).wait()
            product(h, step, 0, 3)
        for copy in forwards(h):
            copy.wait_recv()
        if h == 0:
            for which in range(3):
                load(which, 3).wait()
        product(h, 3, 0, 1)
        finish_value(h)
        send_far(h)
        product(h, 3, 1, 3)
        sums[h, 0] = turned_sums([squared(h, 1), squared(h, 2)])
        for copy in sum_copies(h):
            copy.start()
        if h == 0:
            for copy in own_copies(1):
                copy.wait_recv()
            for copy in forwards(1):
                copy.start()
    for copy in sum_copies(1):
        copy.wait()
    rotate_half(1)
    send_far(5)
    send_far(3)
    aim(hits, meta[2:3, :])
    select(hits, turned.at[1], picked.at[0])
    select(hits, value, picked.at[1])
    flat = (
        pltpu.make_async_copy(picked.at[0], k_flat, flat_sem.at[0]),
        pltpu.make_async_copy(picked.at[1], v_flat, flat_sem.at[1]),
    )
    for copy in flat:
        copy.start()
    for h in range(2):
        for copy in own_copies(h) + forwards(h):
            copy.wait_send()
    for kind in range(8):
        wait_far(kind)
    for copy in flat:
        copy.wait()


def project_heads(piece, w_value, w_query, w_key, q_gain, k_gain, where, frequency, meta, shards):
    rows, width = piece.shape
    full_width = w_query.shape[0]
    half = rows // 2
    head = HEAD_DIM
    inside = pl.BlockSpec(memory_space=pltpu.VMEM)
    outside = pl.BlockSpec(memory_space=pl.ANY)
    dma = pltpu.SemaphoreType.DMA
    return pl.pallas_call(
        functools.partial(project_kernel, shards=shards, full_width=full_width),
        out_shape=(
            jax.ShapeDtypeStruct((shards, rows, 2 * head), jnp.bfloat16),
            jax.ShapeDtypeStruct((shards, rows, head), jnp.bfloat16),
            jax.ShapeDtypeStruct((shards, rows // shards, width), jnp.bfloat16),
            jax.ShapeDtypeStruct((shards,) + meta.shape, jnp.int32),
            jax.ShapeDtypeStruct((rows, width), jnp.bfloat16),
            jax.ShapeDtypeStruct((rows, width), jnp.bfloat16),
        ),
        in_specs=[inside, outside, outside, outside] + [inside] * 5,
        out_specs=(outside,) * 6,
        scratch_shapes=[
            pltpu.VMEM((3, 4, width, width), jnp.bfloat16),
            pltpu.VMEM((3, rows, width), jnp.bfloat16),
            pltpu.VMEM((2, 3, half, width), jnp.float32),
            pltpu.VMEM((2, rows, width), jnp.bfloat16),
            pltpu.VMEM((rows, width), jnp.bfloat16),
            pltpu.VMEM((rows, head), jnp.float32),
            pltpu.VMEM((rows, head), jnp.float32),
            pltpu.VMEM((2, 4, 8, half), jnp.float32),
            pltpu.VMEM((2, rows, width), jnp.bfloat16),
            pltpu.VMEM((rows, rows), jnp.bfloat16),
            dma((3, 4)),
            dma((8,)),
            dma((8,)),
            dma((2, 3)),
            dma((2, 3)),
            dma((8, shards - 1)),
            dma((8, shards - 1)),
            dma((8,)),
            dma((2,)),
        ],
        compiler_params=pltpu.CompilerParams(
            collective_id=1, has_side_effects=True, vmem_limit_bytes=50 << 20
        ),
        cost_estimate=pl.CostEstimate(
            flops=6 * rows * full_width * width,
            bytes_accessed=6 * full_width * width + 16 * rows * width,
            transcendentals=0,
        ),
    )(piece, w_value, w_query, w_key, q_gain, k_gain, where, frequency, meta)


def finish_kernel(
    qk_in, v_in, hid_in, keys_in, values_in, w_out, post_gain, orders, begins,
    out, keys_out, values_out,
    qk_rows, v_rows, arrived, hidden, hits,
    queries, keys, values, scores, heads, attended, held,
    mine, sent, first_got, second_got, sums, result,
    in_sem, w_sem, far_send, far_recv, own_sem, near_send, near_recv, sum_send, sum_recv, out_sem,
    *, shards, full_width,
):
    rows, width = attended.shape
    half = rows // 2
    side = width // 2
    chunk = rows // shards
    head = HEAD_DIM
    reach = shards // 2
    me = lax.axis_index("tok")
    corner, right, over, cross = places()
    owners = (cross, right, over, corner)

    loads = [
        pltpu.make_async_copy(src, dst, in_sem.at[at])
        for at, (src, dst) in enumerate(
            (
                (qk_in, qk_rows),
                (v_in, v_rows),
                (hid_in, arrived),
            )
        )
    ]
    for copy in loads:
        copy.start()

    def load(step):
        return pltpu.make_async_copy(
            w_out.at[:, pl.ds(pl.multiple_of(owners[step] * width, width), width)],
            held.at[step],
            w_sem.at[step],
        )

    for step in range(4):
        load(step).start()
    others = [(me + 1 + d) % shards for d in range(shards - 1)]
    greet([{"rep": peer} for peer in (right, over, cross)] + [{"tok": peer} for peer in others])

    def source_of(kind, peer):
        if kind < 2:
            picked = (keys_in, values_in)[kind]
            return picked.at[pl.ds(pl.multiple_of(peer * chunk, chunk), chunk), :]
        return heads.at[kind - 2, peer]

    def landing(kind):
        if kind < 2:
            landed = (keys_out, values_out)[kind]
            return landed.at[pl.ds(pl.multiple_of(me * chunk, chunk), chunk), :]
        return attended.at[
            pl.ds((kind - 2) * half, half), pl.ds(pl.multiple_of(me * head, head), head)
        ]

    def own_copy(kind):
        return pltpu.make_async_copy(source_of(kind, me), landing(kind), own_sem.at[kind])

    def far_copy(kind, d):
        peer = (me + 1 + d) % shards
        return pltpu.make_async_remote_copy(
            src_ref=source_of(kind, peer),
            dst_ref=landing(kind),
            send_sem=far_send.at[kind, d],
            recv_sem=far_recv.at[kind, d],
            device_id={"tok": peer},
            device_id_type=MESH,
        )

    def send_far(kind):
        def one(d, _):
            far_copy(kind, d).start()
            return _

        lax.fori_loop(0, shards - 1, one, 0)
        own_copy(kind).start()

    def wait_far(kind):
        def one(d, _):
            far_copy(kind, d).wait()
            return _

        lax.fori_loop(0, shards - 1, one, 0)
        own_copy(kind).wait()

    send_far(1)
    loads[0].wait()
    loads[1].wait()

    def pack(block, _):
        aim(hits, orders[pl.ds(block, 1), :])
        at = pl.ds(pl.multiple_of(block * chunk, chunk), chunk)
        into = pl.ds(pl.multiple_of(block * rows, rows), rows)
        both = jnp.dot(
            hits[...],
            qk_rows[:, at, :].reshape(rows, 2 * head),
            preferred_element_type=jnp.float32,
        ).astype(jnp.bfloat16)
        queries[into, :] = both[:, :head]
        keys[into, :] = both[:, head:]
        values[:, into] = (
            jnp.dot(
                hits[...],
                v_rows[:, at, :].reshape(rows, head),
                preferred_element_type=jnp.float32,
            )
            .T.astype(jnp.bfloat16)
        )
        return _

    lax.fori_loop(0, shards, pack, 0)
    scale = head ** (-0.5) * math.log2(math.e)

    def attend(part, block, steps):
        depth = half * (part + 1)
        unrolled = isinstance(steps, int)

        def repeat(step, state):
            if not unrolled:
                return lax.fori_loop(0, steps, step, state)
            for at in range(steps):
                state = step(at, state)
            return state

        def folded(tile, fold):
            return fold(tile.reshape(tile.shape[0] // 8, 8, half), axis=0)

        query = queries[pl.ds(pl.multiple_of(block * rows + part * half, half), half), :]
        begin = begins[pl.ds(2 * block + part, 1), :]

        def score(base, count):
            return lax.dot_general(
                keys[pl.ds(base, count), :],
                query,
                (((1,), (1,)), ((), ())),
                preferred_element_type=jnp.float32,
            )

        def earlier(step):
            return pl.multiple_of((block - 1 - step) * rows, rows)

        def stored(step):
            at = step * rows
            return pl.ds(at if unrolled else pl.multiple_of(at, rows), rows)

        base = pl.multiple_of(block * rows, rows)
        key_row = lax.broadcasted_iota(jnp.int32, (depth, half), 0)
        query_row = lax.broadcasted_iota(jnp.int32, (depth, half), 1) + part * half
        seen = (key_row >= begin - base) & (key_row <= query_row)
        last = jnp.where(seen, score(base, depth), -1e30)
        scores[reach * rows : reach * rows + depth, :] = last

        def first_pass(step, top):
            key_row = lax.broadcasted_iota(jnp.int32, (rows, half), 0)
            tile = jnp.where(
                key_row >= begin - earlier(step), score(earlier(step), rows), -1e30
            )
            scores[stored(step), :] = tile
            return jnp.maximum(top, folded(tile, jnp.max))

        top = repeat(first_pass, folded(last, jnp.max))
        top = jnp.max(top, axis=0, keepdims=True)

        def weigh(tile, base, count):
            weights = jnp.exp2((tile - top) * scale)
            return folded(weights, jnp.sum), jnp.dot(
                values[:, pl.ds(base, count)],
                weights.astype(jnp.bfloat16),
                preferred_element_type=jnp.float32,
            )

        def second_pass(step, state):
            total, weighted = weigh(scores[stored(step), :], earlier(step), rows)
            return state[0] + total, state[1] + weighted

        state = weigh(scores[reach * rows : reach * rows + depth, :], base, depth)
        total, weighted = repeat(second_pass, state)
        total = jnp.sum(total, axis=0, keepdims=True)
        heads[part, block] = (weighted / total).T.astype(jnp.bfloat16)

    def attend_first(part):
        def one(block, _):
            attend(part, block, block)
            return _

        lax.fori_loop(0, reach, one, 0)

    def attend_last(part):
        def one(block, _):
            attend(part, block, reach)
            return _

        lax.fori_loop(reach, shards, one, 0)

    def project(part):
        def one(step, _):
            done = jnp.dot(
                attended[pl.ds(part * half, half), :],
                held[step],
                preferred_element_type=jnp.float32,
            )
            mine[part] = done
            sent[part, step] = done.astype(jnp.bfloat16)
            return _

        lax.fori_loop(0, 4, one, 0)

    def near(src, dst, peer, sem):
        return pltpu.make_async_remote_copy(
            src_ref=src,
            dst_ref=dst,
            send_sem=near_send.at[sem],
            recv_sem=near_recv.at[sem],
            device_id={"rep": peer},
            device_id_type=MESH,
        )

    left, rest = pl.ds(0, side), pl.ds(side, side)

    def first_copies(part):
        return (
            near(sent.at[part, 0, :, left], first_got.at[part, 0], right, 6 * part),
            near(sent.at[part, 1, :, left], first_got.at[part, 1], right, 6 * part + 1),
            near(sent.at[part, 0, :, rest], first_got.at[part, 2], over, 6 * part + 2),
            near(sent.at[part, 2, :, rest], first_got.at[part, 3], over, 6 * part + 3),
        )

    def second_copies(part):
        return (
            near(sent.at[part, 2, :, left], second_got.at[part, 0], over, 6 * part + 4),
            near(sent.at[part, 1, :, rest], second_got.at[part, 1], right, 6 * part + 5),
        )

    def start(copies):
        for copy in copies:
            copy.start()

    def middle(part):
        for copy in first_copies(part):
            copy.wait_recv()
        for step, column, at in ((2, left, 0), (1, rest, 2)):
            sent[part, step, :, column] = (
                sent[part, step, :, column].astype(jnp.float32)
                + first_got[part, at].astype(jnp.float32)
            ).astype(jnp.bfloat16)
        start(second_copies(part))
        for column, at in ((left, 1), (rest, 3)):
            mine[part, :, column] = mine[part, :, column] + first_got[part, at].astype(jnp.float32)

    def sum_copies(part):
        return [
            pltpu.make_async_remote_copy(
                src_ref=sums.at[part, 0],
                dst_ref=sums.at[part, at + 1],
                send_sem=sum_send.at[part, at],
                recv_sem=sum_recv.at[part, at],
                device_id={"rep": peer},
                device_id_type=MESH,
            )
            for at, peer in enumerate((right, over, cross))
        ]

    def total(part):
        for copy in second_copies(part):
            copy.wait_recv()
        squares = jnp.zeros((half, head), jnp.float32)
        for at in range(width // head):
            column = pl.ds(at * head, head)
            got = second_got[part, at * head // side, :, pl.ds(at * head % side, head)]
            rows_now = mine[part, :, column] + got.astype(jnp.float32)
            mine[part, :, column] = rows_now
            squares = squares + rows_now * rows_now
        sums[part, 0] = turned_sums([jnp.sum(squares, axis=1, keepdims=True)])
        start(sum_copies(part))

    def settle(part):
        for copy in sum_copies(part):
            copy.wait()
        whole = sums[part, 0] + sums[part, 1] + sums[part, 2] + sums[part, 3]
        scales = lax.rsqrt(whole / full_width + EPSILON)
        scales = jnp.concatenate([scales] * (128 // 8), axis=0).T[:, 0:1]
        at = pl.ds(part * half, half)
        result[at, :] = (
            hidden[at, :].astype(jnp.float32) + mine[part] * scales * post_gain[...]
        ).astype(jnp.bfloat16)

    def written(part):
        at = pl.ds(part * half, half)
        return pltpu.make_async_copy(result.at[at, :], out.at[at, :], out_sem.at[part])

    attend_first(0)
    attend_last(0)
    send_far(2)
    attend_last(1)
    for step in range(4):
        load(step).wait()
    wait_far(2)
    project(0)
    start(first_copies(0))
    attend_first(1)
    send_far(3)
    loads[2].wait()
    aim(hits, orders[pl.ds(me, 1), :])
    select(hits, arrived, hidden)
    middle(0)
    wait_far(3)
    send_far(0)
    project(1)
    start(first_copies(1))
    total(0)
    middle(1)
    settle(0)
    written(0).start()
    total(1)
    settle(1)
    written(1).start()
    wait_far(1)
    wait_far(0)
    for part in range(2):
        for copy in first_copies(part) + second_copies(part):
            copy.wait_send()
        written(part).wait()


def finish_heads(
    qk_rows, v_rows, hid_rows, key_flat, value_flat, w_out, post_gain, orders, begins
):
    shards, rows, head = v_rows.shape
    width, full_width = w_out.shape
    half = rows // 2
    reach = shards // 2
    inside = pl.BlockSpec(memory_space=pltpu.VMEM)
    outside = pl.BlockSpec(memory_space=pl.ANY)
    dma = pltpu.SemaphoreType.DMA
    return pl.pallas_call(
        functools.partial(finish_kernel, shards=shards, full_width=full_width),
        out_shape=(jax.ShapeDtypeStruct((rows, width), jnp.bfloat16),) * 3,
        in_specs=[outside] * 6 + [inside] * 3,
        out_specs=(outside,) * 3,
        scratch_shapes=[
            pltpu.VMEM((shards, rows, 2 * head), jnp.bfloat16),
            pltpu.VMEM((shards, rows, head), jnp.bfloat16),
            pltpu.VMEM((rows, width), jnp.bfloat16),
            pltpu.VMEM((rows, width), jnp.bfloat16),
            pltpu.VMEM((rows, rows), jnp.bfloat16),
            pltpu.VMEM((shards * rows, head), jnp.bfloat16),
            pltpu.VMEM((shards * rows, head), jnp.bfloat16),
            pltpu.VMEM((head, shards * rows), jnp.bfloat16),
            pltpu.VMEM(((reach + 1) * rows, half), jnp.float32),
            pltpu.VMEM((2, shards, half, head), jnp.bfloat16),
            pltpu.VMEM((rows, width), jnp.bfloat16),
            pltpu.VMEM((4, width, width), jnp.bfloat16),
            pltpu.VMEM((2, half, width), jnp.float32),
            pltpu.VMEM((2, 4, half, width), jnp.bfloat16),
            pltpu.VMEM((2, 4, half, width // 2), jnp.bfloat16),
            pltpu.VMEM((2, 2, half, width // 2), jnp.bfloat16),
            pltpu.VMEM((2, 4, 8, half), jnp.float32),
            pltpu.VMEM((rows, width), jnp.bfloat16),
            dma((3,)),
            dma((4,)),
            dma((4, shards - 1)),
            dma((4, shards - 1)),
            dma((4,)),
            dma((12,)),
            dma((12,)),
            dma((2, 3)),
            dma((2, 3)),
            dma((2,)),
        ],
        compiler_params=pltpu.CompilerParams(
            collective_id=2, has_side_effects=True, vmem_limit_bytes=52 << 20
        ),
        cost_estimate=pl.CostEstimate(
            flops=2 * rows * full_width * width + 20 * rows * rows * shards * head,
            bytes_accessed=2 * full_width * width + 20 * rows * width,
            transcendentals=5 * rows * rows * shards,
        ),
    )(qk_rows, v_rows, hid_rows, key_flat, value_flat, w_out, post_gain, orders, begins)


def place_kernel(order, rows_in, keys_in, values_in, rows_out, keys_out, values_out, hits):
    aim(hits, order[...])
    rows_out[...] = rows_in[...]
    select(hits, keys_in, keys_out)
    select(hits, values_in, values_out)


def place_rows(order, result, keys_landed, values_landed):
    rows, width = result.shape
    block = pl.BlockSpec((rows, width // 4), lambda i: (0, i))
    return pl.pallas_call(
        place_kernel,
        out_shape=(jax.ShapeDtypeStruct((rows, width), jnp.bfloat16),) * 3,
        grid=(4,),
        in_specs=[pl.BlockSpec((1, rows), lambda i: (0, 0))] + [block] * 3,
        out_specs=(block,) * 3,
        scratch_shapes=[pltpu.VMEM((rows, rows), jnp.bfloat16)],
        compiler_params=pltpu.CompilerParams(vmem_limit_bytes=16 << 20),
    )(order, result, keys_landed, values_landed)


def body_heads(
    hidden_in,
    w_query,
    w_key,
    w_value,
    w_out,
    q_gain,
    k_gain,
    post_gain,
    prompt_lengths,
    segment_ids,
    deal,
    inverse,
    slots,
):
    tok_rows, width_dev = hidden_in.shape
    full_width = w_query.shape[0]
    head_size = HEAD_DIM
    shards = lax.axis_size("tok")
    chunk = tok_rows // shards
    me = lax.axis_index("tok")
    first_row = me * tok_rows

    local = jnp.arange(tok_rows, dtype=jnp.int32)
    starts = starts_of(prompt_lengths)
    my_packed = lax.dynamic_slice_in_dim(deal, first_row, tok_rows)
    my_slots = lax.dynamic_slice_in_dim(slots, first_row, tok_rows)

    def ranking(keys):
        return jnp.sum((keys[None, :] < keys[:, None]).astype(jnp.int32), axis=1)

    sort_hits = ranking(my_packed)[None, :] == local[:, None]
    sorted_packed = jnp.sum(jnp.where(sort_hits, my_packed[None, :], 0), axis=1)
    sorted_slots = jnp.sum(jnp.where(sort_hits, my_slots[None, :], 0), axis=1)
    slot_rank = ranking(sorted_slots)
    slot_hits = slot_rank[None, :] == local[:, None]
    slots_rising = jnp.sum(jnp.where(slot_hits, sorted_slots[None, :], 0), axis=1)
    my_start = jnp.max(
        jnp.where(starts[None, :] <= sorted_packed[:, None], starts[None, :], 0), axis=1
    )
    positions = (sorted_packed - my_start).astype(jnp.float32)
    meta = jnp.concatenate(
        [
            sorted_packed[None],
            slots_rising[None],
            slot_rank[None],
            jnp.zeros((5, tok_rows), jnp.int32),
        ],
        axis=0,
    )
    half_size = head_size // 2
    frequency = ROPE_BASE ** (-jnp.arange(half_size, dtype=jnp.float32) * 2.0 / head_size)
    frequency = jnp.concatenate([frequency, frequency])[None, :]

    piece = select_rows(sort_hits, hidden_in)
    qk_rows, v_rows, sent_hidden, meta_all, key_flat, value_half = project_heads(
        piece,
        w_value,
        w_query,
        w_key,
        q_gain[None, :],
        k_gain[None, :],
        positions[:, None],
        frequency,
        meta,
        shards,
    )

    target = meta_all[:, 0, :].reshape(shards, shards, chunk).transpose(1, 0, 2)
    target = target.reshape(shards, tok_rows) - (
        jnp.arange(shards, dtype=jnp.int32)[:, None] * tok_rows
    )
    slot_target = lax.dynamic_slice_in_dim(meta_all[:, 1, :], me * chunk, chunk, axis=1)
    slot_target = slot_target.reshape(1, tok_rows) - first_row
    every = jnp.arange(shards * tok_rows, dtype=jnp.int32)
    begins = jnp.max(jnp.where(starts[:, None] <= every[None, :], starts[:, None], 0), axis=0)
    result, keys_landed, values_landed = finish_heads(
        qk_rows,
        v_rows,
        sent_hidden.reshape(tok_rows, width_dev),
        key_flat,
        value_half,
        w_out,
        post_gain[None, :],
        target,
        begins.reshape(2 * shards, tok_rows // 2),
    )
    return place_rows(slot_target, result, keys_landed, values_landed)


def solution(mesh):
    def pick(*operands):
        heads_dev = operands[0].shape[1] // HEAD_DIM
        fits = heads_dev == mesh.shape["tok"] and mesh.shape["rep"] == 4
        chosen = body_heads if fits else body
        return chosen(*operands)

    return jax.shard_map(
        pick,
        mesh=mesh,
        in_specs=(
            P("tok", "rep"),
            P(None, "rep"),
            P(None, "rep"),
            P(None, "rep"),
            P("rep", None),
            P("rep"),
            P("rep"),
            P("rep"),
            P(),
            P(),
            P(),
            P(),
            P(),
        ),
        out_specs=(P("tok", "rep"), P("tok", "rep"), P("tok", "rep")),
        check_vma=False,
    )
```

```python
import functools
import math

import jax
import jax.numpy as jnp
from jax import lax
from jax.experimental import pallas as pl
from jax.experimental.pallas import tpu as pltpu
from jax.sharding import PartitionSpec as P

HEAD_DIM = 128


EPSILON = 1e-06
ROPE_BASE = 500000.0


def rotate(values, positions):
    half_size = values.shape[-1] // 2
    frequency = ROPE_BASE ** (-jnp.arange(half_size, dtype=jnp.float32) * 2.0 / values.shape[-1])
    angles = positions.astype(jnp.float32)[:, None] * frequency[None, :]
    cosine = jnp.cos(angles)[:, None, :]
    sine_part = jnp.sin(angles)[:, None, :]
    lower_half = values[..., :half_size]
    upper_half = values[..., half_size:]
    return jnp.concatenate(
        [
            lower_half * cosine - upper_half * sine_part,
            upper_half * cosine + lower_half * sine_part,
        ],
        axis=-1,
    )


def starts_of(lengths):
    index = jnp.arange(lengths.shape[0], dtype=jnp.int32)
    return jnp.sum(jnp.where(index[None, :] < index[:, None], lengths[None, :], 0), axis=1)


def bucketed(table_rows, row_order, shards):
    picked = table_rows[row_order]
    return picked.reshape(shards, picked.shape[0] // shards, picked.shape[1])


def placement_order(sources, shard_rows):
    local_ids = jnp.arange(sources.shape[0], dtype=jnp.int32)
    arrival = jnp.argsort(sources * shard_rows + local_ids)
    return jnp.argsort(arrival)


def body(
    hidden_in,
    w_query,
    w_key,
    w_value,
    w_out,
    q_gain,
    k_gain,
    post_gain,
    prompt_lengths,
    segment_ids,
    deal,
    inverse,
    slots,
):
    tok_rows, width_dev = hidden_in.shape
    full_width = w_query.shape[0]
    head_size = HEAD_DIM
    heads_dev = width_dev // head_size
    shards = lax.axis_size("tok")
    first_row = lax.axis_index("tok") * tok_rows
    my_packed = lax.dynamic_slice_in_dim(deal, first_row, tok_rows)
    my_segment = segment_ids[my_packed]
    prompt_ids = jnp.arange(prompt_lengths.shape[0], dtype=jnp.int32)
    prompt_starts = starts_of(prompt_lengths)
    my_start = jnp.sum(
        jnp.where(my_segment[:, None] == prompt_ids[None, :], prompt_starts[None, :], 0), axis=1
    )
    positions = my_packed - my_start
    pieces = lax.all_gather(hidden_in, "rep", axis=1, tiled=True)
    query_rows = jnp.dot(pieces, w_query, preferred_element_type=jnp.float32)
    key_rows = jnp.dot(pieces, w_key, preferred_element_type=jnp.float32)
    value_rows = jnp.dot(pieces, w_value, preferred_element_type=jnp.float32)
    query_sums, key_sums = lax.psum(
        (jnp.sum(query_rows * query_rows, axis=1), jnp.sum(key_rows * key_rows, axis=1)), "rep"
    )
    query_rows = (
        query_rows * lax.rsqrt(query_sums / full_width + EPSILON)[:, None] * q_gain[None, :]
    )
    key_rows = key_rows * lax.rsqrt(key_sums / full_width + EPSILON)[:, None] * k_gain[None, :]
    query_rot = rotate(query_rows.reshape(tok_rows, heads_dev, head_size), positions).astype(
        jnp.bfloat16
    )
    key_rot = (
        rotate(key_rows.reshape(tok_rows, heads_dev, head_size), positions)
        .astype(jnp.bfloat16)
        .reshape(tok_rows, width_dev)
    )
    value_half = value_rows.astype(jnp.bfloat16)
    scale = head_size ** (-0.5)

    def attend(state_now, key_block, value_block, key_packed):
        row_top, totals, weighted = state_now
        block_keys = key_block.reshape(key_block.shape[0], heads_dev, head_size)
        block_values = value_block.reshape(value_block.shape[0], heads_dev, head_size)
        key_segment = segment_ids[key_packed]
        allowed = (key_segment[None, :] == my_segment[:, None]) & (
            key_packed[None, :] <= my_packed[:, None]
        )
        scores = (
            jnp.einsum("qhd,khd->hqk", query_rot, block_keys, preferred_element_type=jnp.float32)
            * scale
        )
        masked = jnp.where(allowed[None], scores, -1e30)
        new_top = jnp.maximum(row_top, jnp.max(masked, axis=2))
        weights = jnp.where(allowed[None], jnp.exp(masked - new_top[:, :, None]), 0.0)
        factor = jnp.exp(row_top - new_top)
        totals = totals * factor + jnp.sum(weights, axis=2)
        weighted = weighted * factor[:, :, None] + jnp.einsum(
            "hqk,khd->hqd",
            weights.astype(jnp.bfloat16),
            block_values,
            preferred_element_type=jnp.float32,
        )
        return (new_top, totals, weighted)

    start_state = (
        jnp.full((heads_dev, tok_rows), -1e30, jnp.float32),
        jnp.zeros((heads_dev, tok_rows), jnp.float32),
        jnp.zeros((heads_dev, tok_rows, head_size), jnp.float32),
    )
    owned_rows = lax.dynamic_slice_in_dim(jnp.argsort(slots), first_row, tok_rows)
    my_slots = lax.dynamic_slice_in_dim(slots, first_row, tok_rows)
    slot_order = jnp.argsort(my_slots)
    sent_keys, sent_values = (
        lax.all_to_all(
            bucketed(key_rot, slot_order, shards), "tok", split_axis=0, concat_axis=0, tiled=True
        ),
        lax.all_to_all(
            bucketed(value_half, slot_order, shards), "tok", split_axis=0, concat_axis=0, tiled=True
        ),
    )
    arrival = placement_order(owned_rows // tok_rows, tok_rows)
    cache_keys = sent_keys.reshape(tok_rows, width_dev)[arrival]
    cache_values = sent_values.reshape(tok_rows, width_dev)[arrival]
    pieces = (
        lax.all_gather(key_rot, "tok", axis=0, tiled=True),
        lax.all_gather(value_half, "tok", axis=0, tiled=True),
    )
    key_all = pieces[0]
    block_size = math.gcd(key_all.shape[0], tok_rows)
    block_count = key_all.shape[0] // block_size

    def advance(state_in, block_set):
        return (attend(state_in, block_set[0], block_set[1], block_set[2]), None)

    state_out, _ = lax.scan(
        advance,
        start_state,
        (
            key_all.reshape(block_count, block_size, width_dev),
            pieces[1].reshape(block_count, block_size, width_dev),
            deal.reshape(block_count, block_size),
        ),
    )
    row_top, totals, weighted = state_out
    attended = (
        (weighted / totals[:, :, None])
        .transpose(1, 0, 2)
        .reshape(tok_rows, width_dev)
        .astype(jnp.bfloat16)
    )
    mixed_rows = (
        lax.psum_scatter(
            lax.dot_general(
                w_out, attended, (((0,), (1,)), ((), ())), preferred_element_type=jnp.float32
            ).astype(jnp.bfloat16),
            "rep",
            scatter_dimension=0,
            tiled=True,
        )
        .astype(jnp.float32)
        .T
    )
    mixed_sums = lax.psum(jnp.sum(mixed_rows * mixed_rows, axis=1), "rep")
    normed_rows = (
        mixed_rows * lax.rsqrt(mixed_sums / full_width + EPSILON)[:, None] * post_gain[None, :]
    )
    result_rows = (hidden_in.astype(jnp.float32) + normed_rows).astype(jnp.bfloat16)
    packed_order = jnp.argsort(my_packed)
    returned = lax.all_to_all(
        bucketed(result_rows, packed_order, shards), "tok", split_axis=0, concat_axis=0, tiled=True
    )
    my_dealt = lax.dynamic_slice_in_dim(inverse, first_row, tok_rows)
    output = returned.reshape(tok_rows, width_dev)[placement_order(my_dealt // tok_rows, tok_rows)]
    return (output, cache_keys, cache_values)


def select_rows(hits, rows):
    return jnp.dot(
        hits.astype(jnp.bfloat16), rows, preferred_element_type=jnp.float32
    ).astype(jnp.bfloat16)


MESH = pl.DeviceIdType.MESH


def greet(peers):
    barrier = pltpu.get_barrier_semaphore()
    for peer in peers:
        pl.semaphore_signal(barrier, inc=1, device_id=peer, device_id_type=MESH)
    pl.semaphore_wait(barrier, len(peers))


def places():
    corner = lax.axis_index("rep")
    right = corner + 1 - 2 * (corner % 2)
    over = corner + 2 - 4 * (corner // 2)
    return corner, right, over, 3 - corner


def turned_sums(columns):
    rows = columns[0].shape[0]
    lane = lax.broadcasted_iota(jnp.int32, (rows, 128), 1)
    wide = jnp.zeros((rows, 128), jnp.float32)
    for at, column in enumerate(columns):
        wide = jnp.where(lane == at, column, wide)
    return wide.T[0:8, :]


def aim(hits, order):
    row = lax.broadcasted_iota(jnp.int32, hits.shape, 0)
    hits[...] = jnp.where(row == order, 1.0, 0.0).astype(jnp.bfloat16)


def select(hits, src, dst):
    dst[...] = jnp.dot(hits[...], src[...], preferred_element_type=jnp.float32).astype(
        jnp.bfloat16
    )


def whole_kernel(
    piece, w_value, w_query, w_key, w_out, q_gain, k_gain, post_gain,
    where, frequency, meta, slot_rank, begins,
    out, keys_out, values_out, slot_order,
    held, got, acc, turned, value, cosine, sine, sums, picked, hits,
    qk_rows, v_rows, arrived, meta_got, queries, keys, values, scores, heads, attended,
    first_got, second_got,
    w_sem, near_send, near_recv, sum_send, sum_recv, far_send, far_recv, own_sem, out_sem,
    *, shards, full_width,
):
    rows, width = piece.shape
    half = rows // 2
    quarter = half // 2
    chunk = rows // shards
    head = HEAD_DIM
    me = lax.axis_index("tok")
    corner, right, over, cross = places()
    reach = shards // 2
    weights = (w_value, w_query, w_key)
    owners = (corner, right, over, cross)

    def load(which, step):
        return pltpu.make_async_copy(
            weights[which].at[pl.ds(pl.multiple_of(owners[step] * width, width), width), :],
            held.at[which, step],
            w_sem.at[which, step],
        )

    for step in range(4):
        for which in range(3):
            load(which, step).start()

    others = [(me + 1 + d) % shards for d in range(shards - 1)]
    greet([{"rep": peer} for peer in (right, over, cross)] + [{"tok": peer} for peer in others])

    def near(src, slot, at, size, peer, sem):
        return pltpu.make_async_remote_copy(
            src_ref=src.at[pl.ds(at, size), :],
            dst_ref=got.at[slot, pl.ds(at, size), :],
            send_sem=near_send.at[sem],
            recv_sem=near_recv.at[sem],
            device_id={"rep": peer},
            device_id_type=MESH,
        )

    def own_copies(h):
        return (
            near(piece, 0, h * half, half, right, 4 * h),
            near(piece, 1, h * half, half, over, 4 * h + 1),
        )

    def forwards(h):
        return (
            near(got.at[1], 2, h * half, quarter, right, 4 * h + 2),
            near(got.at[0], 2, h * half + quarter, quarter, over, 4 * h + 3),
        )

    def to_far(kind, d, src, dst):
        return pltpu.make_async_remote_copy(
            src_ref=src,
            dst_ref=dst,
            send_sem=far_send.at[kind, d],
            recv_sem=far_recv.at[kind, d],
            device_id={"tok": (me + 1 + d) % shards},
            device_id_type=MESH,
        )

    def head_of(ref, h, owner):
        return ref.at[pl.ds(h * half, half), pl.ds(pl.multiple_of(owner * head, head), head)]

    def source_of(kind, peer):
        if kind < 2:
            return head_of(value, kind, peer)
        if kind < 6:
            return head_of(turned.at[(kind - 2) // 2], kind % 2, peer)
        if kind == 7:
            return meta
        if kind < 10 and kind > 7:
            return heads.at[kind - 8, peer]
        source = piece if kind == 6 else picked.at[kind - 10]
        return source.at[pl.ds(pl.multiple_of(peer * chunk, chunk), chunk), :]

    def landing(kind):
        if kind < 2:
            return v_rows.at[me, pl.ds(kind * half, half), :]
        if kind < 6:
            return qk_rows.at[
                me, pl.ds((kind % 2) * half, half), pl.ds(((kind - 2) // 2) * head, head)
            ]
        if kind == 7:
            return meta_got.at[me]
        if kind < 10 and kind > 7:
            return attended.at[
                pl.ds((kind - 8) * half, half), pl.ds(pl.multiple_of(me * head, head), head)
            ]
        target = arrived if kind == 6 else (keys_out, values_out)[kind - 10]
        return target.at[pl.ds(pl.multiple_of(me * chunk, chunk), chunk), :]

    def own_copy(kind):
        return pltpu.make_async_copy(source_of(kind, me), landing(kind), own_sem.at[kind])

    def far_copy(kind, d):
        return to_far(kind, d, source_of(kind, (me + 1 + d) % shards), landing(kind))

    def send_far(kind):
        def one(d, _):
            far_copy(kind, d).start()
            return _

        lax.fori_loop(0, shards - 1, one, 0)
        own_copy(kind).start()

    def send_heads(part, low, high):
        def one(peer, _):
            @pl.when(peer != me)
            def _():
                far_copy(8 + part, (peer + shards - me - 1) % shards).start()

            @pl.when(peer == me)
            def _():
                own_copy(8 + part).start()

            return _

        def each(peer, _):
            one(peer, None)
            return _

        lax.fori_loop(low, high, each, 0)

    def wait_far(kind):
        def one(d, _):
            far_copy(kind, d).wait()
            return _

        lax.fori_loop(0, shards - 1, one, 0)
        own_copy(kind).wait()

    def product(h, step, low, high):
        left = piece if step == 0 else got.at[step - 1]

        def one(which, _):
            part = jnp.dot(
                left[pl.ds(h * half, half), :],
                held[which, step],
                preferred_element_type=jnp.float32,
            )
            if step > 0:
                part = part + acc[h, which]
            acc[h, which] = part
            return _

        lax.fori_loop(low, high, one, 0)

    def squared(h, which):
        total = jnp.zeros((half, head), jnp.float32)
        for at in range(width // head):
            part = acc[h, which, :, at * head : (at + 1) * head]
            total = total + part * part
        return jnp.sum(total, axis=1, keepdims=True)

    def sum_copy(h, at, peer):
        return pltpu.make_async_remote_copy(
            src_ref=sums.at[h, 0],
            dst_ref=sums.at[h, at + 1],
            send_sem=sum_send.at[h, at],
            recv_sem=sum_recv.at[h, at],
            device_id={"rep": peer},
            device_id_type=MESH,
        )

    def sum_copies(h):
        return [sum_copy(h, at, peer) for at, peer in enumerate((right, over, cross))]

    def rotate_half(h):
        total = sums[h, 0] + sums[h, 1] + sums[h, 2] + sums[h, 3]
        scales = lax.rsqrt(total / full_width + EPSILON)
        scales = jnp.concatenate([scales] * (128 // 8), axis=0).T
        mine = pl.ds(h * half, half)
        for which, gain in ((0, q_gain), (1, k_gain)):
            scale = scales[:, which : which + 1]

            def one(at, _):
                column = pl.ds(pl.multiple_of(at * head, head), head)
                normed = acc[h, which + 1, :, column] * scale * gain[:, column]
                other = pltpu.roll(normed, head // 2, 1)
                turned[which, mine, column] = (
                    normed * cosine[mine, :] + other * sine[mine, :]
                ).astype(jnp.bfloat16)
                return _

            lax.fori_loop(0, width // head, one, 0)

    def finish_value(h):
        value[pl.ds(h * half, half), :] = acc[h, 0].astype(jnp.bfloat16)

    for copy in own_copies(0):
        copy.start()
    send_far(7)
    send_far(6)
    angles = where[...] * frequency[...]
    lane = lax.broadcasted_iota(jnp.int32, (rows, head), 1)
    cosine[...] = jnp.cos(angles)
    turn = jnp.sin(angles)
    sine[...] = jnp.where(lane < head // 2, -turn, turn)

    for which in range(3):
        load(which, 0).wait()
    product(0, 0, 0, 3)
    for h in range(2):
        if h == 1:
            product(1, 0, 0, 3)
            for copy in sum_copies(0):
                copy.wait()
            rotate_half(0)
            send_far(4)
            send_far(2)
        else:
            for copy in own_copies(0):
                copy.wait_recv()
            for copy in forwards(0):
                copy.start()
            for copy in own_copies(1):
                copy.start()
        for step in (1, 2):
            if h == 0:
                for which in range(3):
                    load(which, step).wait()
            product(h, step, 0, 3)
        for copy in forwards(h):
            copy.wait_recv()
        if h == 0:
            for which in range(3):
                load(which, 3).wait()
        product(h, 3, 0, 1)
        finish_value(h)
        send_far(h)
        product(h, 3, 1, 3)
        sums[h, 0] = turned_sums([squared(h, 1), squared(h, 2)])
        for copy in sum_copies(h):
            copy.start()
        if h == 0:
            for copy in own_copies(1):
                copy.wait_recv()
            for copy in forwards(1):
                copy.start()
    for copy in sum_copies(1):
        copy.wait()
    rotate_half(1)
    send_far(5)
    send_far(3)
    side = width // 2
    exits = (cross, right, over, corner)

    def load_out(step):
        return pltpu.make_async_copy(
            w_out.at[:, pl.ds(pl.multiple_of(exits[step] * width, width), width)],
            held.at[0, step],
            w_sem.at[3, step],
        )

    def order_of(row):
        per = 128 // chunk
        tiles = []
        for first in range(0, shards, per):
            tile = meta_got[first, pl.ds(row, 1), :]
            for more in range(1, per):
                tile = tile + meta_got[first + more, pl.ds(row, 1), :]
            tiles.append(tile)
        return jnp.concatenate(tiles, axis=1)

    def pack(block, _):
        aim(hits, order_of(block))
        at = pl.ds(pl.multiple_of(block * chunk, chunk), chunk)
        into = pl.ds(pl.multiple_of(block * rows, rows), rows)
        both = jnp.dot(
            hits[...],
            qk_rows[:, at, :].reshape(rows, 2 * head),
            preferred_element_type=jnp.float32,
        ).astype(jnp.bfloat16)
        queries[into, :] = both[:, :head]
        keys[into, :] = both[:, head:]
        values[:, into] = (
            jnp.dot(
                hits[...],
                v_rows[:, at, :].reshape(rows, head),
                preferred_element_type=jnp.float32,
            )
            .T.astype(jnp.bfloat16)
        )
        return _

    scale = head ** (-0.5) * math.log2(math.e)

    def attend(part, block, steps):
        depth = half * (part + 1)
        unrolled = isinstance(steps, int)

        def repeat(step, state):
            if not unrolled:
                return lax.fori_loop(0, steps, step, state)
            for at in range(steps):
                state = step(at, state)
            return state

        def folded(tile, fold):
            return fold(tile.reshape(tile.shape[0] // 8, 8, half), axis=0)

        query = queries[pl.ds(pl.multiple_of(block * rows + part * half, half), half), :]
        begin = begins[pl.ds(2 * block + part, 1), :]

        def score(base, count):
            return lax.dot_general(
                keys[pl.ds(base, count), :],
                query,
                (((1,), (1,)), ((), ())),
                preferred_element_type=jnp.float32,
            )

        def earlier(step):
            return pl.multiple_of((block - 1 - step) * rows, rows)

        def stored(step):
            at = step * rows
            return pl.ds(at if unrolled else pl.multiple_of(at, rows), rows)

        base = pl.multiple_of(block * rows, rows)
        key_row = lax.broadcasted_iota(jnp.int32, (depth, half), 0)
        query_row = lax.broadcasted_iota(jnp.int32, (depth, half), 1) + part * half
        seen = (key_row >= begin - base) & (key_row <= query_row)
        last = jnp.where(seen, score(base, depth), -1e30)
        scores[reach * rows : reach * rows + depth, :] = last

        def first_pass(step, top):
            key_row = lax.broadcasted_iota(jnp.int32, (rows, half), 0)
            tile = jnp.where(
                key_row >= begin - earlier(step), score(earlier(step), rows), -1e30
            )
            scores[stored(step), :] = tile
            return jnp.maximum(top, folded(tile, jnp.max))

        top = repeat(first_pass, folded(last, jnp.max))
        top = jnp.max(top, axis=0, keepdims=True)

        def weigh(tile, base, count):
            weights = jnp.exp2((tile - top) * scale)
            return folded(weights, jnp.sum), jnp.dot(
                values[:, pl.ds(base, count)],
                weights.astype(jnp.bfloat16),
                preferred_element_type=jnp.float32,
            )

        def second_pass(step, state):
            total, weighted = weigh(scores[stored(step), :], earlier(step), rows)
            return state[0] + total, state[1] + weighted

        state = weigh(scores[reach * rows : reach * rows + depth, :], base, depth)
        total, weighted = repeat(second_pass, state)
        total = jnp.sum(total, axis=0, keepdims=True)
        heads[part, block] = (weighted / total).T.astype(jnp.bfloat16)

    def attend_first(part):
        def one(block, _):
            attend(part, block, block)
            return _

        lax.fori_loop(0, reach, one, 0)

    def attend_last(part):
        def one(block, _):
            attend(part, block, reach)
            return _

        lax.fori_loop(reach, shards, one, 0)

    def project(part):
        def one(step, _):
            done = jnp.dot(
                attended[pl.ds(part * half, half), :],
                held[0, step],
                preferred_element_type=jnp.float32,
            )
            acc[part, 0] = done
            held[1, step, pl.ds(part * half, half), :] = done.astype(jnp.bfloat16)
            return _

        lax.fori_loop(0, 4, one, 0)

    def sent_at(part, step, column):
        return held.at[1, step, pl.ds(part * half, half), column]

    def reduce_copy(src, dst, peer, sem):
        return pltpu.make_async_remote_copy(
            src_ref=src,
            dst_ref=dst,
            send_sem=near_send.at[sem],
            recv_sem=near_recv.at[sem],
            device_id={"rep": peer},
            device_id_type=MESH,
        )

    left, rest = pl.ds(0, side), pl.ds(side, side)

    def first_copies(part):
        return (
            reduce_copy(sent_at(part, 0, left), first_got.at[part, 0], right, 8 + 6 * part),
            reduce_copy(sent_at(part, 1, left), first_got.at[part, 1], right, 8 + 6 * part + 1),
            reduce_copy(sent_at(part, 0, rest), first_got.at[part, 2], over, 8 + 6 * part + 2),
            reduce_copy(sent_at(part, 2, rest), first_got.at[part, 3], over, 8 + 6 * part + 3),
        )

    def second_copies(part):
        return (
            reduce_copy(sent_at(part, 2, left), second_got.at[part, 0], over, 8 + 6 * part + 4),
            reduce_copy(sent_at(part, 1, rest), second_got.at[part, 1], right, 8 + 6 * part + 5),
        )

    def start(copies):
        for copy in copies:
            copy.start()

    def middle(part):
        for copy in first_copies(part):
            copy.wait_recv()
        for step, column, at in ((2, left, 0), (1, rest, 2)):
            mine_rows = pl.ds(part * half, half)
            held[1, step, mine_rows, column] = (
                held[1, step, mine_rows, column].astype(jnp.float32)
                + first_got[part, at].astype(jnp.float32)
            ).astype(jnp.bfloat16)
        start(second_copies(part))
        for column, at in ((left, 1), (rest, 3)):
            acc[part, 0, :, column] = acc[part, 0, :, column] + first_got[part, at].astype(jnp.float32)

    def mixed_copies(part):
        return [
            pltpu.make_async_remote_copy(
                src_ref=sums.at[2 + part, 0],
                dst_ref=sums.at[2 + part, at + 1],
                send_sem=sum_send.at[2 + part, at],
                recv_sem=sum_recv.at[2 + part, at],
                device_id={"rep": peer},
                device_id_type=MESH,
            )
            for at, peer in enumerate((right, over, cross))
        ]

    def total(part):
        for copy in second_copies(part):
            copy.wait_recv()
        squares = jnp.zeros((half, head), jnp.float32)
        for at in range(width // head):
            column = pl.ds(at * head, head)
            got = second_got[part, at * head // side, :, pl.ds(at * head % side, head)]
            rows_now = acc[part, 0, :, column] + got.astype(jnp.float32)
            acc[part, 0, :, column] = rows_now
            squares = squares + rows_now * rows_now
        sums[2 + part, 0] = turned_sums([jnp.sum(squares, axis=1, keepdims=True)])
        start(mixed_copies(part))

    def settle(part):
        for copy in mixed_copies(part):
            copy.wait()
        whole = sums[2 + part, 0] + sums[2 + part, 1] + sums[2 + part, 2] + sums[2 + part, 3]
        scales = lax.rsqrt(whole / full_width + EPSILON)
        scales = jnp.concatenate([scales] * (128 // 8), axis=0).T[:, 0:1]
        at = pl.ds(part * half, half)
        got[1, at, :] = (
            got[0, at, :].astype(jnp.float32) + acc[part, 0] * scales * post_gain[...]
        ).astype(jnp.bfloat16)

    def written(part):
        at = pl.ds(part * half, half)
        return pltpu.make_async_copy(got.at[1, at, :], out.at[at, :], out_sem.at[part])

    for step in range(4):
        load_out(step).start()
    for h in range(2):
        for copy in own_copies(h) + forwards(h):
            copy.wait_send()
    aim(hits, slot_rank[...])
    select(hits, value, picked.at[1])
    select(hits, turned.at[1], picked.at[0])
    wait_far(7)
    slot_order[...] = jnp.broadcast_to(order_of(shards + me), slot_order.shape)
    wait_far(6)
    aim(hits, order_of(me))
    select(hits, arrived, got.at[0])
    for kind in (0, 2, 4):
        wait_far(kind)
    lax.fori_loop(0, reach, pack, 0)
    attend_first(0)
    attend_first(1)
    for kind in (1, 3, 5):
        wait_far(kind)
    send_heads(0, 0, reach)
    send_heads(1, 0, reach)
    send_far(11)
    lax.fori_loop(reach, shards, pack, 0)
    attend_last(0)
    send_heads(0, reach, shards)
    attend_last(1)
    send_heads(1, reach, shards)
    for step in range(4):
        load_out(step).wait()
    wait_far(8)
    project(0)
    start(first_copies(0))
    wait_far(9)
    send_far(10)
    project(1)
    start(first_copies(1))
    middle(0)
    total(0)
    middle(1)
    settle(0)
    written(0).start()
    total(1)
    settle(1)
    written(1).start()
    wait_far(11)
    wait_far(10)
    for part in range(2):
        for copy in first_copies(part) + second_copies(part):
            copy.wait_send()
        written(part).wait()


def whole_heads(
    piece, w_value, w_query, w_key, w_out, q_gain, k_gain, post_gain,
    where, frequency, meta, slot_rank, begins, shards,
):
    rows, width = piece.shape
    full_width = w_query.shape[0]
    half = rows // 2
    head = HEAD_DIM
    reach = shards // 2
    inside = pl.BlockSpec(memory_space=pltpu.VMEM)
    outside = pl.BlockSpec(memory_space=pl.ANY)
    dma = pltpu.SemaphoreType.DMA
    return pl.pallas_call(
        functools.partial(whole_kernel, shards=shards, full_width=full_width),
        out_shape=(jax.ShapeDtypeStruct((rows, width), jnp.bfloat16),) * 3
        + (jax.ShapeDtypeStruct((8, rows), jnp.int32),),
        in_specs=[inside] + [outside] * 4 + [inside] * 8,
        out_specs=(outside,) * 3 + (inside,),
        scratch_shapes=[
            pltpu.VMEM((3, 4, width, width), jnp.bfloat16),
            pltpu.VMEM((3, rows, width), jnp.bfloat16),
            pltpu.VMEM((2, 3, half, width), jnp.float32),
            pltpu.VMEM((2, rows, width), jnp.bfloat16),
            pltpu.VMEM((rows, width), jnp.bfloat16),
            pltpu.VMEM((rows, head), jnp.float32),
            pltpu.VMEM((rows, head), jnp.float32),
            pltpu.VMEM((4, 4, 8, half), jnp.float32),
            pltpu.VMEM((2, rows, width), jnp.bfloat16),
            pltpu.VMEM((rows, rows), jnp.bfloat16),
            pltpu.VMEM((shards, rows, 2 * head), jnp.bfloat16),
            pltpu.VMEM((shards, rows, head), jnp.bfloat16),
            pltpu.VMEM((rows, width), jnp.bfloat16),
            pltpu.VMEM((shards,) + meta.shape, jnp.int32),
            pltpu.VMEM((shards * rows, head), jnp.bfloat16),
            pltpu.VMEM((shards * rows, head), jnp.bfloat16),
            pltpu.VMEM((head, shards * rows), jnp.bfloat16),
            pltpu.VMEM(((reach + 1) * rows, half), jnp.float32),
            pltpu.VMEM((2, shards, half, head), jnp.bfloat16),
            pltpu.VMEM((rows, width), jnp.bfloat16),
            pltpu.VMEM((2, 4, half, width // 2), jnp.bfloat16),
            pltpu.VMEM((2, 2, half, width // 2), jnp.bfloat16),
            dma((4, 4)),
            dma((20,)),
            dma((20,)),
            dma((4, 3)),
            dma((4, 3)),
            dma((12, shards - 1)),
            dma((12, shards - 1)),
            dma((12,)),
            dma((2,)),
        ],
        compiler_params=pltpu.CompilerParams(
            collective_id=1, has_side_effects=True, vmem_limit_bytes=60 << 20
        ),
        cost_estimate=pl.CostEstimate(
            flops=8 * rows * full_width * width + 20 * rows * rows * shards * head,
            bytes_accessed=8 * full_width * width + 16 * rows * width,
            transcendentals=5 * rows * rows * shards,
        ),
    )(
        piece, w_value, w_query, w_key, w_out, q_gain, k_gain, post_gain,
        where, frequency, meta, slot_rank, begins,
    )


def place_kernel(order, rows_in, keys_in, values_in, rows_out, keys_out, values_out, hits):
    aim(hits, order[0:1, :])
    rows_out[...] = rows_in[...]
    select(hits, keys_in, keys_out)
    select(hits, values_in, values_out)


def place_rows(order, result, keys_landed, values_landed):
    rows, width = result.shape
    block = pl.BlockSpec((rows, width // 4), lambda i: (0, i))
    return pl.pallas_call(
        place_kernel,
        out_shape=(jax.ShapeDtypeStruct((rows, width), jnp.bfloat16),) * 3,
        grid=(4,),
        in_specs=[pl.BlockSpec((8, rows), lambda i: (0, 0))] + [block] * 3,
        out_specs=(block,) * 3,
        scratch_shapes=[pltpu.VMEM((rows, rows), jnp.bfloat16)],
        compiler_params=pltpu.CompilerParams(vmem_limit_bytes=16 << 20),
    )(order, result, keys_landed, values_landed)


def body_heads(
    hidden_in,
    w_query,
    w_key,
    w_value,
    w_out,
    q_gain,
    k_gain,
    post_gain,
    prompt_lengths,
    segment_ids,
    deal,
    inverse,
    slots,
):
    tok_rows, width_dev = hidden_in.shape
    full_width = w_query.shape[0]
    head_size = HEAD_DIM
    shards = lax.axis_size("tok")
    chunk = tok_rows // shards
    me = lax.axis_index("tok")
    first_row = me * tok_rows

    local = jnp.arange(tok_rows, dtype=jnp.int32)
    starts = starts_of(prompt_lengths)
    my_packed = lax.dynamic_slice_in_dim(deal, first_row, tok_rows)
    my_slots = lax.dynamic_slice_in_dim(slots, first_row, tok_rows)

    def ranking(keys):
        return jnp.sum((keys[None, :] < keys[:, None]).astype(jnp.int32), axis=1)

    sort_hits = ranking(my_packed)[None, :] == local[:, None]
    sorted_packed = jnp.sum(jnp.where(sort_hits, my_packed[None, :], 0), axis=1)
    sorted_slots = jnp.sum(jnp.where(sort_hits, my_slots[None, :], 0), axis=1)
    slot_rank = ranking(sorted_slots)
    slot_hits = slot_rank[None, :] == local[:, None]
    slots_rising = jnp.sum(jnp.where(slot_hits, sorted_slots[None, :], 0), axis=1)
    my_start = jnp.max(
        jnp.where(starts[None, :] <= sorted_packed[:, None], starts[None, :], 0), axis=1
    )
    positions = (sorted_packed - my_start).astype(jnp.float32)
    base = jnp.arange(shards, dtype=jnp.int32)[:, None] * tok_rows
    sent_orders = jnp.concatenate(
        [sorted_packed.reshape(shards, chunk) - base, slots_rising.reshape(shards, chunk) - base],
        axis=0,
    )
    per = 128 // chunk
    column = jnp.arange(per, dtype=jnp.int32)[None, :, None]
    meta = jnp.where(column == me % per, sent_orders[:, None, :], 0).reshape(2 * shards, 128)
    every = jnp.arange(shards * tok_rows, dtype=jnp.int32)
    begins = jnp.max(jnp.where(starts[:, None] <= every[None, :], starts[:, None], 0), axis=0)
    half_size = head_size // 2
    frequency = ROPE_BASE ** (-jnp.arange(half_size, dtype=jnp.float32) * 2.0 / head_size)
    frequency = jnp.concatenate([frequency, frequency])[None, :]

    piece = select_rows(sort_hits, hidden_in)
    result, keys_landed, values_landed, slot_order = whole_heads(
        piece,
        w_value,
        w_query,
        w_key,
        w_out,
        q_gain[None, :],
        k_gain[None, :],
        post_gain[None, :],
        positions[:, None],
        frequency,
        meta,
        slot_rank[None, :],
        begins.reshape(2 * shards, tok_rows // 2),
        shards,
    )
    return place_rows(slot_order, result, keys_landed, values_landed)


def solution(mesh):
    def pick(*operands):
        rows, width = operands[0].shape
        shards = mesh.shape["tok"]
        fits = width == shards * HEAD_DIM and rows == shards * 64 and mesh.shape["rep"] == 4
        chosen = body_heads if fits else body
        return chosen(*operands)

    return jax.shard_map(
        pick,
        mesh=mesh,
        in_specs=(
            P("tok", "rep"),
            P(None, "rep"),
            P(None, "rep"),
            P(None, "rep"),
            P("rep", None),
            P("rep"),
            P("rep"),
            P("rep"),
            P(),
            P(),
            P(),
            P(),
            P(),
        ),
        out_specs=(P("tok", "rep"), P("tok", "rep"), P("tok", "rep")),
        check_vma=False,
    )
```

```python
import functools
import math

import jax
import jax.numpy as jnp
import numpy as np
from jax import lax
from jax.experimental import pallas as pl
from jax.experimental.pallas import tpu as pltpu
from jax.sharding import PartitionSpec as P

HEAD_DIM = 128


EPSILON = 1e-06
ROPE_BASE = 500000.0


def rotate(values, positions):
    half_size = values.shape[-1] // 2
    frequency = ROPE_BASE ** (-jnp.arange(half_size, dtype=jnp.float32) * 2.0 / values.shape[-1])
    angles = positions.astype(jnp.float32)[:, None] * frequency[None, :]
    cosine = jnp.cos(angles)[:, None, :]
    sine_part = jnp.sin(angles)[:, None, :]
    lower_half = values[..., :half_size]
    upper_half = values[..., half_size:]
    return jnp.concatenate(
        [
            lower_half * cosine - upper_half * sine_part,
            upper_half * cosine + lower_half * sine_part,
        ],
        axis=-1,
    )


def starts_of(lengths):
    index = jnp.arange(lengths.shape[0], dtype=jnp.int32)
    return jnp.sum(jnp.where(index[None, :] < index[:, None], lengths[None, :], 0), axis=1)


def bucketed(table_rows, row_order, shards):
    picked = table_rows[row_order]
    return picked.reshape(shards, picked.shape[0] // shards, picked.shape[1])


def placement_order(sources, shard_rows):
    local_ids = jnp.arange(sources.shape[0], dtype=jnp.int32)
    arrival = jnp.argsort(sources * shard_rows + local_ids)
    return jnp.argsort(arrival)


def body(
    hidden_in,
    w_query,
    w_key,
    w_value,
    w_out,
    q_gain,
    k_gain,
    post_gain,
    prompt_lengths,
    segment_ids,
    deal,
    inverse,
    slots,
):
    tok_rows, width_dev = hidden_in.shape
    full_width = w_query.shape[0]
    head_size = HEAD_DIM
    heads_dev = width_dev // head_size
    shards = lax.axis_size("tok")
    first_row = lax.axis_index("tok") * tok_rows
    my_packed = lax.dynamic_slice_in_dim(deal, first_row, tok_rows)
    my_segment = segment_ids[my_packed]
    prompt_ids = jnp.arange(prompt_lengths.shape[0], dtype=jnp.int32)
    prompt_starts = starts_of(prompt_lengths)
    my_start = jnp.sum(
        jnp.where(my_segment[:, None] == prompt_ids[None, :], prompt_starts[None, :], 0), axis=1
    )
    positions = my_packed - my_start
    pieces = lax.all_gather(hidden_in, "rep", axis=1, tiled=True)
    query_rows = jnp.dot(pieces, w_query, preferred_element_type=jnp.float32)
    key_rows = jnp.dot(pieces, w_key, preferred_element_type=jnp.float32)
    value_rows = jnp.dot(pieces, w_value, preferred_element_type=jnp.float32)
    query_sums, key_sums = lax.psum(
        (jnp.sum(query_rows * query_rows, axis=1), jnp.sum(key_rows * key_rows, axis=1)), "rep"
    )
    query_rows = (
        query_rows * lax.rsqrt(query_sums / full_width + EPSILON)[:, None] * q_gain[None, :]
    )
    key_rows = key_rows * lax.rsqrt(key_sums / full_width + EPSILON)[:, None] * k_gain[None, :]
    query_rot = rotate(query_rows.reshape(tok_rows, heads_dev, head_size), positions).astype(
        jnp.bfloat16
    )
    key_rot = (
        rotate(key_rows.reshape(tok_rows, heads_dev, head_size), positions)
        .astype(jnp.bfloat16)
        .reshape(tok_rows, width_dev)
    )
    value_half = value_rows.astype(jnp.bfloat16)
    scale = head_size ** (-0.5)

    def attend(state_now, key_block, value_block, key_packed):
        row_top, totals, weighted = state_now
        block_keys = key_block.reshape(key_block.shape[0], heads_dev, head_size)
        block_values = value_block.reshape(value_block.shape[0], heads_dev, head_size)
        key_segment = segment_ids[key_packed]
        allowed = (key_segment[None, :] == my_segment[:, None]) & (
            key_packed[None, :] <= my_packed[:, None]
        )
        scores = (
            jnp.einsum("qhd,khd->hqk", query_rot, block_keys, preferred_element_type=jnp.float32)
            * scale
        )
        masked = jnp.where(allowed[None], scores, -1e30)
        new_top = jnp.maximum(row_top, jnp.max(masked, axis=2))
        weights = jnp.where(allowed[None], jnp.exp(masked - new_top[:, :, None]), 0.0)
        factor = jnp.exp(row_top - new_top)
        totals = totals * factor + jnp.sum(weights, axis=2)
        weighted = weighted * factor[:, :, None] + jnp.einsum(
            "hqk,khd->hqd",
            weights.astype(jnp.bfloat16),
            block_values,
            preferred_element_type=jnp.float32,
        )
        return (new_top, totals, weighted)

    start_state = (
        jnp.full((heads_dev, tok_rows), -1e30, jnp.float32),
        jnp.zeros((heads_dev, tok_rows), jnp.float32),
        jnp.zeros((heads_dev, tok_rows, head_size), jnp.float32),
    )
    owned_rows = lax.dynamic_slice_in_dim(jnp.argsort(slots), first_row, tok_rows)
    my_slots = lax.dynamic_slice_in_dim(slots, first_row, tok_rows)
    slot_order = jnp.argsort(my_slots)
    sent_keys, sent_values = (
        lax.all_to_all(
            bucketed(key_rot, slot_order, shards), "tok", split_axis=0, concat_axis=0, tiled=True
        ),
        lax.all_to_all(
            bucketed(value_half, slot_order, shards), "tok", split_axis=0, concat_axis=0, tiled=True
        ),
    )
    arrival = placement_order(owned_rows // tok_rows, tok_rows)
    cache_keys = sent_keys.reshape(tok_rows, width_dev)[arrival]
    cache_values = sent_values.reshape(tok_rows, width_dev)[arrival]
    pieces = (
        lax.all_gather(key_rot, "tok", axis=0, tiled=True),
        lax.all_gather(value_half, "tok", axis=0, tiled=True),
    )
    key_all = pieces[0]
    block_size = math.gcd(key_all.shape[0], tok_rows)
    block_count = key_all.shape[0] // block_size

    def advance(state_in, block_set):
        return (attend(state_in, block_set[0], block_set[1], block_set[2]), None)

    state_out, _ = lax.scan(
        advance,
        start_state,
        (
            key_all.reshape(block_count, block_size, width_dev),
            pieces[1].reshape(block_count, block_size, width_dev),
            deal.reshape(block_count, block_size),
        ),
    )
    row_top, totals, weighted = state_out
    attended = (
        (weighted / totals[:, :, None])
        .transpose(1, 0, 2)
        .reshape(tok_rows, width_dev)
        .astype(jnp.bfloat16)
    )
    mixed_rows = (
        lax.psum_scatter(
            lax.dot_general(
                w_out, attended, (((0,), (1,)), ((), ())), preferred_element_type=jnp.float32
            ).astype(jnp.bfloat16),
            "rep",
            scatter_dimension=0,
            tiled=True,
        )
        .astype(jnp.float32)
        .T
    )
    mixed_sums = lax.psum(jnp.sum(mixed_rows * mixed_rows, axis=1), "rep")
    normed_rows = (
        mixed_rows * lax.rsqrt(mixed_sums / full_width + EPSILON)[:, None] * post_gain[None, :]
    )
    result_rows = (hidden_in.astype(jnp.float32) + normed_rows).astype(jnp.bfloat16)
    packed_order = jnp.argsort(my_packed)
    returned = lax.all_to_all(
        bucketed(result_rows, packed_order, shards), "tok", split_axis=0, concat_axis=0, tiled=True
    )
    my_dealt = lax.dynamic_slice_in_dim(inverse, first_row, tok_rows)
    output = returned.reshape(tok_rows, width_dev)[placement_order(my_dealt // tok_rows, tok_rows)]
    return (output, cache_keys, cache_values)


MESH = pl.DeviceIdType.MESH


def greet(peers):
    barrier = pltpu.get_barrier_semaphore()
    for peer in peers:
        pl.semaphore_signal(barrier, inc=1, device_id=peer, device_id_type=MESH)
    pl.semaphore_wait(barrier, len(peers))


def places():
    corner = lax.axis_index("rep")
    right = corner + 1 - 2 * (corner % 2)
    over = corner + 2 - 4 * (corner // 2)
    return corner, right, over, 3 - corner


def turned_sums(columns):
    rows = columns[0].shape[0]
    lane = lax.broadcasted_iota(jnp.int32, (rows, 128), 1)
    wide = jnp.zeros((rows, 128), jnp.float32)
    for at, column in enumerate(columns):
        wide = jnp.where(lane == at, column, wide)
    return wide.T[0:8, :]


def aim(hits, order):
    row = lax.broadcasted_iota(jnp.int32, hits.shape, 0)
    hits[...] = jnp.where(row == order, 1.0, 0.0).astype(jnp.bfloat16)


def select(hits, src, dst):
    dst[...] = jnp.dot(hits[...], src[...], preferred_element_type=jnp.float32).astype(
        jnp.bfloat16
    )


def whole_kernel(
    hidden_in, w_value, w_query, w_key, w_out, q_gain, k_gain, post_gain,
    frequency, deal, slots, lengths,
    out, keys_out, values_out, slot_order,
    piece, meta, slot_rank,
    held, got, acc, turned, value, cosine, sine, sums, picked, hits,
    qk_rows, v_rows, arrived, meta_got, queries, keys, values, scores, heads, attended,
    first_got, second_got,
    w_sem, near_send, near_recv, sum_send, sum_recv, far_send, far_recv, own_sem, out_sem,
    *, shards, full_width,
):
    rows, width = piece.shape
    half = rows // 2
    quarter = half // 2
    chunk = rows // shards
    head = HEAD_DIM
    me = lax.axis_index("tok")
    corner, right, over, cross = places()
    reach = shards // 2
    weights = (w_value, w_query, w_key)
    owners = (corner, right, over, cross)

    def load(which, step):
        return pltpu.make_async_copy(
            weights[which].at[pl.ds(pl.multiple_of(owners[step] * width, width), width), :],
            held.at[which, step],
            w_sem.at[which, step],
        )

    fetch = pltpu.make_async_copy(hidden_in, value, out_sem.at[0])
    fetch.start()
    for step in range(4):
        for which in range(3):
            load(which, step).start()

    starts = [jnp.int32(0)]
    for prompt in range(lengths.shape[0] - 1):
        starts.append(starts[-1] + lengths[prompt])

    def begin_of(tokens):
        begin = jnp.zeros_like(tokens)
        for start in starts:
            start = start.astype(tokens.dtype)
            begin = jnp.where(tokens >= start, start, begin)
        return begin

    def upright(row):
        return jnp.broadcast_to(row, (128, rows)).T

    def ranks(row):
        below = jnp.where(upright(row)[:, 0:1] < row, 1.0, 0.0)
        return jnp.sum(below, axis=0, keepdims=True)

    def ordered(rank, row):
        place = lax.broadcasted_iota(jnp.int32, (rows, rows), 1).astype(jnp.float32)
        chosen = jnp.where(upright(rank)[:, 0:1] == place, upright(row)[:, 0:1], 0.0)
        return jnp.sum(chosen, axis=0, keepdims=True)

    my_packed = deal[pl.ds(me, 1), :].astype(jnp.float32)
    my_slots = slots[pl.ds(me, 1), :].astype(jnp.float32)
    rank = ranks(my_packed)
    aim(hits, rank.astype(jnp.int32))
    fetch.wait()
    select(hits, value, piece)
    sorted_packed = ordered(rank, my_packed)
    sorted_slots = ordered(rank, my_slots)
    rank = ranks(sorted_slots)
    slot_rank[...] = jnp.broadcast_to(rank.astype(jnp.int32), slot_rank.shape)
    lane = lax.broadcasted_iota(jnp.int32, (8, 128), 1)
    for first, row in ((0, sorted_packed), (shards, ordered(rank, sorted_slots))):
        for owner in range(shards):
            at = owner * chunk
            tile = jnp.broadcast_to(row[:, at // 128 * 128 : at // 128 * 128 + 128], (8, 128))
            tile = tile - owner * rows
            moved = pltpu.roll(tile, chunk, 1)
            tile = jnp.where(owner % 2 == me % 2, tile, moved)
            tile = jnp.where(lane // chunk == me % 2, tile, 0.0)
            meta[first + owner : first + owner + 1, :] = tile[0:1, :].astype(jnp.int32)

    others = [(me + 1 + d) % shards for d in range(shards - 1)]
    greet([{"rep": peer} for peer in (right, over, cross)] + [{"tok": peer} for peer in others])

    def near(src, slot, at, size, peer, sem):
        return pltpu.make_async_remote_copy(
            src_ref=src.at[pl.ds(at, size), :],
            dst_ref=got.at[slot, pl.ds(at, size), :],
            send_sem=near_send.at[sem],
            recv_sem=near_recv.at[sem],
            device_id={"rep": peer},
            device_id_type=MESH,
        )

    def own_copies(h):
        return (
            near(piece, 0, h * half, half, right, 4 * h),
            near(piece, 1, h * half, half, over, 4 * h + 1),
        )

    def forwards(h):
        return (
            near(got.at[1], 2, h * half, quarter, right, 4 * h + 2),
            near(got.at[0], 2, h * half + quarter, quarter, over, 4 * h + 3),
        )

    def to_far(kind, d, src, dst):
        return pltpu.make_async_remote_copy(
            src_ref=src,
            dst_ref=dst,
            send_sem=far_send.at[kind, d],
            recv_sem=far_recv.at[kind, d],
            device_id={"tok": (me + 1 + d) % shards},
            device_id_type=MESH,
        )

    def head_of(ref, h, owner):
        return ref.at[pl.ds(h * half, half), pl.ds(pl.multiple_of(owner * head, head), head)]

    def source_of(kind, peer):
        if kind < 2:
            return head_of(value, kind, peer)
        if kind < 6:
            return head_of(turned.at[(kind - 2) // 2], kind % 2, peer)
        if kind == 7:
            return meta
        if kind < 10 and kind > 7:
            return heads.at[kind - 8, peer]
        source = piece if kind == 6 else picked.at[kind - 10]
        return source.at[pl.ds(pl.multiple_of(peer * chunk, chunk), chunk), :]

    def landing(kind):
        if kind < 2:
            return v_rows.at[me, pl.ds(kind * half, half), :]
        if kind < 6:
            return qk_rows.at[
                me, pl.ds((kind % 2) * half, half), pl.ds(((kind - 2) // 2) * head, head)
            ]
        if kind == 7:
            return meta_got.at[me]
        if kind < 10 and kind > 7:
            return attended.at[
                pl.ds((kind - 8) * half, half), pl.ds(pl.multiple_of(me * head, head), head)
            ]
        target = arrived if kind == 6 else (keys_out, values_out)[kind - 10]
        return target.at[pl.ds(pl.multiple_of(me * chunk, chunk), chunk), :]

    def own_copy(kind):
        return pltpu.make_async_copy(source_of(kind, me), landing(kind), own_sem.at[kind])

    def far_copy(kind, d):
        return to_far(kind, d, source_of(kind, (me + 1 + d) % shards), landing(kind))

    def send_far(kind):
        def one(d, _):
            far_copy(kind, d).start()
            return _

        lax.fori_loop(0, shards - 1, one, 0)
        own_copy(kind).start()

    def send_heads(part, low, high):
        def one(peer, _):
            @pl.when(peer != me)
            def _():
                far_copy(8 + part, (peer + shards - me - 1) % shards).start()

            @pl.when(peer == me)
            def _():
                own_copy(8 + part).start()

            return _

        def each(peer, _):
            one(peer, None)
            return _

        lax.fori_loop(low, high, each, 0)

    def wait_far(kind):
        def one(d, _):
            far_copy(kind, d).wait()
            return _

        lax.fori_loop(0, shards - 1, one, 0)
        own_copy(kind).wait()

    def product(h, step, low, high):
        left = piece if step == 0 else got.at[step - 1]

        def one(which, _):
            part = jnp.dot(
                left[pl.ds(h * half, half), :],
                held[which, step],
                preferred_element_type=jnp.float32,
            )
            if step > 0:
                part = part + acc[h, which]
            acc[h, which] = part
            return _

        lax.fori_loop(low, high, one, 0)

    def squared(h, which):
        total = jnp.zeros((half, head), jnp.float32)
        for at in range(width // head):
            part = acc[h, which, :, at * head : (at + 1) * head]
            total = total + part * part
        return jnp.sum(total, axis=1, keepdims=True)

    def sum_copy(h, at, peer):
        return pltpu.make_async_remote_copy(
            src_ref=sums.at[h, 0],
            dst_ref=sums.at[h, at + 1],
            send_sem=sum_send.at[h, at],
            recv_sem=sum_recv.at[h, at],
            device_id={"rep": peer},
            device_id_type=MESH,
        )

    def sum_copies(h):
        return [sum_copy(h, at, peer) for at, peer in enumerate((right, over, cross))]

    def rotate_half(h):
        total = sums[h, 0] + sums[h, 1] + sums[h, 2] + sums[h, 3]
        scales = lax.rsqrt(total / full_width + EPSILON)
        scales = jnp.concatenate([scales] * (128 // 8), axis=0).T
        mine = pl.ds(h * half, half)
        for which, gain in ((0, q_gain), (1, k_gain)):
            scale = scales[:, which : which + 1]

            def one(at, _):
                column = pl.ds(pl.multiple_of(at * head, head), head)
                normed = acc[h, which + 1, :, column] * scale * gain[:, column]
                other = pltpu.roll(normed, head // 2, 1)
                turned[which, mine, column] = (
                    normed * cosine[mine, :] + other * sine[mine, :]
                ).astype(jnp.bfloat16)
                return _

            lax.fori_loop(0, width // head, one, 0)

    def finish_value(h):
        value[pl.ds(h * half, half), :] = acc[h, 0].astype(jnp.bfloat16)

    for copy in own_copies(0):
        copy.start()
    send_far(7)
    send_far(6)
    angles = upright(sorted_packed - begin_of(sorted_packed)) * frequency[...]
    lane = lax.broadcasted_iota(jnp.int32, (rows, head), 1)
    cosine[...] = jnp.cos(angles)
    turn = jnp.sin(angles)
    sine[...] = jnp.where(lane < head // 2, -turn, turn)

    for which in range(3):
        load(which, 0).wait()
    product(0, 0, 0, 3)
    for h in range(2):
        if h == 1:
            product(1, 0, 0, 3)
            for copy in sum_copies(0):
                copy.wait()
            rotate_half(0)
            send_far(4)
            send_far(2)
        else:
            for copy in own_copies(0):
                copy.wait_recv()
            for copy in forwards(0):
                copy.start()
            for copy in own_copies(1):
                copy.start()
        for step in (1, 2):
            if h == 0:
                for which in range(3):
                    load(which, step).wait()
            product(h, step, 0, 3)
        for copy in forwards(h):
            copy.wait_recv()
        if h == 0:
            for which in range(3):
                load(which, 3).wait()
        product(h, 3, 0, 1)
        finish_value(h)
        send_far(h)
        product(h, 3, 1, 3)
        sums[h, 0] = turned_sums([squared(h, 1), squared(h, 2)])
        for copy in sum_copies(h):
            copy.start()
        if h == 0:
            for copy in own_copies(1):
                copy.wait_recv()
            for copy in forwards(1):
                copy.start()
    for copy in sum_copies(1):
        copy.wait()
    rotate_half(1)
    send_far(5)
    send_far(3)
    side = width // 2
    exits = (cross, right, over, corner)

    def load_out(step):
        return pltpu.make_async_copy(
            w_out.at[:, pl.ds(pl.multiple_of(exits[step] * width, width), width)],
            held.at[0, step],
            w_sem.at[3, step],
        )

    def order_of(row):
        per = 128 // chunk
        tiles = []
        for first in range(0, shards, per):
            tile = meta_got[first, pl.ds(row, 1), :]
            for more in range(1, per):
                tile = tile + meta_got[first + more, pl.ds(row, 1), :]
            tiles.append(tile)
        return jnp.concatenate(tiles, axis=1)

    def pack(block, _):
        aim(hits, order_of(block))
        at = pl.ds(pl.multiple_of(block * chunk, chunk), chunk)
        into = pl.ds(pl.multiple_of(block * rows, rows), rows)
        both = jnp.dot(
            hits[...],
            qk_rows[:, at, :].reshape(rows, 2 * head),
            preferred_element_type=jnp.float32,
        ).astype(jnp.bfloat16)
        queries[into, :] = both[:, :head]
        keys[into, :] = both[:, head:]
        values[:, into] = (
            jnp.dot(
                hits[...],
                v_rows[:, at, :].reshape(rows, head),
                preferred_element_type=jnp.float32,
            )
            .T.astype(jnp.bfloat16)
        )
        return _

    scale = head ** (-0.5) * math.log2(math.e)

    def attend(part, block, steps):
        depth = half * (part + 1)
        unrolled = isinstance(steps, int)

        def repeat(step, state):
            if not unrolled:
                return lax.fori_loop(0, steps, step, state)
            for at in range(steps):
                state = step(at, state)
            return state

        def folded(tile, fold):
            return fold(tile.reshape(tile.shape[0] // 8, 8, half), axis=0)

        query = queries[pl.ds(pl.multiple_of(block * rows + part * half, half), half), :]
        begin = begin_of(
            block * rows + part * half + lax.broadcasted_iota(jnp.int32, (1, half), 1)
        )

        def score(base, count):
            return lax.dot_general(
                keys[pl.ds(base, count), :],
                query,
                (((1,), (1,)), ((), ())),
                preferred_element_type=jnp.float32,
            )

        def earlier(step):
            return pl.multiple_of((block - 1 - step) * rows, rows)

        def stored(step):
            at = step * rows
            return pl.ds(at if unrolled else pl.multiple_of(at, rows), rows)

        base = pl.multiple_of(block * rows, rows)
        key_row = lax.broadcasted_iota(jnp.int32, (depth, half), 0)
        query_row = lax.broadcasted_iota(jnp.int32, (depth, half), 1) + part * half
        seen = (key_row >= begin - base) & (key_row <= query_row)
        last = jnp.where(seen, score(base, depth), -1e30)
        scores[reach * rows : reach * rows + depth, :] = last

        def first_pass(step, top):
            key_row = lax.broadcasted_iota(jnp.int32, (rows, half), 0)
            tile = jnp.where(
                key_row >= begin - earlier(step), score(earlier(step), rows), -1e30
            )
            scores[stored(step), :] = tile
            return jnp.maximum(top, folded(tile, jnp.max))

        top = repeat(first_pass, folded(last, jnp.max))
        top = jnp.max(top, axis=0, keepdims=True)

        def weigh(tile, base, count):
            weights = jnp.exp2((tile - top) * scale)
            return folded(weights, jnp.sum), jnp.dot(
                values[:, pl.ds(base, count)],
                weights.astype(jnp.bfloat16),
                preferred_element_type=jnp.float32,
            )

        def second_pass(step, state):
            total, weighted = weigh(scores[stored(step), :], earlier(step), rows)
            return state[0] + total, state[1] + weighted

        state = weigh(scores[reach * rows : reach * rows + depth, :], base, depth)
        total, weighted = repeat(second_pass, state)
        total = jnp.sum(total, axis=0, keepdims=True)
        heads[part, block] = (weighted / total).T.astype(jnp.bfloat16)

    def attend_first(part):
        def one(block, _):
            attend(part, block, block)
            return _

        lax.fori_loop(0, reach, one, 0)

    def attend_last(part):
        def one(block, _):
            attend(part, block, reach)
            return _

        lax.fori_loop(reach, shards, one, 0)

    def project(part):
        def one(step, _):
            done = jnp.dot(
                attended[pl.ds(part * half, half), :],
                held[0, step],
                preferred_element_type=jnp.float32,
            )
            acc[part, 0] = done
            held[1, step, pl.ds(part * half, half), :] = done.astype(jnp.bfloat16)
            return _

        lax.fori_loop(0, 4, one, 0)

    def sent_at(part, step, column):
        return held.at[1, step, pl.ds(part * half, half), column]

    def reduce_copy(src, dst, peer, sem):
        return pltpu.make_async_remote_copy(
            src_ref=src,
            dst_ref=dst,
            send_sem=near_send.at[sem],
            recv_sem=near_recv.at[sem],
            device_id={"rep": peer},
            device_id_type=MESH,
        )

    left, rest = pl.ds(0, side), pl.ds(side, side)

    def first_copies(part):
        return (
            reduce_copy(sent_at(part, 0, left), first_got.at[part, 0], right, 8 + 6 * part),
            reduce_copy(sent_at(part, 1, left), first_got.at[part, 1], right, 8 + 6 * part + 1),
            reduce_copy(sent_at(part, 0, rest), first_got.at[part, 2], over, 8 + 6 * part + 2),
            reduce_copy(sent_at(part, 2, rest), first_got.at[part, 3], over, 8 + 6 * part + 3),
        )

    def second_copies(part):
        return (
            reduce_copy(sent_at(part, 2, left), second_got.at[part, 0], over, 8 + 6 * part + 4),
            reduce_copy(sent_at(part, 1, rest), second_got.at[part, 1], right, 8 + 6 * part + 5),
        )

    def start(copies):
        for copy in copies:
            copy.start()

    def middle(part):
        for copy in first_copies(part):
            copy.wait_recv()
        for step, column, at in ((2, left, 0), (1, rest, 2)):
            mine_rows = pl.ds(part * half, half)
            held[1, step, mine_rows, column] = (
                held[1, step, mine_rows, column].astype(jnp.float32)
                + first_got[part, at].astype(jnp.float32)
            ).astype(jnp.bfloat16)
        start(second_copies(part))
        for column, at in ((left, 1), (rest, 3)):
            acc[part, 0, :, column] = acc[part, 0, :, column] + first_got[part, at].astype(jnp.float32)

    def mixed_copies(part):
        return [
            pltpu.make_async_remote_copy(
                src_ref=sums.at[2 + part, 0],
                dst_ref=sums.at[2 + part, at + 1],
                send_sem=sum_send.at[2 + part, at],
                recv_sem=sum_recv.at[2 + part, at],
                device_id={"rep": peer},
                device_id_type=MESH,
            )
            for at, peer in enumerate((right, over, cross))
        ]

    def total(part):
        for copy in second_copies(part):
            copy.wait_recv()
        squares = jnp.zeros((half, head), jnp.float32)
        for at in range(width // head):
            column = pl.ds(at * head, head)
            got = second_got[part, at * head // side, :, pl.ds(at * head % side, head)]
            rows_now = acc[part, 0, :, column] + got.astype(jnp.float32)
            acc[part, 0, :, column] = rows_now
            squares = squares + rows_now * rows_now
        sums[2 + part, 0] = turned_sums([jnp.sum(squares, axis=1, keepdims=True)])
        start(mixed_copies(part))

    def settle(part):
        for copy in mixed_copies(part):
            copy.wait()
        whole = sums[2 + part, 0] + sums[2 + part, 1] + sums[2 + part, 2] + sums[2 + part, 3]
        scales = lax.rsqrt(whole / full_width + EPSILON)
        scales = jnp.concatenate([scales] * (128 // 8), axis=0).T[:, 0:1]
        at = pl.ds(part * half, half)
        got[1, at, :] = (
            got[0, at, :].astype(jnp.float32) + acc[part, 0] * scales * post_gain[...]
        ).astype(jnp.bfloat16)

    def written(part):
        at = pl.ds(part * half, half)
        return pltpu.make_async_copy(got.at[1, at, :], out.at[at, :], out_sem.at[part])

    for step in range(4):
        load_out(step).start()
    for h in range(2):
        for copy in own_copies(h) + forwards(h):
            copy.wait_send()
    aim(hits, slot_rank[0:1, :])
    select(hits, value, picked.at[1])
    select(hits, turned.at[1], picked.at[0])
    wait_far(7)
    slot_order[...] = jnp.broadcast_to(order_of(shards + me), slot_order.shape)
    wait_far(6)
    aim(hits, order_of(me))
    select(hits, arrived, got.at[0])
    for kind in (0, 2, 4):
        wait_far(kind)
    lax.fori_loop(0, reach, pack, 0)
    attend_first(0)
    attend_first(1)
    for kind in (1, 3, 5):
        wait_far(kind)
    send_heads(0, 0, reach)
    send_heads(1, 0, reach)
    lax.fori_loop(reach, shards, pack, 0)
    attend_last(0)
    send_heads(0, reach, shards)
    attend_last(1)
    send_heads(1, reach, shards)
    send_far(11)
    for step in range(4):
        load_out(step).wait()
    wait_far(8)
    project(0)
    start(first_copies(0))
    wait_far(9)
    send_far(10)
    project(1)
    start(first_copies(1))
    middle(0)
    total(0)
    middle(1)
    settle(0)
    written(0).start()
    total(1)
    settle(1)
    written(1).start()
    wait_far(11)
    wait_far(10)
    for part in range(2):
        for copy in first_copies(part) + second_copies(part):
            copy.wait_send()
        written(part).wait()


def whole_heads(
    hidden_in, w_value, w_query, w_key, w_out, q_gain, k_gain, post_gain,
    frequency, deal, slots, lengths,
):
    rows, width = hidden_in.shape
    shards = deal.shape[0]
    full_width = w_query.shape[0]
    half = rows // 2
    head = HEAD_DIM
    reach = shards // 2
    inside = pl.BlockSpec(memory_space=pltpu.VMEM)
    outside = pl.BlockSpec(memory_space=pl.ANY)
    dma = pltpu.SemaphoreType.DMA
    return pl.pallas_call(
        functools.partial(whole_kernel, shards=shards, full_width=full_width),
        out_shape=(jax.ShapeDtypeStruct((rows, width), jnp.bfloat16),) * 3
        + (jax.ShapeDtypeStruct((8, rows), jnp.int32),),
        in_specs=[outside] * 5
        + [inside] * 6
        + [pl.BlockSpec(memory_space=pltpu.SMEM)],
        out_specs=(outside,) * 3 + (inside,),
        scratch_shapes=[
            pltpu.VMEM((rows, width), jnp.bfloat16),
            pltpu.VMEM((2 * shards, 128), jnp.int32),
            pltpu.VMEM((8, rows), jnp.int32),
            pltpu.VMEM((3, 4, width, width), jnp.bfloat16),
            pltpu.VMEM((3, rows, width), jnp.bfloat16),
            pltpu.VMEM((2, 3, half, width), jnp.float32),
            pltpu.VMEM((2, rows, width), jnp.bfloat16),
            pltpu.VMEM((rows, width), jnp.bfloat16),
            pltpu.VMEM((rows, head), jnp.float32),
            pltpu.VMEM((rows, head), jnp.float32),
            pltpu.VMEM((4, 4, 8, half), jnp.float32),
            pltpu.VMEM((2, rows, width), jnp.bfloat16),
            pltpu.VMEM((rows, rows), jnp.bfloat16),
            pltpu.VMEM((shards, rows, 2 * head), jnp.bfloat16),
            pltpu.VMEM((shards, rows, head), jnp.bfloat16),
            pltpu.VMEM((rows, width), jnp.bfloat16),
            pltpu.VMEM((shards, 2 * shards, 128), jnp.int32),
            pltpu.VMEM((shards * rows, head), jnp.bfloat16),
            pltpu.VMEM((shards * rows, head), jnp.bfloat16),
            pltpu.VMEM((head, shards * rows), jnp.bfloat16),
            pltpu.VMEM(((reach + 1) * rows, half), jnp.float32),
            pltpu.VMEM((2, shards, half, head), jnp.bfloat16),
            pltpu.VMEM((rows, width), jnp.bfloat16),
            pltpu.VMEM((2, 4, half, width // 2), jnp.bfloat16),
            pltpu.VMEM((2, 2, half, width // 2), jnp.bfloat16),
            dma((4, 4)),
            dma((20,)),
            dma((20,)),
            dma((4, 3)),
            dma((4, 3)),
            dma((12, shards - 1)),
            dma((12, shards - 1)),
            dma((12,)),
            dma((2,)),
        ],
        compiler_params=pltpu.CompilerParams(
            collective_id=1, has_side_effects=True, vmem_limit_bytes=60 << 20
        ),
        cost_estimate=pl.CostEstimate(
            flops=8 * rows * full_width * width + 20 * rows * rows * shards * head,
            bytes_accessed=8 * full_width * width + 16 * rows * width,
            transcendentals=5 * rows * rows * shards,
        ),
    )(
        hidden_in, w_value, w_query, w_key, w_out, q_gain, k_gain, post_gain,
        frequency, deal, slots, lengths,
    )


def place_kernel(
    order, rows_in, keys_in, values_in, rows_out, keys_out, values_out,
    hits, taken, placed, in_sem, out_sem,
):
    loads = [
        pltpu.make_async_copy(src, taken.at[at], in_sem.at[at])
        for at, src in enumerate((keys_in, values_in))
    ]
    stores = [
        pltpu.make_async_copy(placed.at[at], dst, out_sem.at[at])
        for at, dst in enumerate((keys_out, values_out))
    ]
    through = pltpu.make_async_copy(rows_in, rows_out, out_sem.at[2])
    for copy in loads:
        copy.start()
    through.start()
    aim(hits, order[0:1, :])
    for at in range(2):
        loads[at].wait()
        select(hits, taken.at[at], placed.at[at])
        stores[at].start()
    for copy in stores:
        copy.wait()
    through.wait()


def place_rows(order, result, keys_landed, values_landed):
    rows, width = result.shape
    inside = pl.BlockSpec(memory_space=pltpu.VMEM)
    outside = pl.BlockSpec(memory_space=pl.ANY)
    return pl.pallas_call(
        place_kernel,
        out_shape=(jax.ShapeDtypeStruct((rows, width), jnp.bfloat16),) * 3,
        in_specs=[inside] + [outside] * 3,
        out_specs=(outside,) * 3,
        scratch_shapes=[
            pltpu.VMEM((rows, rows), jnp.bfloat16),
            pltpu.VMEM((2, rows, width), jnp.bfloat16),
            pltpu.VMEM((2, rows, width), jnp.bfloat16),
            pltpu.SemaphoreType.DMA((2,)),
            pltpu.SemaphoreType.DMA((3,)),
        ],
        compiler_params=pltpu.CompilerParams(vmem_limit_bytes=60 << 20),
    )(order, result, keys_landed, values_landed)


def body_heads(
    hidden_in,
    w_query,
    w_key,
    w_value,
    w_out,
    q_gain,
    k_gain,
    post_gain,
    prompt_lengths,
    segment_ids,
    deal,
    inverse,
    slots,
):
    shards, rows = lax.axis_size("tok"), hidden_in.shape[0]
    half_size = HEAD_DIM // 2
    frequency = ROPE_BASE ** (-np.arange(half_size) * 2.0 / HEAD_DIM)
    frequency = np.concatenate([frequency, frequency]).astype(np.float32)
    result, keys_landed, values_landed, slot_order = whole_heads(
        hidden_in,
        w_value,
        w_query,
        w_key,
        w_out,
        q_gain[None, :],
        k_gain[None, :],
        post_gain[None, :],
        jnp.asarray(frequency[None, :]),
        deal.reshape(shards, rows),
        slots.reshape(shards, rows),
        prompt_lengths,
    )
    return place_rows(slot_order, result, keys_landed, values_landed)


def solution(mesh):
    def pick(*operands):
        rows, width = operands[0].shape
        shards = mesh.shape["tok"]
        fits = width == shards * HEAD_DIM and rows == shards * 64 and mesh.shape["rep"] == 4
        chosen = body_heads if fits else body
        return chosen(*operands)

    return jax.shard_map(
        pick,
        mesh=mesh,
        in_specs=(
            P("tok", "rep"),
            P(None, "rep"),
            P(None, "rep"),
            P(None, "rep"),
            P("rep", None),
            P("rep"),
            P("rep"),
            P("rep"),
            P(),
            P(),
            P(),
            P(),
            P(),
        ),
        out_specs=(P("tok", "rep"), P("tok", "rep"), P("tok", "rep")),
        check_vma=False,
    )
```

```python
import functools
import math

import jax
import jax.numpy as jnp
import numpy as np
from jax import lax
from jax.experimental import pallas as pl
from jax.experimental.pallas import tpu as pltpu
from jax.sharding import PartitionSpec as P

HEAD_DIM = 128


EPSILON = 1e-06
ROPE_BASE = 500000.0


def rotate(values, positions):
    half_size = values.shape[-1] // 2
    frequency = ROPE_BASE ** (-jnp.arange(half_size, dtype=jnp.float32) * 2.0 / values.shape[-1])
    angles = positions.astype(jnp.float32)[:, None] * frequency[None, :]
    cosine = jnp.cos(angles)[:, None, :]
    sine_part = jnp.sin(angles)[:, None, :]
    lower_half = values[..., :half_size]
    upper_half = values[..., half_size:]
    return jnp.concatenate(
        [
            lower_half * cosine - upper_half * sine_part,
            upper_half * cosine + lower_half * sine_part,
        ],
        axis=-1,
    )


def starts_of(lengths):
    index = jnp.arange(lengths.shape[0], dtype=jnp.int32)
    return jnp.sum(jnp.where(index[None, :] < index[:, None], lengths[None, :], 0), axis=1)


def bucketed(table_rows, row_order, shards):
    picked = table_rows[row_order]
    return picked.reshape(shards, picked.shape[0] // shards, picked.shape[1])


def placement_order(sources, shard_rows):
    local_ids = jnp.arange(sources.shape[0], dtype=jnp.int32)
    arrival = jnp.argsort(sources * shard_rows + local_ids)
    return jnp.argsort(arrival)


def body(
    hidden_in,
    w_query,
    w_key,
    w_value,
    w_out,
    q_gain,
    k_gain,
    post_gain,
    prompt_lengths,
    segment_ids,
    deal,
    inverse,
    slots,
):
    tok_rows, width_dev = hidden_in.shape
    full_width = w_query.shape[0]
    head_size = HEAD_DIM
    heads_dev = width_dev // head_size
    shards = lax.axis_size("tok")
    first_row = lax.axis_index("tok") * tok_rows
    my_packed = lax.dynamic_slice_in_dim(deal, first_row, tok_rows)
    my_segment = segment_ids[my_packed]
    prompt_ids = jnp.arange(prompt_lengths.shape[0], dtype=jnp.int32)
    prompt_starts = starts_of(prompt_lengths)
    my_start = jnp.sum(
        jnp.where(my_segment[:, None] == prompt_ids[None, :], prompt_starts[None, :], 0), axis=1
    )
    positions = my_packed - my_start
    pieces = lax.all_gather(hidden_in, "rep", axis=1, tiled=True)
    query_rows = jnp.dot(pieces, w_query, preferred_element_type=jnp.float32)
    key_rows = jnp.dot(pieces, w_key, preferred_element_type=jnp.float32)
    value_rows = jnp.dot(pieces, w_value, preferred_element_type=jnp.float32)
    query_sums, key_sums = lax.psum(
        (jnp.sum(query_rows * query_rows, axis=1), jnp.sum(key_rows * key_rows, axis=1)), "rep"
    )
    query_rows = (
        query_rows * lax.rsqrt(query_sums / full_width + EPSILON)[:, None] * q_gain[None, :]
    )
    key_rows = key_rows * lax.rsqrt(key_sums / full_width + EPSILON)[:, None] * k_gain[None, :]
    query_rot = rotate(query_rows.reshape(tok_rows, heads_dev, head_size), positions).astype(
        jnp.bfloat16
    )
    key_rot = (
        rotate(key_rows.reshape(tok_rows, heads_dev, head_size), positions)
        .astype(jnp.bfloat16)
        .reshape(tok_rows, width_dev)
    )
    value_half = value_rows.astype(jnp.bfloat16)
    scale = head_size ** (-0.5)

    def attend(state_now, key_block, value_block, key_packed):
        row_top, totals, weighted = state_now
        block_keys = key_block.reshape(key_block.shape[0], heads_dev, head_size)
        block_values = value_block.reshape(value_block.shape[0], heads_dev, head_size)
        key_segment = segment_ids[key_packed]
        allowed = (key_segment[None, :] == my_segment[:, None]) & (
            key_packed[None, :] <= my_packed[:, None]
        )
        scores = (
            jnp.einsum("qhd,khd->hqk", query_rot, block_keys, preferred_element_type=jnp.float32)
            * scale
        )
        masked = jnp.where(allowed[None], scores, -1e30)
        new_top = jnp.maximum(row_top, jnp.max(masked, axis=2))
        weights = jnp.where(allowed[None], jnp.exp(masked - new_top[:, :, None]), 0.0)
        factor = jnp.exp(row_top - new_top)
        totals = totals * factor + jnp.sum(weights, axis=2)
        weighted = weighted * factor[:, :, None] + jnp.einsum(
            "hqk,khd->hqd",
            weights.astype(jnp.bfloat16),
            block_values,
            preferred_element_type=jnp.float32,
        )
        return (new_top, totals, weighted)

    start_state = (
        jnp.full((heads_dev, tok_rows), -1e30, jnp.float32),
        jnp.zeros((heads_dev, tok_rows), jnp.float32),
        jnp.zeros((heads_dev, tok_rows, head_size), jnp.float32),
    )
    owned_rows = lax.dynamic_slice_in_dim(jnp.argsort(slots), first_row, tok_rows)
    my_slots = lax.dynamic_slice_in_dim(slots, first_row, tok_rows)
    slot_order = jnp.argsort(my_slots)
    sent_keys, sent_values = (
        lax.all_to_all(
            bucketed(key_rot, slot_order, shards), "tok", split_axis=0, concat_axis=0, tiled=True
        ),
        lax.all_to_all(
            bucketed(value_half, slot_order, shards), "tok", split_axis=0, concat_axis=0, tiled=True
        ),
    )
    arrival = placement_order(owned_rows // tok_rows, tok_rows)
    cache_keys = sent_keys.reshape(tok_rows, width_dev)[arrival]
    cache_values = sent_values.reshape(tok_rows, width_dev)[arrival]
    pieces = (
        lax.all_gather(key_rot, "tok", axis=0, tiled=True),
        lax.all_gather(value_half, "tok", axis=0, tiled=True),
    )
    key_all = pieces[0]
    block_size = math.gcd(key_all.shape[0], tok_rows)
    block_count = key_all.shape[0] // block_size

    def advance(state_in, block_set):
        return (attend(state_in, block_set[0], block_set[1], block_set[2]), None)

    state_out, _ = lax.scan(
        advance,
        start_state,
        (
            key_all.reshape(block_count, block_size, width_dev),
            pieces[1].reshape(block_count, block_size, width_dev),
            deal.reshape(block_count, block_size),
        ),
    )
    row_top, totals, weighted = state_out
    attended = (
        (weighted / totals[:, :, None])
        .transpose(1, 0, 2)
        .reshape(tok_rows, width_dev)
        .astype(jnp.bfloat16)
    )
    mixed_rows = (
        lax.psum_scatter(
            lax.dot_general(
                w_out, attended, (((0,), (1,)), ((), ())), preferred_element_type=jnp.float32
            ).astype(jnp.bfloat16),
            "rep",
            scatter_dimension=0,
            tiled=True,
        )
        .astype(jnp.float32)
        .T
    )
    mixed_sums = lax.psum(jnp.sum(mixed_rows * mixed_rows, axis=1), "rep")
    normed_rows = (
        mixed_rows * lax.rsqrt(mixed_sums / full_width + EPSILON)[:, None] * post_gain[None, :]
    )
    result_rows = (hidden_in.astype(jnp.float32) + normed_rows).astype(jnp.bfloat16)
    packed_order = jnp.argsort(my_packed)
    returned = lax.all_to_all(
        bucketed(result_rows, packed_order, shards), "tok", split_axis=0, concat_axis=0, tiled=True
    )
    my_dealt = lax.dynamic_slice_in_dim(inverse, first_row, tok_rows)
    output = returned.reshape(tok_rows, width_dev)[placement_order(my_dealt // tok_rows, tok_rows)]
    return (output, cache_keys, cache_values)


MESH = pl.DeviceIdType.MESH


def places():
    corner = lax.axis_index("rep")
    right = corner + 1 - 2 * (corner % 2)
    over = corner + 2 - 4 * (corner // 2)
    return corner, right, over, 3 - corner


def turned_sums(columns):
    rows = columns[0].shape[0]
    lane = lax.broadcasted_iota(jnp.int32, (rows, 128), 1)
    wide = jnp.zeros((rows, 128), jnp.float32)
    for at, column in enumerate(columns):
        wide = jnp.where(lane == at, column, wide)
    return wide.T[0:8, :]


def aim(hits, order):
    row = lax.broadcasted_iota(jnp.int32, hits.shape, 0)
    hits[...] = jnp.where(row == order, 1.0, 0.0).astype(jnp.bfloat16)


def select(hits, src, dst):
    dst[...] = jnp.dot(hits[...], src[...], preferred_element_type=jnp.float32).astype(
        jnp.bfloat16
    )


def whole_kernel(
    hidden_in, w_value, w_query, w_key, w_out, q_gain, k_gain, post_gain,
    frequency, deal, slots, lengths,
    out, keys_out, values_out, slot_order,
    piece, meta, slot_rank,
    held, got, acc, turned, value, cosine, sine, sums, picked, hits,
    qk_rows, v_rows, arrived, meta_got, queries, keys, values, scores, heads, attended,
    first_got, second_got,
    w_sem, near_send, near_recv, sum_send, sum_recv, far_send, far_recv, own_sem, out_sem,
    *, shards, full_width,
):
    rows, width = piece.shape
    half = rows // 2
    quarter = half // 2
    chunk = rows // shards
    head = HEAD_DIM
    me = lax.axis_index("tok")
    corner, right, over, cross = places()
    reach = shards // 2
    weights = (w_value, w_query, w_key)
    owners = (corner, right, over, cross)

    def load(which, step):
        return pltpu.make_async_copy(
            weights[which].at[pl.ds(pl.multiple_of(owners[step] * width, width), width), :],
            held.at[which, step],
            w_sem.at[which, step],
        )

    peers = [{"rep": peer} for peer in (right, over, cross)]
    peers += [{"tok": (me + 1 + d) % shards} for d in range(shards - 1)]
    barrier = pltpu.get_barrier_semaphore()
    for peer in peers:
        pl.semaphore_signal(barrier, inc=1, device_id=peer, device_id_type=MESH)

    fetch = pltpu.make_async_copy(hidden_in, value, out_sem.at[0])
    fetch.start()
    for step in range(4):
        for which in range(3):
            load(which, step).start()

    starts = [jnp.int32(0)]
    for prompt in range(lengths.shape[0] - 1):
        starts.append(starts[-1] + lengths[prompt])

    def begin_of(tokens):
        begin = jnp.zeros_like(tokens)
        for start in starts:
            start = start.astype(tokens.dtype)
            begin = jnp.where(tokens >= start, start, begin)
        return begin

    def upright(row):
        return jnp.broadcast_to(row, (128, rows)).T

    def ranks(row):
        below = jnp.where(upright(row)[:, 0:1] < row, 1.0, 0.0)
        return jnp.sum(below, axis=0, keepdims=True)

    def ordered(rank, row):
        place = lax.broadcasted_iota(jnp.int32, (rows, rows), 1).astype(jnp.float32)
        chosen = jnp.where(upright(rank)[:, 0:1] == place, upright(row)[:, 0:1], 0.0)
        return jnp.sum(chosen, axis=0, keepdims=True)

    my_packed = deal[pl.ds(me, 1), :].astype(jnp.float32)
    my_slots = slots[pl.ds(me, 1), :].astype(jnp.float32)
    rank = ranks(my_packed)
    aim(hits, rank.astype(jnp.int32))
    fetch.wait()
    select(hits, value, piece)
    def near(src, slot, at, size, peer, sem):
        return pltpu.make_async_remote_copy(
            src_ref=src.at[pl.ds(at, size), :],
            dst_ref=got.at[slot, pl.ds(at, size), :],
            send_sem=near_send.at[sem],
            recv_sem=near_recv.at[sem],
            device_id={"rep": peer},
            device_id_type=MESH,
        )

    def own_copies(h):
        return (
            near(piece, 0, h * half, half, right, 4 * h),
            near(piece, 1, h * half, half, over, 4 * h + 1),
        )

    def forwards(h):
        return (
            near(got.at[1], 2, h * half, quarter, right, 4 * h + 2),
            near(got.at[0], 2, h * half + quarter, quarter, over, 4 * h + 3),
        )

    def to_far(kind, d, src, dst):
        return pltpu.make_async_remote_copy(
            src_ref=src,
            dst_ref=dst,
            send_sem=far_send.at[kind, d],
            recv_sem=far_recv.at[kind, d],
            device_id={"tok": (me + 1 + d) % shards},
            device_id_type=MESH,
        )

    def head_of(ref, h, owner):
        return ref.at[pl.ds(h * half, half), pl.ds(pl.multiple_of(owner * head, head), head)]

    def source_of(kind, peer):
        if kind < 2:
            return head_of(value, kind, peer)
        if kind < 6:
            return head_of(turned.at[(kind - 2) // 2], kind % 2, peer)
        if kind == 7:
            return meta
        if kind < 10 and kind > 7:
            return heads.at[kind - 8, peer]
        source = piece if kind == 6 else picked.at[kind - 10]
        return source.at[pl.ds(pl.multiple_of(peer * chunk, chunk), chunk), :]

    def landing(kind):
        if kind < 2:
            return v_rows.at[me, pl.ds(kind * half, half), :]
        if kind < 6:
            return qk_rows.at[
                me, pl.ds((kind % 2) * half, half), pl.ds(((kind - 2) // 2) * head, head)
            ]
        if kind == 7:
            return meta_got.at[me]
        if kind < 10 and kind > 7:
            return attended.at[
                pl.ds((kind - 8) * half, half), pl.ds(pl.multiple_of(me * head, head), head)
            ]
        target = arrived if kind == 6 else (keys_out, values_out)[kind - 10]
        return target.at[pl.ds(pl.multiple_of(me * chunk, chunk), chunk), :]

    def own_copy(kind):
        return pltpu.make_async_copy(source_of(kind, me), landing(kind), own_sem.at[kind])

    def far_copy(kind, d):
        return to_far(kind, d, source_of(kind, (me + 1 + d) % shards), landing(kind))

    def send_far(kind):
        def one(d, _):
            far_copy(kind, d).start()
            return _

        lax.fori_loop(0, shards - 1, one, 0)
        own_copy(kind).start()

    def send_heads(part, low, high):
        def one(peer, _):
            @pl.when(peer != me)
            def _():
                far_copy(8 + part, (peer + shards - me - 1) % shards).start()

            @pl.when(peer == me)
            def _():
                own_copy(8 + part).start()

            return _

        def each(peer, _):
            one(peer, None)
            return _

        lax.fori_loop(low, high, each, 0)

    def wait_far(kind):
        def one(d, _):
            far_copy(kind, d).wait()
            return _

        lax.fori_loop(0, shards - 1, one, 0)
        own_copy(kind).wait()

    def product(h, step, low, high):
        left = piece if step == 0 else got.at[step - 1]

        def one(which, _):
            part = jnp.dot(
                left[pl.ds(h * half, half), :],
                held[which, step],
                preferred_element_type=jnp.float32,
            )
            if step > 0:
                part = part + acc[h, which]
            acc[h, which] = part
            return _

        lax.fori_loop(low, high, one, 0)

    def squared(h, which):
        total = jnp.zeros((half, head), jnp.float32)
        for at in range(width // head):
            part = acc[h, which, :, at * head : (at + 1) * head]
            total = total + part * part
        return jnp.sum(total, axis=1, keepdims=True)

    def sum_copy(h, at, peer):
        return pltpu.make_async_remote_copy(
            src_ref=sums.at[h, 0],
            dst_ref=sums.at[h, at + 1],
            send_sem=sum_send.at[h, at],
            recv_sem=sum_recv.at[h, at],
            device_id={"rep": peer},
            device_id_type=MESH,
        )

    def sum_copies(h):
        return [sum_copy(h, at, peer) for at, peer in enumerate((right, over, cross))]

    def rotate_half(h):
        total = sums[h, 0] + sums[h, 1] + sums[h, 2] + sums[h, 3]
        scales = lax.rsqrt(total / full_width + EPSILON)
        scales = jnp.concatenate([scales] * (128 // 8), axis=0).T
        mine = pl.ds(h * half, half)
        for which, gain in ((0, q_gain), (1, k_gain)):
            scale = scales[:, which : which + 1]

            def one(at, _):
                column = pl.ds(pl.multiple_of(at * head, head), head)
                normed = acc[h, which + 1, :, column] * scale * gain[:, column]
                other = pltpu.roll(normed, head // 2, 1)
                turned[which, mine, column] = (
                    normed * cosine[mine, :] + other * sine[mine, :]
                ).astype(jnp.bfloat16)
                return _

            lax.fori_loop(0, width // head, one, 0)

    def finish_value(h):
        value[pl.ds(h * half, half), :] = acc[h, 0].astype(jnp.bfloat16)

    pl.semaphore_wait(barrier, len(peers))
    for copy in own_copies(0):
        copy.start()
    send_far(6)
    sorted_packed = ordered(rank, my_packed)
    sorted_slots = ordered(rank, my_slots)
    rank = ranks(sorted_slots)
    slot_rank[...] = jnp.broadcast_to(rank.astype(jnp.int32), slot_rank.shape)
    lane = lax.broadcasted_iota(jnp.int32, (8, 128), 1)
    for first, row in ((0, sorted_packed), (shards, ordered(rank, sorted_slots))):
        for owner in range(shards):
            at = owner * chunk
            tile = jnp.broadcast_to(row[:, at // 128 * 128 : at // 128 * 128 + 128], (8, 128))
            tile = tile - owner * rows
            moved = pltpu.roll(tile, chunk, 1)
            tile = jnp.where(owner % 2 == me % 2, tile, moved)
            tile = jnp.where(lane // chunk == me % 2, tile, 0.0)
            meta[first + owner : first + owner + 1, :] = tile[0:1, :].astype(jnp.int32)
    send_far(7)
    angles = upright(sorted_packed - begin_of(sorted_packed)) * frequency[...]
    lane = lax.broadcasted_iota(jnp.int32, (rows, head), 1)
    cosine[...] = jnp.cos(angles)
    turn = jnp.sin(angles)
    sine[...] = jnp.where(lane < head // 2, -turn, turn)

    for which in range(3):
        load(which, 0).wait()
    product(0, 0, 0, 3)
    for h in range(2):
        if h == 1:
            product(1, 0, 0, 3)
            for copy in sum_copies(0):
                copy.wait()
            rotate_half(0)
            send_far(4)
            send_far(2)
        else:
            for copy in own_copies(0):
                copy.wait_recv()
            for copy in forwards(0):
                copy.start()
            for copy in own_copies(1):
                copy.start()
        for step in (1, 2):
            if h == 0:
                for which in range(3):
                    load(which, step).wait()
            product(h, step, 0, 3)
        for copy in forwards(h):
            copy.wait_recv()
        if h == 0:
            for which in range(3):
                load(which, 3).wait()
        product(h, 3, 0, 1)
        finish_value(h)
        send_far(h)
        product(h, 3, 1, 3)
        sums[h, 0] = turned_sums([squared(h, 1), squared(h, 2)])
        for copy in sum_copies(h):
            copy.start()
        if h == 0:
            for copy in own_copies(1):
                copy.wait_recv()
            for copy in forwards(1):
                copy.start()
    for copy in sum_copies(1):
        copy.wait()
    rotate_half(1)
    send_far(5)
    send_far(3)
    side = width // 2
    exits = (cross, right, over, corner)

    def load_out(step):
        return pltpu.make_async_copy(
            w_out.at[:, pl.ds(pl.multiple_of(exits[step] * width, width), width)],
            held.at[0, step],
            w_sem.at[3, step],
        )

    def order_of(row):
        per = 128 // chunk
        tiles = []
        for first in range(0, shards, per):
            tile = meta_got[first, pl.ds(row, 1), :]
            for more in range(1, per):
                tile = tile + meta_got[first + more, pl.ds(row, 1), :]
            tiles.append(tile)
        return jnp.concatenate(tiles, axis=1)

    def pack(block, _):
        aim(hits, order_of(block))
        at = pl.ds(pl.multiple_of(block * chunk, chunk), chunk)
        into = pl.ds(pl.multiple_of(block * rows, rows), rows)
        both = jnp.dot(
            hits[...],
            qk_rows[:, at, :].reshape(rows, 2 * head),
            preferred_element_type=jnp.float32,
        ).astype(jnp.bfloat16)
        queries[into, :] = both[:, :head]
        keys[into, :] = both[:, head:]
        values[:, into] = (
            jnp.dot(
                hits[...],
                v_rows[:, at, :].reshape(rows, head),
                preferred_element_type=jnp.float32,
            )
            .T.astype(jnp.bfloat16)
        )
        return _

    scale = head ** (-0.5) * math.log2(math.e)

    def attend(part, block, steps):
        depth = half * (part + 1)
        unrolled = isinstance(steps, int)

        def repeat(step, state):
            if not unrolled:
                return lax.fori_loop(0, steps, step, state)
            for at in range(steps):
                state = step(at, state)
            return state

        def folded(tile, fold):
            return fold(tile.reshape(tile.shape[0] // 8, 8, half), axis=0)

        query = queries[pl.ds(pl.multiple_of(block * rows + part * half, half), half), :]
        begin = begin_of(
            block * rows + part * half + lax.broadcasted_iota(jnp.int32, (1, half), 1)
        )

        def score(base, count):
            return lax.dot_general(
                keys[pl.ds(base, count), :],
                query,
                (((1,), (1,)), ((), ())),
                preferred_element_type=jnp.float32,
            )

        def earlier(step):
            return pl.multiple_of((block - 1 - step) * rows, rows)

        def stored(step):
            at = step * rows
            return pl.ds(at if unrolled else pl.multiple_of(at, rows), rows)

        base = pl.multiple_of(block * rows, rows)
        key_row = lax.broadcasted_iota(jnp.int32, (depth, half), 0)
        query_row = lax.broadcasted_iota(jnp.int32, (depth, half), 1) + part * half
        seen = (key_row >= begin - base) & (key_row <= query_row)
        last = jnp.where(seen, score(base, depth), -1e30)
        scores[reach * rows : reach * rows + depth, :] = last

        def first_pass(step, top):
            key_row = lax.broadcasted_iota(jnp.int32, (rows, half), 0)
            tile = jnp.where(
                key_row >= begin - earlier(step), score(earlier(step), rows), -1e30
            )
            scores[stored(step), :] = tile
            return jnp.maximum(top, folded(tile, jnp.max))

        top = repeat(first_pass, folded(last, jnp.max))
        top = jnp.max(top, axis=0, keepdims=True)

        def weigh(tile, base, count):
            weights = jnp.exp2((tile - top) * scale)
            return folded(weights, jnp.sum), jnp.dot(
                values[:, pl.ds(base, count)],
                weights.astype(jnp.bfloat16),
                preferred_element_type=jnp.float32,
            )

        def second_pass(step, state):
            total, weighted = weigh(scores[stored(step), :], earlier(step), rows)
            return state[0] + total, state[1] + weighted

        state = weigh(scores[reach * rows : reach * rows + depth, :], base, depth)
        total, weighted = repeat(second_pass, state)
        total = jnp.sum(total, axis=0, keepdims=True)
        heads[part, block] = (weighted / total).T.astype(jnp.bfloat16)

    def attend_first(part):
        def one(block, _):
            attend(part, block, block)
            return _

        lax.fori_loop(0, reach, one, 0)

    def attend_last(part):
        def one(block, _):
            attend(part, block, reach)
            send_heads(part, block, block + 1)
            return _

        lax.fori_loop(reach, shards, one, 0)

    def project(part):
        def one(step, _):
            done = jnp.dot(
                attended[pl.ds(part * half, half), :],
                held[0, step],
                preferred_element_type=jnp.float32,
            )
            acc[part, 0] = done
            held[1, step, pl.ds(part * half, half), :] = done.astype(jnp.bfloat16)
            return _

        lax.fori_loop(0, 4, one, 0)

    def sent_at(part, step, column):
        return held.at[1, step, pl.ds(part * half, half), column]

    def reduce_copy(src, dst, peer, sem):
        return pltpu.make_async_remote_copy(
            src_ref=src,
            dst_ref=dst,
            send_sem=near_send.at[sem],
            recv_sem=near_recv.at[sem],
            device_id={"rep": peer},
            device_id_type=MESH,
        )

    left, rest = pl.ds(0, side), pl.ds(side, side)

    def first_copies(part):
        return (
            reduce_copy(sent_at(part, 0, left), first_got.at[part, 0], right, 8 + 6 * part),
            reduce_copy(sent_at(part, 1, left), first_got.at[part, 1], right, 8 + 6 * part + 1),
            reduce_copy(sent_at(part, 0, rest), first_got.at[part, 2], over, 8 + 6 * part + 2),
            reduce_copy(sent_at(part, 2, rest), first_got.at[part, 3], over, 8 + 6 * part + 3),
        )

    def second_copies(part):
        return (
            reduce_copy(sent_at(part, 2, left), second_got.at[part, 0], over, 8 + 6 * part + 4),
            reduce_copy(sent_at(part, 1, rest), second_got.at[part, 1], right, 8 + 6 * part + 5),
        )

    def start(copies):
        for copy in copies:
            copy.start()

    def middle(part):
        for copy in first_copies(part):
            copy.wait_recv()
        for step, column, at in ((2, left, 0), (1, rest, 2)):
            mine_rows = pl.ds(part * half, half)
            held[1, step, mine_rows, column] = (
                held[1, step, mine_rows, column].astype(jnp.float32)
                + first_got[part, at].astype(jnp.float32)
            ).astype(jnp.bfloat16)
        start(second_copies(part))
        for column, at in ((left, 1), (rest, 3)):
            acc[part, 0, :, column] = acc[part, 0, :, column] + first_got[part, at].astype(jnp.float32)

    def mixed_copies(part):
        return [
            pltpu.make_async_remote_copy(
                src_ref=sums.at[2 + part, 0],
                dst_ref=sums.at[2 + part, at + 1],
                send_sem=sum_send.at[2 + part, at],
                recv_sem=sum_recv.at[2 + part, at],
                device_id={"rep": peer},
                device_id_type=MESH,
            )
            for at, peer in enumerate((right, over, cross))
        ]

    def total(part):
        for copy in second_copies(part):
            copy.wait_recv()
        squares = jnp.zeros((half, head), jnp.float32)
        for at in range(width // head):
            column = pl.ds(at * head, head)
            got = second_got[part, at * head // side, :, pl.ds(at * head % side, head)]
            rows_now = acc[part, 0, :, column] + got.astype(jnp.float32)
            acc[part, 0, :, column] = rows_now
            squares = squares + rows_now * rows_now
        sums[2 + part, 0] = turned_sums([jnp.sum(squares, axis=1, keepdims=True)])
        start(mixed_copies(part))

    def settle(part):
        for copy in mixed_copies(part):
            copy.wait()
        whole = sums[2 + part, 0] + sums[2 + part, 1] + sums[2 + part, 2] + sums[2 + part, 3]
        scales = lax.rsqrt(whole / full_width + EPSILON)
        scales = jnp.concatenate([scales] * (128 // 8), axis=0).T[:, 0:1]
        at = pl.ds(part * half, half)
        got[1, at, :] = (
            got[0, at, :].astype(jnp.float32) + acc[part, 0] * scales * post_gain[...]
        ).astype(jnp.bfloat16)

    def written(part):
        at = pl.ds(part * half, half)
        return pltpu.make_async_copy(got.at[1, at, :], out.at[at, :], out_sem.at[part])

    for step in range(4):
        load_out(step).start()
    for h in range(2):
        for copy in own_copies(h) + forwards(h):
            copy.wait_send()
    aim(hits, slot_rank[0:1, :])
    select(hits, value, picked.at[1])
    select(hits, turned.at[1], picked.at[0])
    wait_far(7)
    slot_order[...] = jnp.broadcast_to(order_of(shards + me), slot_order.shape)
    wait_far(6)
    aim(hits, order_of(me))
    select(hits, arrived, got.at[0])
    for kind in (0, 2, 4):
        wait_far(kind)
    lax.fori_loop(0, reach, pack, 0)
    attend_first(0)
    attend_first(1)
    for kind in (1, 3, 5):
        wait_far(kind)
    send_heads(0, 0, reach)
    send_heads(1, 0, reach)
    lax.fori_loop(reach, shards, pack, 0)
    attend_last(0)
    attend_last(1)
    send_far(11)
    for step in range(4):
        load_out(step).wait()
    wait_far(8)
    project(0)
    start(first_copies(0))
    wait_far(9)
    send_far(10)
    project(1)
    start(first_copies(1))
    middle(0)
    total(0)
    middle(1)
    settle(0)
    written(0).start()
    total(1)
    settle(1)
    written(1).start()
    wait_far(11)
    wait_far(10)
    for part in range(2):
        for copy in first_copies(part) + second_copies(part):
            copy.wait_send()
        written(part).wait()


def whole_heads(
    hidden_in, w_value, w_query, w_key, w_out, q_gain, k_gain, post_gain,
    frequency, deal, slots, lengths,
):
    rows, width = hidden_in.shape
    shards = deal.shape[0]
    full_width = w_query.shape[0]
    half = rows // 2
    head = HEAD_DIM
    reach = shards // 2
    inside = pl.BlockSpec(memory_space=pltpu.VMEM)
    outside = pl.BlockSpec(memory_space=pl.ANY)
    dma = pltpu.SemaphoreType.DMA
    return pl.pallas_call(
        functools.partial(whole_kernel, shards=shards, full_width=full_width),
        out_shape=(jax.ShapeDtypeStruct((rows, width), jnp.bfloat16),) * 3
        + (jax.ShapeDtypeStruct((8, rows), jnp.int32),),
        in_specs=[outside] * 5
        + [inside] * 6
        + [pl.BlockSpec(memory_space=pltpu.SMEM)],
        out_specs=(outside,) * 3 + (inside,),
        scratch_shapes=[
            pltpu.VMEM((rows, width), jnp.bfloat16),
            pltpu.VMEM((2 * shards, 128), jnp.int32),
            pltpu.VMEM((8, rows), jnp.int32),
            pltpu.VMEM((3, 4, width, width), jnp.bfloat16),
            pltpu.VMEM((3, rows, width), jnp.bfloat16),
            pltpu.VMEM((2, 3, half, width), jnp.float32),
            pltpu.VMEM((2, rows, width), jnp.bfloat16),
            pltpu.VMEM((rows, width), jnp.bfloat16),
            pltpu.VMEM((rows, head), jnp.float32),
            pltpu.VMEM((rows, head), jnp.float32),
            pltpu.VMEM((4, 4, 8, half), jnp.float32),
            pltpu.VMEM((2, rows, width), jnp.bfloat16),
            pltpu.VMEM((rows, rows), jnp.bfloat16),
            pltpu.VMEM((shards, rows, 2 * head), jnp.bfloat16),
            pltpu.VMEM((shards, rows, head), jnp.bfloat16),
            pltpu.VMEM((rows, width), jnp.bfloat16),
            pltpu.VMEM((shards, 2 * shards, 128), jnp.int32),
            pltpu.VMEM((shards * rows, head), jnp.bfloat16),
            pltpu.VMEM((shards * rows, head), jnp.bfloat16),
            pltpu.VMEM((head, shards * rows), jnp.bfloat16),
            pltpu.VMEM(((reach + 1) * rows, half), jnp.float32),
            pltpu.VMEM((2, shards, half, head), jnp.bfloat16),
            pltpu.VMEM((rows, width), jnp.bfloat16),
            pltpu.VMEM((2, 4, half, width // 2), jnp.bfloat16),
            pltpu.VMEM((2, 2, half, width // 2), jnp.bfloat16),
            dma((4, 4)),
            dma((20,)),
            dma((20,)),
            dma((4, 3)),
            dma((4, 3)),
            dma((12, shards - 1)),
            dma((12, shards - 1)),
            dma((12,)),
            dma((2,)),
        ],
        compiler_params=pltpu.CompilerParams(
            collective_id=1, has_side_effects=True, vmem_limit_bytes=60 << 20
        ),
        cost_estimate=pl.CostEstimate(
            flops=8 * rows * full_width * width + 20 * rows * rows * shards * head,
            bytes_accessed=8 * full_width * width + 16 * rows * width,
            transcendentals=5 * rows * rows * shards,
        ),
    )(
        hidden_in, w_value, w_query, w_key, w_out, q_gain, k_gain, post_gain,
        frequency, deal, slots, lengths,
    )


def place_kernel(
    order, rows_in, keys_in, values_in, rows_out, keys_out, values_out,
    hits, taken, placed, in_sem, out_sem,
):
    loads = [
        pltpu.make_async_copy(src, taken.at[at], in_sem.at[at])
        for at, src in enumerate((keys_in, values_in, rows_in))
    ]
    stores = [
        pltpu.make_async_copy(src, dst, out_sem.at[at])
        for at, (src, dst) in enumerate(
            ((placed.at[0], keys_out), (placed.at[1], values_out), (taken.at[2], rows_out))
        )
    ]
    for copy in loads:
        copy.start()
    aim(hits, order[0:1, :])
    for at in range(2):
        loads[at].wait()
        select(hits, taken.at[at], placed.at[at])
        stores[at].start()
    loads[2].wait()
    stores[2].start()
    for copy in stores:
        copy.wait()


def place_rows(order, result, keys_landed, values_landed):
    rows, width = result.shape
    inside = pl.BlockSpec(memory_space=pltpu.VMEM)
    outside = pl.BlockSpec(memory_space=pl.ANY)
    return pl.pallas_call(
        place_kernel,
        out_shape=(jax.ShapeDtypeStruct((rows, width), jnp.bfloat16),) * 3,
        in_specs=[inside] + [outside] * 3,
        out_specs=(outside,) * 3,
        scratch_shapes=[
            pltpu.VMEM((rows, rows), jnp.bfloat16),
            pltpu.VMEM((3, rows, width), jnp.bfloat16),
            pltpu.VMEM((2, rows, width), jnp.bfloat16),
            pltpu.SemaphoreType.DMA((3,)),
            pltpu.SemaphoreType.DMA((3,)),
        ],
        compiler_params=pltpu.CompilerParams(vmem_limit_bytes=60 << 20),
    )(order, result, keys_landed, values_landed)


def body_heads(
    hidden_in,
    w_query,
    w_key,
    w_value,
    w_out,
    q_gain,
    k_gain,
    post_gain,
    prompt_lengths,
    segment_ids,
    deal,
    inverse,
    slots,
):
    shards, rows = lax.axis_size("tok"), hidden_in.shape[0]
    half_size = HEAD_DIM // 2
    frequency = ROPE_BASE ** (-np.arange(half_size) * 2.0 / HEAD_DIM)
    frequency = np.concatenate([frequency, frequency]).astype(np.float32)
    result, keys_landed, values_landed, slot_order = whole_heads(
        hidden_in,
        w_value,
        w_query,
        w_key,
        w_out,
        q_gain[None, :],
        k_gain[None, :],
        post_gain[None, :],
        jnp.asarray(frequency[None, :]),
        deal.reshape(shards, rows),
        slots.reshape(shards, rows),
        prompt_lengths,
    )
    return place_rows(slot_order, result, keys_landed, values_landed)


def solution(mesh):
    def pick(*operands):
        rows, width = operands[0].shape
        shards = mesh.shape["tok"]
        fits = width == shards * HEAD_DIM and rows == shards * 64 and mesh.shape["rep"] == 4
        chosen = body_heads if fits else body
        return chosen(*operands)

    return jax.shard_map(
        pick,
        mesh=mesh,
        in_specs=(
            P("tok", "rep"),
            P(None, "rep"),
            P(None, "rep"),
            P(None, "rep"),
            P("rep", None),
            P("rep"),
            P("rep"),
            P("rep"),
            P(),
            P(),
            P(),
            P(),
            P(),
        ),
        out_specs=(P("tok", "rep"), P("tok", "rep"), P("tok", "rep")),
        check_vma=False,
    )
```

```python
import functools
import math

import jax
import jax.numpy as jnp
import numpy as np
from jax import lax
from jax.experimental import pallas as pl
from jax.experimental.pallas import tpu as pltpu
from jax.sharding import PartitionSpec as P

HEAD_DIM = 128


EPSILON = 1e-06
ROPE_BASE = 500000.0


def rotate(values, positions):
    half_size = values.shape[-1] // 2
    frequency = ROPE_BASE ** (-jnp.arange(half_size, dtype=jnp.float32) * 2.0 / values.shape[-1])
    angles = positions.astype(jnp.float32)[:, None] * frequency[None, :]
    cosine = jnp.cos(angles)[:, None, :]
    sine_part = jnp.sin(angles)[:, None, :]
    lower_half = values[..., :half_size]
    upper_half = values[..., half_size:]
    return jnp.concatenate(
        [
            lower_half * cosine - upper_half * sine_part,
            upper_half * cosine + lower_half * sine_part,
        ],
        axis=-1,
    )


def starts_of(lengths):
    index = jnp.arange(lengths.shape[0], dtype=jnp.int32)
    return jnp.sum(jnp.where(index[None, :] < index[:, None], lengths[None, :], 0), axis=1)


def bucketed(table_rows, row_order, shards):
    picked = table_rows[row_order]
    return picked.reshape(shards, picked.shape[0] // shards, picked.shape[1])


def placement_order(sources, shard_rows):
    local_ids = jnp.arange(sources.shape[0], dtype=jnp.int32)
    arrival = jnp.argsort(sources * shard_rows + local_ids)
    return jnp.argsort(arrival)


def body(
    hidden_in,
    w_query,
    w_key,
    w_value,
    w_out,
    q_gain,
    k_gain,
    post_gain,
    prompt_lengths,
    segment_ids,
    deal,
    inverse,
    slots,
):
    tok_rows, width_dev = hidden_in.shape
    full_width = w_query.shape[0]
    head_size = HEAD_DIM
    heads_dev = width_dev // head_size
    shards = lax.axis_size("tok")
    first_row = lax.axis_index("tok") * tok_rows
    my_packed = lax.dynamic_slice_in_dim(deal, first_row, tok_rows)
    my_segment = segment_ids[my_packed]
    prompt_ids = jnp.arange(prompt_lengths.shape[0], dtype=jnp.int32)
    prompt_starts = starts_of(prompt_lengths)
    my_start = jnp.sum(
        jnp.where(my_segment[:, None] == prompt_ids[None, :], prompt_starts[None, :], 0), axis=1
    )
    positions = my_packed - my_start
    pieces = lax.all_gather(hidden_in, "rep", axis=1, tiled=True)
    query_rows = jnp.dot(pieces, w_query, preferred_element_type=jnp.float32)
    key_rows = jnp.dot(pieces, w_key, preferred_element_type=jnp.float32)
    value_rows = jnp.dot(pieces, w_value, preferred_element_type=jnp.float32)
    query_sums, key_sums = lax.psum(
        (jnp.sum(query_rows * query_rows, axis=1), jnp.sum(key_rows * key_rows, axis=1)), "rep"
    )
    query_rows = (
        query_rows * lax.rsqrt(query_sums / full_width + EPSILON)[:, None] * q_gain[None, :]
    )
    key_rows = key_rows * lax.rsqrt(key_sums / full_width + EPSILON)[:, None] * k_gain[None, :]
    query_rot = rotate(query_rows.reshape(tok_rows, heads_dev, head_size), positions).astype(
        jnp.bfloat16
    )
    key_rot = (
        rotate(key_rows.reshape(tok_rows, heads_dev, head_size), positions)
        .astype(jnp.bfloat16)
        .reshape(tok_rows, width_dev)
    )
    value_half = value_rows.astype(jnp.bfloat16)
    scale = head_size ** (-0.5)

    def attend(state_now, key_block, value_block, key_packed):
        row_top, totals, weighted = state_now
        block_keys = key_block.reshape(key_block.shape[0], heads_dev, head_size)
        block_values = value_block.reshape(value_block.shape[0], heads_dev, head_size)
        key_segment = segment_ids[key_packed]
        allowed = (key_segment[None, :] == my_segment[:, None]) & (
            key_packed[None, :] <= my_packed[:, None]
        )
        scores = (
            jnp.einsum("qhd,khd->hqk", query_rot, block_keys, preferred_element_type=jnp.float32)
            * scale
        )
        masked = jnp.where(allowed[None], scores, -1e30)
        new_top = jnp.maximum(row_top, jnp.max(masked, axis=2))
        weights = jnp.where(allowed[None], jnp.exp(masked - new_top[:, :, None]), 0.0)
        factor = jnp.exp(row_top - new_top)
        totals = totals * factor + jnp.sum(weights, axis=2)
        weighted = weighted * factor[:, :, None] + jnp.einsum(
            "hqk,khd->hqd",
            weights.astype(jnp.bfloat16),
            block_values,
            preferred_element_type=jnp.float32,
        )
        return (new_top, totals, weighted)

    start_state = (
        jnp.full((heads_dev, tok_rows), -1e30, jnp.float32),
        jnp.zeros((heads_dev, tok_rows), jnp.float32),
        jnp.zeros((heads_dev, tok_rows, head_size), jnp.float32),
    )
    owned_rows = lax.dynamic_slice_in_dim(jnp.argsort(slots), first_row, tok_rows)
    my_slots = lax.dynamic_slice_in_dim(slots, first_row, tok_rows)
    slot_order = jnp.argsort(my_slots)
    sent_keys, sent_values = (
        lax.all_to_all(
            bucketed(key_rot, slot_order, shards), "tok", split_axis=0, concat_axis=0, tiled=True
        ),
        lax.all_to_all(
            bucketed(value_half, slot_order, shards), "tok", split_axis=0, concat_axis=0, tiled=True
        ),
    )
    arrival = placement_order(owned_rows // tok_rows, tok_rows)
    cache_keys = sent_keys.reshape(tok_rows, width_dev)[arrival]
    cache_values = sent_values.reshape(tok_rows, width_dev)[arrival]
    pieces = (
        lax.all_gather(key_rot, "tok", axis=0, tiled=True),
        lax.all_gather(value_half, "tok", axis=0, tiled=True),
    )
    key_all = pieces[0]
    block_size = math.gcd(key_all.shape[0], tok_rows)
    block_count = key_all.shape[0] // block_size

    def advance(state_in, block_set):
        return (attend(state_in, block_set[0], block_set[1], block_set[2]), None)

    state_out, _ = lax.scan(
        advance,
        start_state,
        (
            key_all.reshape(block_count, block_size, width_dev),
            pieces[1].reshape(block_count, block_size, width_dev),
            deal.reshape(block_count, block_size),
        ),
    )
    row_top, totals, weighted = state_out
    attended = (
        (weighted / totals[:, :, None])
        .transpose(1, 0, 2)
        .reshape(tok_rows, width_dev)
        .astype(jnp.bfloat16)
    )
    mixed_rows = (
        lax.psum_scatter(
            lax.dot_general(
                w_out, attended, (((0,), (1,)), ((), ())), preferred_element_type=jnp.float32
            ).astype(jnp.bfloat16),
            "rep",
            scatter_dimension=0,
            tiled=True,
        )
        .astype(jnp.float32)
        .T
    )
    mixed_sums = lax.psum(jnp.sum(mixed_rows * mixed_rows, axis=1), "rep")
    normed_rows = (
        mixed_rows * lax.rsqrt(mixed_sums / full_width + EPSILON)[:, None] * post_gain[None, :]
    )
    result_rows = (hidden_in.astype(jnp.float32) + normed_rows).astype(jnp.bfloat16)
    packed_order = jnp.argsort(my_packed)
    returned = lax.all_to_all(
        bucketed(result_rows, packed_order, shards), "tok", split_axis=0, concat_axis=0, tiled=True
    )
    my_dealt = lax.dynamic_slice_in_dim(inverse, first_row, tok_rows)
    output = returned.reshape(tok_rows, width_dev)[placement_order(my_dealt // tok_rows, tok_rows)]
    return (output, cache_keys, cache_values)


MESH = pl.DeviceIdType.MESH


def places():
    corner = lax.axis_index("rep")
    right = corner + 1 - 2 * (corner % 2)
    over = corner + 2 - 4 * (corner // 2)
    return corner, right, over, 3 - corner


def turned_sums(columns):
    rows = columns[0].shape[0]
    lane = lax.broadcasted_iota(jnp.int32, (rows, 128), 1)
    wide = jnp.zeros((rows, 128), jnp.float32)
    for at, column in enumerate(columns):
        wide = jnp.where(lane == at, column, wide)
    return wide.T[0:8, :]


def aim(hits, order):
    row = lax.broadcasted_iota(jnp.int32, hits.shape, 0)
    hits[...] = jnp.where(row == order, 1.0, 0.0).astype(jnp.bfloat16)


def select(hits, src, dst):
    dst[...] = jnp.dot(hits[...], src[...], preferred_element_type=jnp.float32).astype(
        jnp.bfloat16
    )


def whole_kernel(
    hidden_in, w_value, w_query, w_key, w_out, q_gain, k_gain, post_gain,
    frequency, deal, slots, lengths,
    out, keys_out, values_out, slot_order,
    piece, meta, slot_rank,
    held, got, acc, turned, value, cosine, sine, sums, picked, hits,
    qk_rows, v_rows, arrived, meta_got, queries, keys, values, scores, heads, attended,
    first_got, second_got,
    w_sem, near_send, near_recv, sum_send, sum_recv, far_send, far_recv, own_sem, out_sem,
    *, shards, full_width,
):
    rows, width = piece.shape
    half = rows // 2
    quarter = half // 2
    chunk = rows // shards
    head = HEAD_DIM
    me = lax.axis_index("tok")
    corner, right, over, cross = places()
    reach = shards // 2
    weights = (w_value, w_query, w_key)
    owners = (corner, right, over, cross)

    def load(which, step):
        return pltpu.make_async_copy(
            weights[which].at[pl.ds(pl.multiple_of(owners[step] * width, width), width), :],
            held.at[which, step],
            w_sem.at[which, step],
        )

    peers = [{"rep": peer} for peer in (right, over, cross)]
    peers += [{"tok": (me + 1 + d) % shards} for d in range(shards - 1)]
    barrier = pltpu.get_barrier_semaphore()
    for peer in peers:
        pl.semaphore_signal(barrier, inc=1, device_id=peer, device_id_type=MESH)

    fetch = pltpu.make_async_copy(hidden_in, value, out_sem.at[0])
    fetch.start()
    for step in range(4):
        for which in range(3):
            load(which, step).start()

    starts = [jnp.int32(0)]
    for prompt in range(lengths.shape[0] - 1):
        starts.append(starts[-1] + lengths[prompt])

    def begin_of(tokens):
        begin = jnp.zeros_like(tokens)
        for start in starts:
            start = start.astype(tokens.dtype)
            begin = jnp.where(tokens >= start, start, begin)
        return begin

    def upright(row):
        return jnp.broadcast_to(row, (128, rows)).T

    def ranks(row):
        below = jnp.where(upright(row)[:, 0:1] < row, 1.0, 0.0)
        return jnp.sum(below, axis=0, keepdims=True)

    def ordered(rank, row):
        place = lax.broadcasted_iota(jnp.int32, (rows, rows), 1).astype(jnp.float32)
        chosen = jnp.where(upright(rank)[:, 0:1] == place, upright(row)[:, 0:1], 0.0)
        return jnp.sum(chosen, axis=0, keepdims=True)

    def mine_of(table):
        tiles = rows // 128
        parts = [table[pl.ds(me * tiles + at, 1), :] for at in range(tiles)]
        return jnp.concatenate(parts, axis=1).astype(jnp.float32)

    my_packed, my_slots = mine_of(deal), mine_of(slots)
    rank = ranks(my_packed)
    aim(hits, rank.astype(jnp.int32))
    fetch.wait()
    select(hits, value, piece)
    def near(src, slot, at, size, peer, sem):
        return pltpu.make_async_remote_copy(
            src_ref=src.at[pl.ds(at, size), :],
            dst_ref=got.at[slot, pl.ds(at, size), :],
            send_sem=near_send.at[sem],
            recv_sem=near_recv.at[sem],
            device_id={"rep": peer},
            device_id_type=MESH,
        )

    def own_copies(h):
        return (
            near(piece, 0, h * half, half, right, 4 * h),
            near(piece, 1, h * half, half, over, 4 * h + 1),
        )

    def forwards(h):
        return (
            near(got.at[1], 2, h * half, quarter, right, 4 * h + 2),
            near(got.at[0], 2, h * half + quarter, quarter, over, 4 * h + 3),
        )

    def to_far(kind, d, src, dst):
        return pltpu.make_async_remote_copy(
            src_ref=src,
            dst_ref=dst,
            send_sem=far_send.at[kind, d],
            recv_sem=far_recv.at[kind, d],
            device_id={"tok": (me + 1 + d) % shards},
            device_id_type=MESH,
        )

    def head_of(ref, h, owner):
        return ref.at[pl.ds(h * half, half), pl.ds(pl.multiple_of(owner * head, head), head)]

    def source_of(kind, peer):
        if kind < 2:
            return head_of(value, kind, peer)
        if kind < 6:
            return head_of(turned.at[(kind - 2) // 2], kind % 2, peer)
        if kind == 7:
            return meta
        if kind < 10 and kind > 7:
            return heads.at[kind - 8, peer]
        source = piece if kind == 6 else picked.at[kind - 10]
        return source.at[pl.ds(pl.multiple_of(peer * chunk, chunk), chunk), :]

    def landing(kind):
        if kind < 2:
            return v_rows.at[me, pl.ds(kind * half, half), :]
        if kind < 6:
            return qk_rows.at[
                me, pl.ds((kind % 2) * half, half), pl.ds(((kind - 2) // 2) * head, head)
            ]
        if kind == 7:
            return meta_got.at[me]
        if kind < 10 and kind > 7:
            return attended.at[
                pl.ds((kind - 8) * half, half), pl.ds(pl.multiple_of(me * head, head), head)
            ]
        target = arrived if kind == 6 else (keys_out, values_out)[kind - 10]
        return target.at[pl.ds(pl.multiple_of(me * chunk, chunk), chunk), :]

    def own_copy(kind):
        return pltpu.make_async_copy(source_of(kind, me), landing(kind), own_sem.at[kind])

    def far_copy(kind, d):
        return to_far(kind, d, source_of(kind, (me + 1 + d) % shards), landing(kind))

    def send_far(kind):
        def one(d, _):
            far_copy(kind, d).start()
            return _

        lax.fori_loop(0, shards - 1, one, 0)
        own_copy(kind).start()

    def send_heads(part, low, high):
        def one(peer, _):
            @pl.when(peer != me)
            def _():
                far_copy(8 + part, (peer + shards - me - 1) % shards).start()

            @pl.when(peer == me)
            def _():
                own_copy(8 + part).start()

            return _

        def each(peer, _):
            one(peer, None)
            return _

        lax.fori_loop(low, high, each, 0)

    def wait_far(kind):
        def one(d, _):
            far_copy(kind, d).wait()
            return _

        lax.fori_loop(0, shards - 1, one, 0)
        own_copy(kind).wait()

    def product(h, step, low, high):
        left = piece if step == 0 else got.at[step - 1]

        def one(which, _):
            part = jnp.dot(
                left[pl.ds(h * half, half), :],
                held[which, step],
                preferred_element_type=jnp.float32,
            )
            if step > 0:
                part = part + acc[h, which]
            acc[h, which] = part
            return _

        lax.fori_loop(low, high, one, 0)

    def squared(h, which):
        total = jnp.zeros((half, head), jnp.float32)
        for at in range(width // head):
            part = acc[h, which, :, at * head : (at + 1) * head]
            total = total + part * part
        return jnp.sum(total, axis=1, keepdims=True)

    def sum_copy(h, at, peer):
        return pltpu.make_async_remote_copy(
            src_ref=sums.at[h, 0],
            dst_ref=sums.at[h, at + 1],
            send_sem=sum_send.at[h, at],
            recv_sem=sum_recv.at[h, at],
            device_id={"rep": peer},
            device_id_type=MESH,
        )

    def sum_copies(h):
        return [sum_copy(h, at, peer) for at, peer in enumerate((right, over, cross))]

    def rotate_half(h):
        total = sums[h, 0] + sums[h, 1] + sums[h, 2] + sums[h, 3]
        scales = lax.rsqrt(total / full_width + EPSILON)
        scales = jnp.concatenate([scales] * (128 // 8), axis=0).T
        mine = pl.ds(h * half, half)
        for which, gain in ((0, q_gain), (1, k_gain)):
            scale = scales[:, which : which + 1]

            def one(at, _):
                column = pl.ds(pl.multiple_of(at * head, head), head)
                normed = acc[h, which + 1, :, column] * scale * gain[:, column]
                other = pltpu.roll(normed, head // 2, 1)
                turned[which, mine, column] = (
                    normed * cosine[mine, :] + other * sine[mine, :]
                ).astype(jnp.bfloat16)
                return _

            lax.fori_loop(0, width // head, one, 0)

    def finish_value(h):
        value[pl.ds(h * half, half), :] = acc[h, 0].astype(jnp.bfloat16)

    pl.semaphore_wait(barrier, len(peers))
    for copy in own_copies(0):
        copy.start()
    send_far(6)
    sorted_packed = ordered(rank, my_packed)
    sorted_slots = ordered(rank, my_slots)
    rank = ranks(sorted_slots)
    slot_rank[...] = jnp.broadcast_to(rank.astype(jnp.int32), slot_rank.shape)
    lane = lax.broadcasted_iota(jnp.int32, (8, 128), 1)
    for first, row in ((0, sorted_packed), (shards, ordered(rank, sorted_slots))):
        for owner in range(shards):
            at = owner * chunk
            tile = jnp.broadcast_to(row[:, at // 128 * 128 : at // 128 * 128 + 128], (8, 128))
            tile = tile - owner * rows
            moved = pltpu.roll(tile, chunk, 1)
            tile = jnp.where(owner % 2 == me % 2, tile, moved)
            tile = jnp.where(lane // chunk == me % 2, tile, 0.0)
            meta[first + owner : first + owner + 1, :] = tile[0:1, :].astype(jnp.int32)
    send_far(7)
    angles = upright(sorted_packed - begin_of(sorted_packed)) * frequency[...]
    lane = lax.broadcasted_iota(jnp.int32, (rows, head), 1)
    cosine[...] = jnp.cos(angles)
    turn = jnp.sin(angles)
    sine[...] = jnp.where(lane < head // 2, -turn, turn)

    for which in range(3):
        load(which, 0).wait()
    product(0, 0, 0, 3)
    for h in range(2):
        if h == 1:
            product(1, 0, 0, 3)
            for copy in sum_copies(0):
                copy.wait()
            rotate_half(0)
            send_far(4)
            send_far(2)
        else:
            for copy in own_copies(0):
                copy.wait_recv()
            for copy in forwards(0):
                copy.start()
            for copy in own_copies(1):
                copy.start()
        for step in (1, 2):
            if h == 0:
                for which in range(3):
                    load(which, step).wait()
            product(h, step, 0, 3)
        for copy in forwards(h):
            copy.wait_recv()
        if h == 0:
            for which in range(3):
                load(which, 3).wait()
        product(h, 3, 0, 1)
        finish_value(h)
        send_far(h)
        product(h, 3, 1, 3)
        sums[h, 0] = turned_sums([squared(h, 1), squared(h, 2)])
        for copy in sum_copies(h):
            copy.start()
        if h == 0:
            for copy in own_copies(1):
                copy.wait_recv()
            for copy in forwards(1):
                copy.start()
    for copy in sum_copies(1):
        copy.wait()
    rotate_half(1)
    send_far(5)
    send_far(3)
    side = width // 2
    exits = (cross, right, over, corner)

    def load_out(step):
        return pltpu.make_async_copy(
            w_out.at[:, pl.ds(pl.multiple_of(exits[step] * width, width), width)],
            held.at[0, step],
            w_sem.at[3, step],
        )

    def order_of(row):
        per = 128 // chunk
        tiles = []
        for first in range(0, shards, per):
            tile = meta_got[first, pl.ds(row, 1), :]
            for more in range(1, per):
                tile = tile + meta_got[first + more, pl.ds(row, 1), :]
            tiles.append(tile)
        return jnp.concatenate(tiles, axis=1)

    def pack(block, _):
        aim(hits, order_of(block))
        at = pl.ds(pl.multiple_of(block * chunk, chunk), chunk)
        into = pl.ds(pl.multiple_of(block * rows, rows), rows)
        both = jnp.dot(
            hits[...],
            qk_rows[:, at, :].reshape(rows, 2 * head),
            preferred_element_type=jnp.float32,
        ).astype(jnp.bfloat16)
        queries[into, :] = both[:, :head]
        keys[into, :] = both[:, head:]
        values[:, into] = (
            jnp.dot(
                hits[...],
                v_rows[:, at, :].reshape(rows, head),
                preferred_element_type=jnp.float32,
            )
            .T.astype(jnp.bfloat16)
        )
        return _

    scale = head ** (-0.5) * math.log2(math.e)

    def attend(part, block, steps):
        depth = half * (part + 1)
        unrolled = isinstance(steps, int)

        def repeat(step, state):
            if not unrolled:
                return lax.fori_loop(0, steps, step, state)
            for at in range(steps):
                state = step(at, state)
            return state

        def folded(tile, fold):
            return fold(tile.reshape(tile.shape[0] // 8, 8, half), axis=0)

        query = queries[pl.ds(pl.multiple_of(block * rows + part * half, half), half), :]
        begin = begin_of(
            block * rows + part * half + lax.broadcasted_iota(jnp.int32, (1, half), 1)
        )

        def score(base, count):
            return lax.dot_general(
                keys[pl.ds(base, count), :],
                query,
                (((1,), (1,)), ((), ())),
                preferred_element_type=jnp.float32,
            )

        def earlier(step):
            return pl.multiple_of((block - 1 - step) * rows, rows)

        def stored(step):
            at = step * rows
            return pl.ds(at if unrolled else pl.multiple_of(at, rows), rows)

        base = pl.multiple_of(block * rows, rows)
        key_row = lax.broadcasted_iota(jnp.int32, (depth, half), 0)
        query_row = lax.broadcasted_iota(jnp.int32, (depth, half), 1) + part * half
        seen = (key_row >= begin - base) & (key_row <= query_row)
        last = jnp.where(seen, score(base, depth), -1e30)
        scores[reach * rows : reach * rows + depth, :] = last

        def first_pass(step, top):
            key_row = lax.broadcasted_iota(jnp.int32, (rows, half), 0)
            tile = jnp.where(
                key_row >= begin - earlier(step), score(earlier(step), rows), -1e30
            )
            scores[stored(step), :] = tile
            return jnp.maximum(top, folded(tile, jnp.max))

        top = repeat(first_pass, folded(last, jnp.max))
        top = jnp.max(top, axis=0, keepdims=True)

        def weigh(tile, base, count):
            weights = jnp.exp2((tile - top) * scale)
            return folded(weights, jnp.sum), jnp.dot(
                values[:, pl.ds(base, count)],
                weights.astype(jnp.bfloat16),
                preferred_element_type=jnp.float32,
            )

        def second_pass(step, state):
            total, weighted = weigh(scores[stored(step), :], earlier(step), rows)
            return state[0] + total, state[1] + weighted

        state = weigh(scores[reach * rows : reach * rows + depth, :], base, depth)
        total, weighted = repeat(second_pass, state)
        total = jnp.sum(total, axis=0, keepdims=True)
        heads[part, block] = (weighted / total).T.astype(jnp.bfloat16)

    def attend_first(part):
        def one(block, _):
            attend(part, block, block)
            return _

        lax.fori_loop(0, reach, one, 0)

    def attend_last(part, low, high):
        def one(block, _):
            attend(part, block, reach)
            send_heads(part, block, block + 1)
            return _

        lax.fori_loop(low, high, one, 0)

    def project(part):
        def one(step, _):
            done = jnp.dot(
                attended[pl.ds(part * half, half), :],
                held[0, step],
                preferred_element_type=jnp.float32,
            )
            acc[part, 0] = done
            held[1, step, pl.ds(part * half, half), :] = done.astype(jnp.bfloat16)
            return _

        lax.fori_loop(0, 4, one, 0)

    def sent_at(part, step, column):
        return held.at[1, step, pl.ds(part * half, half), column]

    def reduce_copy(src, dst, peer, sem):
        return pltpu.make_async_remote_copy(
            src_ref=src,
            dst_ref=dst,
            send_sem=near_send.at[sem],
            recv_sem=near_recv.at[sem],
            device_id={"rep": peer},
            device_id_type=MESH,
        )

    left, rest = pl.ds(0, side), pl.ds(side, side)

    def first_copies(part):
        return (
            reduce_copy(sent_at(part, 0, left), first_got.at[part, 0], right, 8 + 6 * part),
            reduce_copy(sent_at(part, 1, left), first_got.at[part, 1], right, 8 + 6 * part + 1),
            reduce_copy(sent_at(part, 0, rest), first_got.at[part, 2], over, 8 + 6 * part + 2),
            reduce_copy(sent_at(part, 2, rest), first_got.at[part, 3], over, 8 + 6 * part + 3),
        )

    def second_copies(part):
        return (
            reduce_copy(sent_at(part, 2, left), second_got.at[part, 0], over, 8 + 6 * part + 4),
            reduce_copy(sent_at(part, 1, rest), second_got.at[part, 1], right, 8 + 6 * part + 5),
        )

    def start(copies):
        for copy in copies:
            copy.start()

    def middle(part):
        for copy in first_copies(part):
            copy.wait_recv()
        for step, column, at in ((2, left, 0), (1, rest, 2)):
            mine_rows = pl.ds(part * half, half)
            held[1, step, mine_rows, column] = (
                held[1, step, mine_rows, column].astype(jnp.float32)
                + first_got[part, at].astype(jnp.float32)
            ).astype(jnp.bfloat16)
        start(second_copies(part))
        for column, at in ((left, 1), (rest, 3)):
            acc[part, 0, :, column] = acc[part, 0, :, column] + first_got[part, at].astype(jnp.float32)

    def mixed_copies(part):
        return [
            pltpu.make_async_remote_copy(
                src_ref=sums.at[2 + part, 0],
                dst_ref=sums.at[2 + part, at + 1],
                send_sem=sum_send.at[2 + part, at],
                recv_sem=sum_recv.at[2 + part, at],
                device_id={"rep": peer},
                device_id_type=MESH,
            )
            for at, peer in enumerate((right, over, cross))
        ]

    def total(part):
        for copy in second_copies(part):
            copy.wait_recv()
        squares = jnp.zeros((half, head), jnp.float32)
        for at in range(width // head):
            column = pl.ds(at * head, head)
            got = second_got[part, at * head // side, :, pl.ds(at * head % side, head)]
            rows_now = acc[part, 0, :, column] + got.astype(jnp.float32)
            acc[part, 0, :, column] = rows_now
            squares = squares + rows_now * rows_now
        sums[2 + part, 0] = turned_sums([jnp.sum(squares, axis=1, keepdims=True)])
        start(mixed_copies(part))

    def settle(part):
        for copy in mixed_copies(part):
            copy.wait()
        whole = sums[2 + part, 0] + sums[2 + part, 1] + sums[2 + part, 2] + sums[2 + part, 3]
        scales = lax.rsqrt(whole / full_width + EPSILON)
        scales = jnp.concatenate([scales] * (128 // 8), axis=0).T[:, 0:1]
        at = pl.ds(part * half, half)
        got[1, at, :] = (
            got[0, at, :].astype(jnp.float32) + acc[part, 0] * scales * post_gain[...]
        ).astype(jnp.bfloat16)

    def written(part):
        at = pl.ds(part * half, half)
        return pltpu.make_async_copy(got.at[1, at, :], out.at[at, :], out_sem.at[part])

    for step in range(4):
        load_out(step).start()
    for h in range(2):
        for copy in own_copies(h) + forwards(h):
            copy.wait_send()
    aim(hits, slot_rank[0:1, :])
    select(hits, value, picked.at[1])
    select(hits, turned.at[1], picked.at[0])
    wait_far(7)
    slot_order[...] = jnp.broadcast_to(order_of(shards + me), slot_order.shape)
    wait_far(6)
    aim(hits, order_of(me))
    select(hits, arrived, got.at[0])
    for kind in (0, 2, 4):
        wait_far(kind)
    lax.fori_loop(0, reach, pack, 0)
    attend_first(0)
    attend_first(1)
    for kind in (1, 3, 5):
        wait_far(kind)
    send_heads(0, 0, reach)
    send_heads(1, 0, reach)
    lax.fori_loop(reach, shards, pack, 0)
    for step in range(4):
        load_out(step).wait()
    attend_last(0, reach, shards)
    attend_last(1, reach, shards - 1)
    wait_far(8)
    project(0)
    start(first_copies(0))
    attend_last(1, shards - 1, shards)
    send_far(11)
    wait_far(9)
    send_far(10)
    project(1)
    start(first_copies(1))
    middle(0)
    middle(1)
    total(0)
    settle(0)
    written(0).start()
    total(1)
    settle(1)
    written(1).start()
    wait_far(11)
    wait_far(10)
    for part in range(2):
        for copy in first_copies(part) + second_copies(part):
            copy.wait_send()
        written(part).wait()


def whole_heads(
    hidden_in, w_value, w_query, w_key, w_out, q_gain, k_gain, post_gain,
    frequency, deal, slots, shards, lengths,
):
    rows, width = hidden_in.shape
    full_width = w_query.shape[0]
    half = rows // 2
    head = HEAD_DIM
    reach = shards // 2
    inside = pl.BlockSpec(memory_space=pltpu.VMEM)
    outside = pl.BlockSpec(memory_space=pl.ANY)
    dma = pltpu.SemaphoreType.DMA
    return pl.pallas_call(
        functools.partial(whole_kernel, shards=shards, full_width=full_width),
        out_shape=(jax.ShapeDtypeStruct((rows, width), jnp.bfloat16),) * 3
        + (jax.ShapeDtypeStruct((8, rows), jnp.int32),),
        in_specs=[outside] * 5
        + [inside] * 6
        + [pl.BlockSpec(memory_space=pltpu.SMEM)],
        out_specs=(outside,) * 3 + (inside,),
        scratch_shapes=[
            pltpu.VMEM((rows, width), jnp.bfloat16),
            pltpu.VMEM((2 * shards, 128), jnp.int32),
            pltpu.VMEM((8, rows), jnp.int32),
            pltpu.VMEM((3, 4, width, width), jnp.bfloat16),
            pltpu.VMEM((3, rows, width), jnp.bfloat16),
            pltpu.VMEM((2, 3, half, width), jnp.float32),
            pltpu.VMEM((2, rows, width), jnp.bfloat16),
            pltpu.VMEM((rows, width), jnp.bfloat16),
            pltpu.VMEM((rows, head), jnp.float32),
            pltpu.VMEM((rows, head), jnp.float32),
            pltpu.VMEM((4, 4, 8, half), jnp.float32),
            pltpu.VMEM((2, rows, width), jnp.bfloat16),
            pltpu.VMEM((rows, rows), jnp.bfloat16),
            pltpu.VMEM((shards, rows, 2 * head), jnp.bfloat16),
            pltpu.VMEM((shards, rows, head), jnp.bfloat16),
            pltpu.VMEM((rows, width), jnp.bfloat16),
            pltpu.VMEM((shards, 2 * shards, 128), jnp.int32),
            pltpu.VMEM((shards * rows, head), jnp.bfloat16),
            pltpu.VMEM((shards * rows, head), jnp.bfloat16),
            pltpu.VMEM((head, shards * rows), jnp.bfloat16),
            pltpu.VMEM(((reach + 1) * rows, half), jnp.float32),
            pltpu.VMEM((2, shards, half, head), jnp.bfloat16),
            pltpu.VMEM((rows, width), jnp.bfloat16),
            pltpu.VMEM((2, 4, half, width // 2), jnp.bfloat16),
            pltpu.VMEM((2, 2, half, width // 2), jnp.bfloat16),
            dma((4, 4)),
            dma((20,)),
            dma((20,)),
            dma((4, 3)),
            dma((4, 3)),
            dma((12, shards - 1)),
            dma((12, shards - 1)),
            dma((12,)),
            dma((2,)),
        ],
        compiler_params=pltpu.CompilerParams(
            collective_id=1, has_side_effects=True, vmem_limit_bytes=60 << 20
        ),
        cost_estimate=pl.CostEstimate(
            flops=8 * rows * full_width * width + 20 * rows * rows * shards * head,
            bytes_accessed=8 * full_width * width + 16 * rows * width,
            transcendentals=5 * rows * rows * shards,
        ),
    )(
        hidden_in, w_value, w_query, w_key, w_out, q_gain, k_gain, post_gain,
        frequency, deal, slots, lengths,
    )


def place_kernel(
    order, rows_in, keys_in, values_in, rows_out, keys_out, values_out,
    hits, taken, placed, in_sem, out_sem,
):
    side = taken.shape[2] // 2
    pieces = [(at, pl.ds(half * side, side)) for at in range(2) for half in range(2)]
    arrays = ((keys_in, keys_out), (values_in, values_out))
    loads = [
        pltpu.make_async_copy(arrays[at][0].at[:, to], taken.at[at, :, to], in_sem.at[n])
        for n, (at, to) in enumerate(pieces)
    ]
    stores = [
        pltpu.make_async_copy(placed.at[at, :, to], arrays[at][1].at[:, to], out_sem.at[n])
        for n, (at, to) in enumerate(pieces)
    ]
    load_rows = pltpu.make_async_copy(rows_in, taken.at[2], in_sem.at[4])
    store_rows = pltpu.make_async_copy(taken.at[2], rows_out, out_sem.at[4])
    for copy in loads + [load_rows]:
        copy.start()
    aim(hits, order[0:1, :])
    for n, (at, to) in enumerate(pieces):
        loads[n].wait()
        select(hits, taken.at[at, :, to], placed.at[at, :, to])
        stores[n].start()
        if n == 2:
            load_rows.wait()
            store_rows.start()
    for copy in stores + [store_rows]:
        copy.wait()


def place_rows(order, result, keys_landed, values_landed):
    rows, width = result.shape
    inside = pl.BlockSpec(memory_space=pltpu.VMEM)
    outside = pl.BlockSpec(memory_space=pl.ANY)
    return pl.pallas_call(
        place_kernel,
        out_shape=(jax.ShapeDtypeStruct((rows, width), jnp.bfloat16),) * 3,
        in_specs=[inside] + [outside] * 3,
        out_specs=(outside,) * 3,
        scratch_shapes=[
            pltpu.VMEM((rows, rows), jnp.bfloat16),
            pltpu.VMEM((3, rows, width), jnp.bfloat16),
            pltpu.VMEM((2, rows, width), jnp.bfloat16),
            pltpu.SemaphoreType.DMA((5,)),
            pltpu.SemaphoreType.DMA((5,)),
        ],
        compiler_params=pltpu.CompilerParams(vmem_limit_bytes=60 << 20),
    )(order, result, keys_landed, values_landed)


def body_heads(
    hidden_in,
    w_query,
    w_key,
    w_value,
    w_out,
    q_gain,
    k_gain,
    post_gain,
    prompt_lengths,
    segment_ids,
    deal,
    inverse,
    slots,
):
    shards, rows = lax.axis_size("tok"), hidden_in.shape[0]
    half_size = HEAD_DIM // 2
    frequency = ROPE_BASE ** (-np.arange(half_size) * 2.0 / HEAD_DIM)
    frequency = np.concatenate([frequency, frequency]).astype(np.float32)
    result, keys_landed, values_landed, slot_order = whole_heads(
        hidden_in,
        w_value,
        w_query,
        w_key,
        w_out,
        q_gain[None, :],
        k_gain[None, :],
        post_gain[None, :],
        jnp.asarray(frequency[None, :]),
        deal.reshape(shards * rows // 128, 128),
        slots.reshape(shards * rows // 128, 128),
        shards,
        prompt_lengths,
    )
    return place_rows(slot_order, result, keys_landed, values_landed)


def solution(mesh):
    def pick(*operands):
        rows, width = operands[0].shape
        shards = mesh.shape["tok"]
        fits = width == shards * HEAD_DIM and rows == shards * 64 and mesh.shape["rep"] == 4
        chosen = body_heads if fits else body
        return chosen(*operands)

    return jax.shard_map(
        pick,
        mesh=mesh,
        in_specs=(
            P("tok", "rep"),
            P(None, "rep"),
            P(None, "rep"),
            P(None, "rep"),
            P("rep", None),
            P("rep"),
            P("rep"),
            P("rep"),
            P(),
            P(),
            P(),
            P(),
            P(),
        ),
        out_specs=(P("tok", "rep"), P("tok", "rep"), P("tok", "rep")),
        check_vma=False,
    )
```

```python
import functools
import math

import jax
import jax.numpy as jnp
import numpy as np
from jax import lax
from jax.experimental import pallas as pl
from jax.experimental.pallas import tpu as pltpu
from jax.sharding import PartitionSpec as P

HEAD_DIM = 128


EPSILON = 1e-06
ROPE_BASE = 500000.0


def rotate(values, positions):
    half_size = values.shape[-1] // 2
    frequency = ROPE_BASE ** (-jnp.arange(half_size, dtype=jnp.float32) * 2.0 / values.shape[-1])
    angles = positions.astype(jnp.float32)[:, None] * frequency[None, :]
    cosine = jnp.cos(angles)[:, None, :]
    sine_part = jnp.sin(angles)[:, None, :]
    lower_half = values[..., :half_size]
    upper_half = values[..., half_size:]
    return jnp.concatenate(
        [
            lower_half * cosine - upper_half * sine_part,
            upper_half * cosine + lower_half * sine_part,
        ],
        axis=-1,
    )


def starts_of(lengths):
    index = jnp.arange(lengths.shape[0], dtype=jnp.int32)
    return jnp.sum(jnp.where(index[None, :] < index[:, None], lengths[None, :], 0), axis=1)


def bucketed(table_rows, row_order, shards):
    picked = table_rows[row_order]
    return picked.reshape(shards, picked.shape[0] // shards, picked.shape[1])


def placement_order(sources, shard_rows):
    local_ids = jnp.arange(sources.shape[0], dtype=jnp.int32)
    arrival = jnp.argsort(sources * shard_rows + local_ids)
    return jnp.argsort(arrival)


def body(
    hidden_in,
    w_query,
    w_key,
    w_value,
    w_out,
    q_gain,
    k_gain,
    post_gain,
    prompt_lengths,
    segment_ids,
    deal,
    inverse,
    slots,
):
    tok_rows, width_dev = hidden_in.shape
    full_width = w_query.shape[0]
    head_size = HEAD_DIM
    heads_dev = width_dev // head_size
    shards = lax.axis_size("tok")
    first_row = lax.axis_index("tok") * tok_rows
    my_packed = lax.dynamic_slice_in_dim(deal, first_row, tok_rows)
    my_segment = segment_ids[my_packed]
    prompt_ids = jnp.arange(prompt_lengths.shape[0], dtype=jnp.int32)
    prompt_starts = starts_of(prompt_lengths)
    my_start = jnp.sum(
        jnp.where(my_segment[:, None] == prompt_ids[None, :], prompt_starts[None, :], 0), axis=1
    )
    positions = my_packed - my_start
    pieces = lax.all_gather(hidden_in, "rep", axis=1, tiled=True)
    query_rows = jnp.dot(pieces, w_query, preferred_element_type=jnp.float32)
    key_rows = jnp.dot(pieces, w_key, preferred_element_type=jnp.float32)
    value_rows = jnp.dot(pieces, w_value, preferred_element_type=jnp.float32)
    query_sums, key_sums = lax.psum(
        (jnp.sum(query_rows * query_rows, axis=1), jnp.sum(key_rows * key_rows, axis=1)), "rep"
    )
    query_rows = (
        query_rows * lax.rsqrt(query_sums / full_width + EPSILON)[:, None] * q_gain[None, :]
    )
    key_rows = key_rows * lax.rsqrt(key_sums / full_width + EPSILON)[:, None] * k_gain[None, :]
    query_rot = rotate(query_rows.reshape(tok_rows, heads_dev, head_size), positions).astype(
        jnp.bfloat16
    )
    key_rot = (
        rotate(key_rows.reshape(tok_rows, heads_dev, head_size), positions)
        .astype(jnp.bfloat16)
        .reshape(tok_rows, width_dev)
    )
    value_half = value_rows.astype(jnp.bfloat16)
    scale = head_size ** (-0.5)

    def attend(state_now, key_block, value_block, key_packed):
        row_top, totals, weighted = state_now
        block_keys = key_block.reshape(key_block.shape[0], heads_dev, head_size)
        block_values = value_block.reshape(value_block.shape[0], heads_dev, head_size)
        key_segment = segment_ids[key_packed]
        allowed = (key_segment[None, :] == my_segment[:, None]) & (
            key_packed[None, :] <= my_packed[:, None]
        )
        scores = (
            jnp.einsum("qhd,khd->hqk", query_rot, block_keys, preferred_element_type=jnp.float32)
            * scale
        )
        masked = jnp.where(allowed[None], scores, -1e30)
        new_top = jnp.maximum(row_top, jnp.max(masked, axis=2))
        weights = jnp.where(allowed[None], jnp.exp(masked - new_top[:, :, None]), 0.0)
        factor = jnp.exp(row_top - new_top)
        totals = totals * factor + jnp.sum(weights, axis=2)
        weighted = weighted * factor[:, :, None] + jnp.einsum(
            "hqk,khd->hqd",
            weights.astype(jnp.bfloat16),
            block_values,
            preferred_element_type=jnp.float32,
        )
        return (new_top, totals, weighted)

    start_state = (
        jnp.full((heads_dev, tok_rows), -1e30, jnp.float32),
        jnp.zeros((heads_dev, tok_rows), jnp.float32),
        jnp.zeros((heads_dev, tok_rows, head_size), jnp.float32),
    )
    owned_rows = lax.dynamic_slice_in_dim(jnp.argsort(slots), first_row, tok_rows)
    my_slots = lax.dynamic_slice_in_dim(slots, first_row, tok_rows)
    slot_order = jnp.argsort(my_slots)
    sent_keys, sent_values = (
        lax.all_to_all(
            bucketed(key_rot, slot_order, shards), "tok", split_axis=0, concat_axis=0, tiled=True
        ),
        lax.all_to_all(
            bucketed(value_half, slot_order, shards), "tok", split_axis=0, concat_axis=0, tiled=True
        ),
    )
    arrival = placement_order(owned_rows // tok_rows, tok_rows)
    cache_keys = sent_keys.reshape(tok_rows, width_dev)[arrival]
    cache_values = sent_values.reshape(tok_rows, width_dev)[arrival]
    pieces = (
        lax.all_gather(key_rot, "tok", axis=0, tiled=True),
        lax.all_gather(value_half, "tok", axis=0, tiled=True),
    )
    key_all = pieces[0]
    block_size = math.gcd(key_all.shape[0], tok_rows)
    block_count = key_all.shape[0] // block_size

    def advance(state_in, block_set):
        return (attend(state_in, block_set[0], block_set[1], block_set[2]), None)

    state_out, _ = lax.scan(
        advance,
        start_state,
        (
            key_all.reshape(block_count, block_size, width_dev),
            pieces[1].reshape(block_count, block_size, width_dev),
            deal.reshape(block_count, block_size),
        ),
    )
    row_top, totals, weighted = state_out
    attended = (
        (weighted / totals[:, :, None])
        .transpose(1, 0, 2)
        .reshape(tok_rows, width_dev)
        .astype(jnp.bfloat16)
    )
    mixed_rows = (
        lax.psum_scatter(
            lax.dot_general(
                w_out, attended, (((0,), (1,)), ((), ())), preferred_element_type=jnp.float32
            ).astype(jnp.bfloat16),
            "rep",
            scatter_dimension=0,
            tiled=True,
        )
        .astype(jnp.float32)
        .T
    )
    mixed_sums = lax.psum(jnp.sum(mixed_rows * mixed_rows, axis=1), "rep")
    normed_rows = (
        mixed_rows * lax.rsqrt(mixed_sums / full_width + EPSILON)[:, None] * post_gain[None, :]
    )
    result_rows = (hidden_in.astype(jnp.float32) + normed_rows).astype(jnp.bfloat16)
    packed_order = jnp.argsort(my_packed)
    returned = lax.all_to_all(
        bucketed(result_rows, packed_order, shards), "tok", split_axis=0, concat_axis=0, tiled=True
    )
    my_dealt = lax.dynamic_slice_in_dim(inverse, first_row, tok_rows)
    output = returned.reshape(tok_rows, width_dev)[placement_order(my_dealt // tok_rows, tok_rows)]
    return (output, cache_keys, cache_values)


MESH = pl.DeviceIdType.MESH


def places():
    corner = lax.axis_index("rep")
    right = corner + 1 - 2 * (corner % 2)
    over = corner + 2 - 4 * (corner // 2)
    return corner, right, over, 3 - corner


def turned_sums(columns):
    rows = columns[0].shape[0]
    lane = lax.broadcasted_iota(jnp.int32, (rows, 128), 1)
    wide = jnp.zeros((rows, 128), jnp.float32)
    for at, column in enumerate(columns):
        wide = jnp.where(lane == at, column, wide)
    return wide.T[0:8, :]


def aim(hits, order):
    row = lax.broadcasted_iota(jnp.int32, hits.shape, 0)
    hits[...] = jnp.where(row == order, 1.0, 0.0).astype(jnp.bfloat16)


def select(hits, src, dst):
    dst[...] = jnp.dot(hits[...], src[...], preferred_element_type=jnp.float32).astype(
        jnp.bfloat16
    )


def whole_kernel(
    hidden_in, w_value, w_query, w_key, w_out, q_gain, k_gain, post_gain,
    frequency, deal, slots, lengths,
    out, keys_out, values_out, slot_order,
    piece, meta, slot_rank,
    held, got, acc, turned, value, cosine, sine, sums, picked, hits,
    qk_rows, v_rows, arrived, meta_got, queries, keys, values, scores, heads, attended,
    first_got, second_got,
    w_sem, near_send, near_recv, sum_send, sum_recv, far_send, far_recv, own_sem, out_sem,
    *, shards, full_width,
):
    rows, width = piece.shape
    half = rows // 2
    quarter = half // 2
    chunk = rows // shards
    head = HEAD_DIM
    me = lax.axis_index("tok")
    corner, right, over, cross = places()
    reach = shards // 2
    weights = (w_value, w_query, w_key)
    owners = (corner, right, over, cross)

    def load(which, step):
        return pltpu.make_async_copy(
            weights[which].at[pl.ds(pl.multiple_of(owners[step] * width, width), width), :],
            held.at[which, step],
            w_sem.at[which, step],
        )

    peers = [{"rep": peer} for peer in (right, over, cross)]
    peers += [{"tok": (me + 1 + d) % shards} for d in range(shards - 1)]
    barrier = pltpu.get_barrier_semaphore()
    for peer in peers:
        pl.semaphore_signal(barrier, inc=1, device_id=peer, device_id_type=MESH)

    fetch = pltpu.make_async_copy(hidden_in, value, out_sem.at[0])
    fetch.start()
    for step in range(4):
        for which in range(3):
            load(which, step).start()

    starts = [jnp.int32(0)]
    for prompt in range(lengths.shape[0] - 1):
        starts.append(starts[-1] + lengths[prompt])

    def begin_of(tokens):
        begin = jnp.zeros_like(tokens)
        for start in starts:
            start = start.astype(tokens.dtype)
            begin = jnp.where(tokens >= start, start, begin)
        return begin

    def upright(row):
        return jnp.broadcast_to(row, (128, rows)).T

    def ranks(row):
        below = jnp.where(upright(row)[:, 0:1] < row, 1.0, 0.0)
        return jnp.sum(below, axis=0, keepdims=True)

    def ordered(rank, row):
        place = lax.broadcasted_iota(jnp.int32, (rows, rows), 1).astype(jnp.float32)
        chosen = jnp.where(upright(rank)[:, 0:1] == place, upright(row)[:, 0:1], 0.0)
        return jnp.sum(chosen, axis=0, keepdims=True)

    def mine_of(table):
        tiles = rows // 128
        parts = [table[pl.ds(me * tiles + at, 1), :] for at in range(tiles)]
        return jnp.concatenate(parts, axis=1).astype(jnp.float32)

    my_packed, my_slots = mine_of(deal), mine_of(slots)
    rank = ranks(my_packed)
    aim(hits, rank.astype(jnp.int32))
    fetch.wait()
    select(hits, value, piece)
    def near(src, slot, at, size, peer, sem):
        return pltpu.make_async_remote_copy(
            src_ref=src.at[pl.ds(at, size), :],
            dst_ref=got.at[slot, pl.ds(at, size), :],
            send_sem=near_send.at[sem],
            recv_sem=near_recv.at[sem],
            device_id={"rep": peer},
            device_id_type=MESH,
        )

    def own_copies(h):
        return (
            near(piece, 0, h * half, half, right, 4 * h),
            near(piece, 1, h * half, half, over, 4 * h + 1),
        )

    def forwards(h):
        return (
            near(got.at[1], 2, h * half, quarter, right, 4 * h + 2),
            near(got.at[0], 2, h * half + quarter, quarter, over, 4 * h + 3),
        )

    def to_far(kind, d, src, dst):
        return pltpu.make_async_remote_copy(
            src_ref=src,
            dst_ref=dst,
            send_sem=far_send.at[kind, d],
            recv_sem=far_recv.at[kind, d],
            device_id={"tok": (me + 1 + d) % shards},
            device_id_type=MESH,
        )

    def head_of(ref, h, owner):
        return ref.at[pl.ds(h * half, half), pl.ds(pl.multiple_of(owner * head, head), head)]

    def source_of(kind, peer):
        if kind < 2:
            return head_of(value, kind, peer)
        if kind < 6:
            return head_of(turned.at[(kind - 2) // 2], kind % 2, peer)
        if kind == 7:
            return meta
        if kind < 10 and kind > 7:
            return heads.at[kind - 8, peer]
        source = piece if kind == 6 else picked.at[kind - 10]
        return source.at[pl.ds(pl.multiple_of(peer * chunk, chunk), chunk), :]

    def landing(kind):
        if kind < 2:
            return v_rows.at[me, pl.ds(kind * half, half), :]
        if kind < 6:
            return qk_rows.at[
                me, pl.ds((kind % 2) * half, half), pl.ds(((kind - 2) // 2) * head, head)
            ]
        if kind == 7:
            return meta_got.at[me]
        if kind < 10 and kind > 7:
            return attended.at[
                pl.ds((kind - 8) * half, half), pl.ds(pl.multiple_of(me * head, head), head)
            ]
        target = arrived if kind == 6 else (keys_out, values_out)[kind - 10]
        return target.at[pl.ds(pl.multiple_of(me * chunk, chunk), chunk), :]

    def own_copy(kind):
        return pltpu.make_async_copy(source_of(kind, me), landing(kind), own_sem.at[kind])

    def far_copy(kind, d):
        return to_far(kind, d, source_of(kind, (me + 1 + d) % shards), landing(kind))

    def send_far(kind):
        def one(d, _):
            far_copy(kind, d).start()
            return _

        lax.fori_loop(0, shards - 1, one, 0)
        own_copy(kind).start()

    def send_heads(part, low, high):
        def one(peer, _):
            @pl.when(peer != me)
            def _():
                far_copy(8 + part, (peer + shards - me - 1) % shards).start()

            @pl.when(peer == me)
            def _():
                own_copy(8 + part).start()

            return _

        def each(peer, _):
            one(peer, None)
            return _

        lax.fori_loop(low, high, each, 0)

    def wait_far(kind):
        def one(d, _):
            far_copy(kind, d).wait()
            return _

        lax.fori_loop(0, shards - 1, one, 0)
        own_copy(kind).wait()

    def product(h, step, low, high):
        left = piece if step == 0 else got.at[step - 1]

        def one(which, _):
            part = jnp.dot(
                left[pl.ds(h * half, half), :],
                held[which, step],
                preferred_element_type=jnp.float32,
            )
            if step > 0:
                part = part + acc[h, which]
            acc[h, which] = part
            return _

        lax.fori_loop(low, high, one, 0)

    def squared(h, which):
        total = jnp.zeros((half, head), jnp.float32)
        for at in range(width // head):
            part = acc[h, which, :, at * head : (at + 1) * head]
            total = total + part * part
        return jnp.sum(total, axis=1, keepdims=True)

    def sum_copy(h, at, peer):
        return pltpu.make_async_remote_copy(
            src_ref=sums.at[h, 0],
            dst_ref=sums.at[h, at + 1],
            send_sem=sum_send.at[h, at],
            recv_sem=sum_recv.at[h, at],
            device_id={"rep": peer},
            device_id_type=MESH,
        )

    def sum_copies(h):
        return [sum_copy(h, at, peer) for at, peer in enumerate((right, over, cross))]

    def rotate_half(h):
        total = sums[h, 0] + sums[h, 1] + sums[h, 2] + sums[h, 3]
        scales = lax.rsqrt(total / full_width + EPSILON)
        scales = jnp.concatenate([scales] * (128 // 8), axis=0).T
        mine = pl.ds(h * half, half)
        for which, gain in ((0, q_gain), (1, k_gain)):
            scale = scales[:, which : which + 1]

            def one(at, _):
                column = pl.ds(pl.multiple_of(at * head, head), head)
                normed = acc[h, which + 1, :, column] * scale * gain[:, column]
                other = pltpu.roll(normed, head // 2, 1)
                turned[which, mine, column] = (
                    normed * cosine[mine, :] + other * sine[mine, :]
                ).astype(jnp.bfloat16)
                return _

            lax.fori_loop(0, width // head, one, 0)

    def finish_value(h):
        value[pl.ds(h * half, half), :] = acc[h, 0].astype(jnp.bfloat16)

    pl.semaphore_wait(barrier, len(peers))
    for copy in own_copies(0):
        copy.start()
    send_far(6)
    sorted_packed = ordered(rank, my_packed)
    sorted_slots = ordered(rank, my_slots)
    rank = ranks(sorted_slots)
    slot_rank[...] = jnp.broadcast_to(rank.astype(jnp.int32), slot_rank.shape)
    lane = lax.broadcasted_iota(jnp.int32, (8, 128), 1)
    for first, row in ((0, sorted_packed), (shards, ordered(rank, sorted_slots))):
        for owner in range(shards):
            at = owner * chunk
            tile = jnp.broadcast_to(row[:, at // 128 * 128 : at // 128 * 128 + 128], (8, 128))
            tile = tile - owner * rows
            moved = pltpu.roll(tile, chunk, 1)
            tile = jnp.where(owner % 2 == me % 2, tile, moved)
            tile = jnp.where(lane // chunk == me % 2, tile, 0.0)
            meta[first + owner : first + owner + 1, :] = tile[0:1, :].astype(jnp.int32)
    send_far(7)
    angles = upright(sorted_packed - begin_of(sorted_packed)) * frequency[...]
    lane = lax.broadcasted_iota(jnp.int32, (rows, head), 1)
    cosine[...] = jnp.cos(angles)
    turn = jnp.sin(angles)
    sine[...] = jnp.where(lane < head // 2, -turn, turn)

    for which in range(3):
        load(which, 0).wait()
    product(0, 0, 0, 3)
    for h in range(2):
        if h == 1:
            product(1, 0, 0, 3)
            for copy in sum_copies(0):
                copy.wait()
            rotate_half(0)
            send_far(4)
            send_far(2)
        else:
            for copy in own_copies(0):
                copy.wait_recv()
            for copy in forwards(0):
                copy.start()
            for copy in own_copies(1):
                copy.start()
        for step in (1, 2):
            if h == 0:
                for which in range(3):
                    load(which, step).wait()
            product(h, step, 0, 3)
        for copy in forwards(h):
            copy.wait_recv()
        if h == 0:
            for which in range(3):
                load(which, 3).wait()
        product(h, 3, 0, 1)
        finish_value(h)
        send_far(h)
        product(h, 3, 1, 3)
        sums[h, 0] = turned_sums([squared(h, 1), squared(h, 2)])
        for copy in sum_copies(h):
            copy.start()
        if h == 0:
            for copy in own_copies(1):
                copy.wait_recv()
            for copy in forwards(1):
                copy.start()
    for copy in sum_copies(1):
        copy.wait()
    rotate_half(1)
    send_far(5)
    send_far(3)
    side = width // 2
    exits = (cross, right, over, corner)

    def load_out(step):
        return pltpu.make_async_copy(
            w_out.at[:, pl.ds(pl.multiple_of(exits[step] * width, width), width)],
            held.at[0, step],
            w_sem.at[3, step],
        )

    def order_of(row):
        per = 128 // chunk
        tiles = []
        for first in range(0, shards, per):
            tile = meta_got[first, pl.ds(row, 1), :]
            for more in range(1, per):
                tile = tile + meta_got[first + more, pl.ds(row, 1), :]
            tiles.append(tile)
        return jnp.concatenate(tiles, axis=1)

    def pack(block, _):
        aim(hits, order_of(block))
        at = pl.ds(pl.multiple_of(block * chunk, chunk), chunk)
        into = pl.ds(pl.multiple_of(block * rows, rows), rows)
        both = jnp.dot(
            hits[...],
            qk_rows[:, at, :].reshape(rows, 2 * head),
            preferred_element_type=jnp.float32,
        ).astype(jnp.bfloat16)
        queries[into, :] = both[:, :head]
        keys[into, :] = both[:, head:]
        values[:, into] = (
            jnp.dot(
                hits[...],
                v_rows[:, at, :].reshape(rows, head),
                preferred_element_type=jnp.float32,
            )
            .T.astype(jnp.bfloat16)
        )
        return _

    scale = head ** (-0.5) * math.log2(math.e)

    def attend(part, block, steps):
        depth = half * (part + 1)
        unrolled = isinstance(steps, int)

        def repeat(step, state):
            if not unrolled:
                return lax.fori_loop(0, steps, step, state)
            for at in range(steps):
                state = step(at, state)
            return state

        def folded(tile, fold):
            return fold(tile.reshape(tile.shape[0] // 8, 8, half), axis=0)

        query = queries[pl.ds(pl.multiple_of(block * rows + part * half, half), half), :]
        begin = begin_of(
            block * rows + part * half + lax.broadcasted_iota(jnp.int32, (1, half), 1)
        )

        def score(base, count):
            return lax.dot_general(
                keys[pl.ds(base, count), :],
                query,
                (((1,), (1,)), ((), ())),
                preferred_element_type=jnp.float32,
            )

        def earlier(step):
            return pl.multiple_of((block - 1 - step) * rows, rows)

        def stored(step):
            at = step * rows
            return pl.ds(at if unrolled else pl.multiple_of(at, rows), rows)

        base = pl.multiple_of(block * rows, rows)
        key_row = lax.broadcasted_iota(jnp.int32, (depth, half), 0)
        query_row = lax.broadcasted_iota(jnp.int32, (depth, half), 1) + part * half
        seen = (key_row >= begin - base) & (key_row <= query_row)
        last = jnp.where(seen, score(base, depth), -1e30)
        scores[reach * rows : reach * rows + depth, :] = last

        def first_pass(step, top):
            key_row = lax.broadcasted_iota(jnp.int32, (rows, half), 0)
            tile = jnp.where(
                key_row >= begin - earlier(step), score(earlier(step), rows), -1e30
            )
            scores[stored(step), :] = tile
            return jnp.maximum(top, folded(tile, jnp.max))

        top = repeat(first_pass, folded(last, jnp.max))
        top = jnp.max(top, axis=0, keepdims=True)

        def weigh(tile, base, count):
            weights = jnp.exp2((tile - top) * scale)
            return folded(weights, jnp.sum), jnp.dot(
                values[:, pl.ds(base, count)],
                weights.astype(jnp.bfloat16),
                preferred_element_type=jnp.float32,
            )

        def second_pass(step, state):
            total, weighted = weigh(scores[stored(step), :], earlier(step), rows)
            return state[0] + total, state[1] + weighted

        state = weigh(scores[reach * rows : reach * rows + depth, :], base, depth)
        total, weighted = repeat(second_pass, state)
        total = jnp.sum(total, axis=0, keepdims=True)
        heads[part, block] = (weighted / total).T.astype(jnp.bfloat16)

    def attend_first(part):
        def one(block, _):
            attend(part, block, block)
            return _

        lax.fori_loop(0, reach, one, 0)

    def attend_last(part, low, high):
        def one(block, _):
            attend(part, block, reach)
            send_heads(part, block, block + 1)
            return _

        lax.fori_loop(low, high, one, 0)

    def project(part):
        at = pl.ds(part * half, half)

        def share(step):
            return jnp.dot(
                attended[at, :], held[0, step], preferred_element_type=jnp.float32
            )

        def one(step, _):
            held[1, step, at, :] = share(step).astype(jnp.bfloat16)
            return _

        lax.fori_loop(0, 3, one, 0)
        acc[part, 0] = share(3)

    def sent_at(part, step, column):
        return held.at[1, step, pl.ds(part * half, half), column]

    def reduce_copy(src, dst, peer, sem):
        return pltpu.make_async_remote_copy(
            src_ref=src,
            dst_ref=dst,
            send_sem=near_send.at[sem],
            recv_sem=near_recv.at[sem],
            device_id={"rep": peer},
            device_id_type=MESH,
        )

    left, rest = pl.ds(0, side), pl.ds(side, side)

    def first_copies(part):
        return (
            reduce_copy(sent_at(part, 0, left), first_got.at[part, 0], right, 8 + 6 * part),
            reduce_copy(sent_at(part, 1, left), first_got.at[part, 1], right, 8 + 6 * part + 1),
            reduce_copy(sent_at(part, 0, rest), first_got.at[part, 2], over, 8 + 6 * part + 2),
            reduce_copy(sent_at(part, 2, rest), first_got.at[part, 3], over, 8 + 6 * part + 3),
        )

    def second_copies(part):
        return (
            reduce_copy(sent_at(part, 2, left), second_got.at[part, 0], over, 8 + 6 * part + 4),
            reduce_copy(sent_at(part, 1, rest), second_got.at[part, 1], right, 8 + 6 * part + 5),
        )

    def start(copies):
        for copy in copies:
            copy.start()

    def middle(part):
        for copy in first_copies(part):
            copy.wait_recv()
        for step, column, at in ((2, left, 0), (1, rest, 2)):
            mine_rows = pl.ds(part * half, half)
            held[1, step, mine_rows, column] = (
                held[1, step, mine_rows, column].astype(jnp.float32)
                + first_got[part, at].astype(jnp.float32)
            ).astype(jnp.bfloat16)
        start(second_copies(part))
        for column, at in ((left, 1), (rest, 3)):
            acc[part, 0, :, column] = acc[part, 0, :, column] + first_got[part, at].astype(jnp.float32)

    def mixed_copies(part):
        return [
            pltpu.make_async_remote_copy(
                src_ref=sums.at[2 + part, 0],
                dst_ref=sums.at[2 + part, at + 1],
                send_sem=sum_send.at[2 + part, at],
                recv_sem=sum_recv.at[2 + part, at],
                device_id={"rep": peer},
                device_id_type=MESH,
            )
            for at, peer in enumerate((right, over, cross))
        ]

    def total(part):
        for copy in second_copies(part):
            copy.wait_recv()
        squares = jnp.zeros((half, head), jnp.float32)
        for at in range(width // head):
            column = pl.ds(at * head, head)
            got = second_got[part, at * head // side, :, pl.ds(at * head % side, head)]
            rows_now = acc[part, 0, :, column] + got.astype(jnp.float32)
            acc[part, 0, :, column] = rows_now
            squares = squares + rows_now * rows_now
        sums[2 + part, 0] = turned_sums([jnp.sum(squares, axis=1, keepdims=True)])
        start(mixed_copies(part))

    def settle(part):
        for copy in mixed_copies(part):
            copy.wait()
        whole = sums[2 + part, 0] + sums[2 + part, 1] + sums[2 + part, 2] + sums[2 + part, 3]
        scales = lax.rsqrt(whole / full_width + EPSILON)
        scales = jnp.concatenate([scales] * (128 // 8), axis=0).T[:, 0:1]
        at = pl.ds(part * half, half)
        got[1, at, :] = (
            got[0, at, :].astype(jnp.float32) + acc[part, 0] * scales * post_gain[...]
        ).astype(jnp.bfloat16)

    def written(part):
        at = pl.ds(part * half, half)
        return pltpu.make_async_copy(got.at[1, at, :], out.at[at, :], out_sem.at[part])

    for step in range(4):
        load_out(step).start()
    for h in range(2):
        for copy in own_copies(h) + forwards(h):
            copy.wait_send()
    aim(hits, slot_rank[0:1, :])
    select(hits, value, picked.at[1])
    select(hits, turned.at[1], picked.at[0])
    wait_far(7)
    slot_order[...] = jnp.broadcast_to(order_of(shards + me), slot_order.shape)
    wait_far(6)
    aim(hits, order_of(me))
    select(hits, arrived, got.at[0])
    for kind in (0, 2, 4):
        wait_far(kind)
    lax.fori_loop(0, reach, pack, 0)
    attend_first(0)
    attend_first(1)
    for kind in (1, 3, 5):
        wait_far(kind)
    send_heads(0, 0, reach)
    send_heads(1, 0, reach)
    lax.fori_loop(reach, shards, pack, 0)
    for step in range(4):
        load_out(step).wait()
    attend_last(0, reach, shards)
    attend_last(1, reach, shards - 1)
    wait_far(8)
    project(0)
    start(first_copies(0))
    attend_last(1, shards - 1, shards)
    send_far(11)
    wait_far(9)
    send_far(10)
    project(1)
    start(first_copies(1))
    middle(0)
    middle(1)
    total(0)
    settle(0)
    written(0).start()
    total(1)
    settle(1)
    written(1).start()
    wait_far(11)
    wait_far(10)
    for part in range(2):
        for copy in first_copies(part) + second_copies(part):
            copy.wait_send()
        written(part).wait()


def whole_heads(
    hidden_in, w_value, w_query, w_key, w_out, q_gain, k_gain, post_gain,
    frequency, deal, slots, shards, lengths,
):
    rows, width = hidden_in.shape
    full_width = w_query.shape[0]
    half = rows // 2
    head = HEAD_DIM
    reach = shards // 2
    inside = pl.BlockSpec(memory_space=pltpu.VMEM)
    outside = pl.BlockSpec(memory_space=pl.ANY)
    dma = pltpu.SemaphoreType.DMA
    return pl.pallas_call(
        functools.partial(whole_kernel, shards=shards, full_width=full_width),
        out_shape=(jax.ShapeDtypeStruct((rows, width), jnp.bfloat16),) * 3
        + (jax.ShapeDtypeStruct((8, rows), jnp.int32),),
        in_specs=[outside] * 5
        + [inside] * 6
        + [pl.BlockSpec(memory_space=pltpu.SMEM)],
        out_specs=(outside,) * 3 + (inside,),
        scratch_shapes=[
            pltpu.VMEM((rows, width), jnp.bfloat16),
            pltpu.VMEM((2 * shards, 128), jnp.int32),
            pltpu.VMEM((8, rows), jnp.int32),
            pltpu.VMEM((3, 4, width, width), jnp.bfloat16),
            pltpu.VMEM((3, rows, width), jnp.bfloat16),
            pltpu.VMEM((2, 3, half, width), jnp.float32),
            pltpu.VMEM((2, rows, width), jnp.bfloat16),
            pltpu.VMEM((rows, width), jnp.bfloat16),
            pltpu.VMEM((rows, head), jnp.float32),
            pltpu.VMEM((rows, head), jnp.float32),
            pltpu.VMEM((4, 4, 8, half), jnp.float32),
            pltpu.VMEM((2, rows, width), jnp.bfloat16),
            pltpu.VMEM((rows, rows), jnp.bfloat16),
            pltpu.VMEM((shards, rows, 2 * head), jnp.bfloat16),
            pltpu.VMEM((shards, rows, head), jnp.bfloat16),
            pltpu.VMEM((rows, width), jnp.bfloat16),
            pltpu.VMEM((shards, 2 * shards, 128), jnp.int32),
            pltpu.VMEM((shards * rows, head), jnp.bfloat16),
            pltpu.VMEM((shards * rows, head), jnp.bfloat16),
            pltpu.VMEM((head, shards * rows), jnp.bfloat16),
            pltpu.VMEM(((reach + 1) * rows, half), jnp.float32),
            pltpu.VMEM((2, shards, half, head), jnp.bfloat16),
            pltpu.VMEM((rows, width), jnp.bfloat16),
            pltpu.VMEM((2, 4, half, width // 2), jnp.bfloat16),
            pltpu.VMEM((2, 2, half, width // 2), jnp.bfloat16),
            dma((4, 4)),
            dma((20,)),
            dma((20,)),
            dma((4, 3)),
            dma((4, 3)),
            dma((12, shards - 1)),
            dma((12, shards - 1)),
            dma((12,)),
            dma((2,)),
        ],
        compiler_params=pltpu.CompilerParams(
            collective_id=1, has_side_effects=True, vmem_limit_bytes=60 << 20
        ),
        cost_estimate=pl.CostEstimate(
            flops=8 * rows * full_width * width + 20 * rows * rows * shards * head,
            bytes_accessed=8 * full_width * width + 16 * rows * width,
            transcendentals=5 * rows * rows * shards,
        ),
    )(
        hidden_in, w_value, w_query, w_key, w_out, q_gain, k_gain, post_gain,
        frequency, deal, slots, lengths,
    )


def place_kernel(
    order, rows_in, keys_in, values_in, rows_out, keys_out, values_out,
    hits, taken, placed, in_sem, out_sem,
):
    side = taken.shape[2] // 2
    pieces = [(at, pl.ds(half * side, side)) for at in range(2) for half in range(2)]
    arrays = ((keys_in, keys_out), (values_in, values_out))
    loads = [
        pltpu.make_async_copy(arrays[at][0].at[:, to], taken.at[at, :, to], in_sem.at[n])
        for n, (at, to) in enumerate(pieces)
    ]
    stores = [
        pltpu.make_async_copy(placed.at[at, :, to], arrays[at][1].at[:, to], out_sem.at[n])
        for n, (at, to) in enumerate(pieces)
    ]
    load_rows = pltpu.make_async_copy(rows_in, taken.at[2], in_sem.at[4])
    store_rows = pltpu.make_async_copy(taken.at[2], rows_out, out_sem.at[4])
    for copy in loads + [load_rows]:
        copy.start()
    aim(hits, order[0:1, :])
    for n, (at, to) in enumerate(pieces):
        loads[n].wait()
        select(hits, taken.at[at, :, to], placed.at[at, :, to])
        stores[n].start()
        if n == 2:
            load_rows.wait()
            store_rows.start()
    for copy in stores + [store_rows]:
        copy.wait()


def place_rows(order, result, keys_landed, values_landed):
    rows, width = result.shape
    inside = pl.BlockSpec(memory_space=pltpu.VMEM)
    outside = pl.BlockSpec(memory_space=pl.ANY)
    return pl.pallas_call(
        place_kernel,
        out_shape=(jax.ShapeDtypeStruct((rows, width), jnp.bfloat16),) * 3,
        in_specs=[inside] + [outside] * 3,
        out_specs=(outside,) * 3,
        scratch_shapes=[
            pltpu.VMEM((rows, rows), jnp.bfloat16),
            pltpu.VMEM((3, rows, width), jnp.bfloat16),
            pltpu.VMEM((2, rows, width), jnp.bfloat16),
            pltpu.SemaphoreType.DMA((5,)),
            pltpu.SemaphoreType.DMA((5,)),
        ],
        compiler_params=pltpu.CompilerParams(vmem_limit_bytes=60 << 20),
    )(order, result, keys_landed, values_landed)


def body_heads(
    hidden_in,
    w_query,
    w_key,
    w_value,
    w_out,
    q_gain,
    k_gain,
    post_gain,
    prompt_lengths,
    segment_ids,
    deal,
    inverse,
    slots,
):
    shards, rows = lax.axis_size("tok"), hidden_in.shape[0]
    half_size = HEAD_DIM // 2
    frequency = ROPE_BASE ** (-np.arange(half_size) * 2.0 / HEAD_DIM)
    frequency = np.concatenate([frequency, frequency]).astype(np.float32)
    result, keys_landed, values_landed, slot_order = whole_heads(
        hidden_in,
        w_value,
        w_query,
        w_key,
        w_out,
        q_gain[None, :],
        k_gain[None, :],
        post_gain[None, :],
        jnp.asarray(frequency[None, :]),
        deal.reshape(shards * rows // 128, 128),
        slots.reshape(shards * rows // 128, 128),
        shards,
        prompt_lengths,
    )
    return place_rows(slot_order, result, keys_landed, values_landed)


def solution(mesh):
    def pick(*operands):
        rows, width = operands[0].shape
        shards = mesh.shape["tok"]
        fits = width == shards * HEAD_DIM and rows == shards * 64 and mesh.shape["rep"] == 4
        chosen = body_heads if fits else body
        return chosen(*operands)

    return jax.shard_map(
        pick,
        mesh=mesh,
        in_specs=(
            P("tok", "rep"),
            P(None, "rep"),
            P(None, "rep"),
            P(None, "rep"),
            P("rep", None),
            P("rep"),
            P("rep"),
            P("rep"),
            P(),
            P(),
            P(),
            P(),
            P(),
        ),
        out_specs=(P("tok", "rep"), P("tok", "rep"), P("tok", "rep")),
        check_vma=False,
    )
```
